128 devices in a mesh: cols: 32 (over y, z, core), grp: 4 (over x).
Axes of the slice: x: 4, y: 4, z: 4, core: 2. Of those that a mesh axis runs over, the one named last changes fastest.
Arguments:
- pilot_seed: int32 [16384], P(('cols', 'grp')), may hold values from 0 to 16777215
- delay_shift: int32 [131072], P(('cols', 'grp')), may hold values from 0 to 511
- active_column: int32 [512], replicated, may hold values from 0 to 131071
- channel: bfloat16 [512, 524288], P(None, ('cols', 'grp')), may hold values from -24 to 24
- initial_power: float32 [131072], P(('cols', 'grp')), may hold values from 0.0001 to 4, as said below
- noise_power: float32 [1], replicated, may hold values from 0.5 to 1.5
Outputs:
- powers: float32 [131072], P(('cols', 'grp'))
- gradient: float32 [131072], P(('cols', 'grp'))
The draws below stay inside these ranges and needn't reach their ends.
Inputs may be any that keep to these rules, and one draw needn't show every extreme that they name: `initial_power`: every entry is positive.
All inputs are finite; a program needn't handle non-finite values.
Results may differ from the reference program's by a relative error of at most 0.0003.
Values sent between devices are 32-bit elements; how exact they have to be, the bound alone decides.
No kernel may reach another device: no remote copies, remote signals or barrier semaphores. Data moves between devices by JAX's collectives and lax.ppermute only.
A program may use at most 64 MiB of HBM per device.

```python
import math
import jax
import jax.numpy as jnp
from jax import lax

L = 512
COL_DEV = 1024
DELAYS = 8
ACTIVE = 512
SAMP_DEV = 4096
ITERS = 2
N = 131072
USERS = 16384
M = 524288


def draw_channel(key, part):
    keys = jax.random.split(jax.random.fold_in(key, 17), 3)
    row_scale = jnp.exp(jax.random.uniform(keys[0], (ACTIVE, 1), jnp.float32, math.log(0.5), math.log(2.0)))
    col_scale = jnp.exp(jax.random.uniform(keys[1], (1, M), jnp.float32, 0.0, math.log(10.0)))
    base = jnp.clip(jax.random.normal(keys[2], (ACTIVE, M), jnp.float32), -6.0, 6.0)
    return (base * row_scale * col_scale * 0.2).astype(jnp.bfloat16)


def draw_initial_power(key, part):
    keys = jax.random.split(jax.random.fold_in(key, 29), 3)
    chooser = jax.random.uniform(keys[0], (N,), jnp.float32)
    floor_part = jnp.exp(jax.random.uniform(keys[1], (N,), jnp.float32, math.log(0.0001), math.log(0.01)))
    strong = jnp.exp(jax.random.uniform(keys[2], (N,), jnp.float32, math.log(0.3), math.log(3.0)))
    return jnp.where(chooser < 1.0 / 512.0, strong, floor_part).astype(jnp.float32)


def touch_ends(result, rng, smallest, high):
    index_at = [jax.random.randint(jax.random.fold_in(rng, axis), (), 0, length) for axis, length in enumerate(result.shape)]
    longest = result.shape.index(max(result.shape))
    neighbour = index_at[:longest] + [(index_at[longest] + 1) % result.shape[longest]] + index_at[longest + 1:]
    return result.at[tuple(index_at)].set(smallest).at[tuple(neighbour)].set(high)


def setup_inputs(seed: int = 0) -> dict:
    splits = jax.random.split(jax.random.key(seed), 7)
    return {
        "pilot_seed": touch_ends(jax.random.randint(splits[0], (USERS,), 0, 16777216), jax.random.fold_in(splits[0], 1), 0, 16777215).astype(jnp.int32),
        "delay_shift": touch_ends(jax.random.randint(splits[1], (N,), 0, L), jax.random.fold_in(splits[1], 1), 0, L - 1).astype(jnp.int32),
        "active_column": touch_ends(jax.random.randint(splits[2], (ACTIVE,), 0, N), jax.random.fold_in(splits[2], 1), 0, N - 1).astype(jnp.int32),
        "channel": draw_channel(jax.random.fold_in(splits[6], 71), 0),
        "initial_power": draw_initial_power(jax.random.fold_in(splits[6], 71), 0),
        "noise_power": jnp.clip(jax.random.uniform(splits[5], (1,), jnp.float32, 0.5, 1.5), 0.5, 1.5),
    }


mult_first = 747796405
mult_second = 289133645
add_first = 1442695041
mult_third = 2073658381
contract_cols = (((1,), (1,)), ((), ()))

def pilot_matrix(seed_list, shifts):
    row_index = jnp.arange(L, dtype=jnp.int32)[:, None]
    offsets = (row_index - shifts[None, :].astype(jnp.int32) + L) % L
    hashed = seed_list[None, :].astype(jnp.int32) * jnp.int32(mult_first) + offsets * jnp.int32(mult_second) + jnp.int32(add_first)
    hashed = jnp.bitwise_xor(hashed, jnp.bitwise_and(jnp.right_shift(hashed, 15), jnp.int32(131071)))
    hashed = hashed * jnp.int32(mult_third)
    hashed = jnp.bitwise_xor(hashed, jnp.bitwise_and(jnp.right_shift(hashed, 13), jnp.int32(524287)))
    low_bit = jnp.bitwise_and(jnp.right_shift(hashed, 11), jnp.int32(1))
    return (1 - 2 * low_bit).astype(jnp.float32)

def reference(pilot_seed, delay_shift, active_column, channel, initial_power, noise_power):
    inv_root = 1.0 / math.sqrt(L)
    seed_cols = jnp.repeat(pilot_seed, DELAYS)
    active = pilot_matrix(seed_cols[active_column], delay_shift[active_column]).astype(jnp.bfloat16)
    sample_blocks = M // SAMP_DEV
    chan_blocks = jnp.transpose(channel.reshape(ACTIVE, sample_blocks, SAMP_DEV), (1, 0, 2))

    def add_samples(running, chan_block):
        samples = (jnp.dot(active.astype(jnp.float32), chan_block.astype(jnp.float32), preferred_element_type=jnp.float32) * inv_root).astype(jnp.bfloat16)
        return (running + lax.dot_general(samples.astype(jnp.float32), samples.astype(jnp.float32), contract_cols, preferred_element_type=jnp.float32), None)
    cov_sum, ignored = lax.scan(add_samples, jnp.zeros((L, L), jnp.float32), chan_blocks)
    identity = jnp.eye(L, dtype=jnp.float32)
    noise_level = noise_power[0]
    sample_cov = cov_sum / M + noise_level * identity
    col_blocks = N // COL_DEV
    seed_blocks = seed_cols.reshape(col_blocks, COL_DEV)
    shift_blocks = delay_shift.reshape(col_blocks, COL_DEV)
    powers = initial_power
    gradient = jnp.zeros_like(initial_power)
    for iteration in range(ITERS):
        power_blocks = powers.reshape(col_blocks, COL_DEV)

        def add_model(running, pieces):
            dictionary = pilot_matrix(pieces[0], pieces[1])
            weighted = dictionary * (pieces[2] / L)[None, :]
            product = lax.dot_general(weighted.astype(jnp.float32), dictionary.astype(jnp.float32), contract_cols, precision=lax.Precision.HIGHEST, preferred_element_type=jnp.float32)
            return (running + product, None)
        model_sum, ignored = lax.scan(add_model, jnp.zeros((L, L), jnp.float32), (seed_blocks, shift_blocks, power_blocks))
        model_cov = model_sum + noise_level * identity
        factor = jnp.linalg.cholesky(model_cov)
        inverse = jax.scipy.linalg.cho_solve((factor, True), identity)

        def slope(pieces):
            dictionary = pilot_matrix(pieces[0], pieces[1])
            mapped = jnp.dot(inverse.astype(jnp.float32), dictionary.astype(jnp.float32), precision=lax.Precision.HIGHEST, preferred_element_type=jnp.float32)
            weighed = jnp.dot(sample_cov.astype(jnp.float32), mapped.astype(jnp.float32), precision=lax.Precision.HIGHEST, preferred_element_type=jnp.float32)
            return (lax.optimization_barrier(jnp.sum(dictionary * mapped, axis=0)) - lax.optimization_barrier(jnp.sum(mapped * weighed, axis=0))) / L
        gradient = lax.map(slope, (seed_blocks, shift_blocks)).reshape(N)
        powers = jnp.maximum(powers - gradient, 0.0)
    return (powers, gradient)
```

```python
import functools
import math

import jax
import jax.numpy as jnp
from jax import lax
from jax.experimental import pallas as pl
from jax.experimental.pallas import tpu as pltpu
from jax.sharding import PartitionSpec as P

L = 512
DELAYS = 8
ITERS = 2
AXES = ("cols", "grp")
CORE = 4
GROUP_X = (1, 2, 3)
GROUP_Z = (8, 16, 24)
GROUP_Y = (32, 64, 96)

mult_first = 747796405
mult_second = 289133645
add_first = 1442695041
mult_third = 2073658381

B = 128
NB = L // B
BLOCKS = [(i, j) for i in range(NB) for j in range(i, NB)]
PACK = len(BLOCKS) * B
PIECES = 8
ROWS = PACK // PIECES
EXTRA = 8

f32 = jnp.float32
bf16 = jnp.bfloat16
contract_cols = (((1,), (1,)), ((), ()))


def dot(left, right):
    return jnp.dot(left, right, preferred_element_type=f32)


def dot_t(left, right):
    return lax.dot_general(left, right, contract_cols, preferred_element_type=f32)


def split(value):
    high = value.astype(bf16)
    return high, (value - high.astype(f32)).astype(bf16)


def dot_split(left, right):
    lh, ll = split(left)
    rh, rl = split(right)
    return dot(lh, rh) + (dot(lh, rl) + dot(ll, rh))


def dot_exact(left, right):
    return jnp.dot(left, right, precision=lax.Precision.HIGHEST, preferred_element_type=f32)


def identity_like(value):
    rows = lax.broadcasted_iota(jnp.int32, value.shape, 0)
    cols = lax.broadcasted_iota(jnp.int32, value.shape, 1)
    return rows == cols


def write_dictionary(out_ref, seeds, shifts):
    step = 64
    low = seeds * jnp.int32(mult_first) + jnp.int32(add_first) - shifts * jnp.int32(mult_second)
    wrapped = low + jnp.int32((L * mult_second) % (1 << 32) - (1 << 32) if (L * mult_second) % (1 << 32) >= (1 << 31) else (L * mult_second) % (1 << 32))
    width = seeds.shape[1]

    def block(index, carry):
        row = lax.broadcasted_iota(jnp.int32, (step, width), 0) + index * step
        x = row * jnp.int32(mult_second) + jnp.where(row < shifts, wrapped, low)
        x = x ^ lax.shift_right_logical(x, 15)
        x = x * jnp.int32(mult_third)
        x = (x ^ lax.shift_right_logical(x, 13)) & jnp.int32(1 << 11)
        value = jnp.where(x == 0, jnp.float32(1), jnp.float32(-1))
        out_ref[pl.ds(pl.multiple_of(index * step, step), step), :] = value.astype(bf16)
        return carry

    lax.fori_loop(0, L // step, block, 0)


def pack_upper(pack_ref, top, corner):
    for number, (i, j) in enumerate(BLOCKS):
        if i < NB // 2:
            block = top[i * B : (i + 1) * B, j * B : (j + 1) * B]
        else:
            i2, j2 = i - NB // 2, j - NB // 2
            block = corner[i2 * B : (i2 + 1) * B, j2 * B : (j2 + 1) * B]
        pack_ref[number * B : (number + 1) * B, :] = block


def unpack_upper(pack_ref, out_ref):
    for number, (i, j) in enumerate(BLOCKS):
        block = pack_ref[number * B : (number + 1) * B, :]
        out_ref[i * B : (i + 1) * B, j * B : (j + 1) * B] = block
        if i != j:
            out_ref[j * B : (j + 1) * B, i * B : (i + 1) * B] = block.T


def piece(which, place):
    return pl.multiple_of(((which & 7) ^ place) * ROWS, ROWS)


def send_pieces(pack_ref, keep_ref, send_ref, which, height, offset):
    half = PIECES // 2
    for place in range(PIECES):
        target, at = (keep_ref, place) if place < half else (send_ref, place - half)
        start = at * height + offset
        target[start : start + ROWS, :] = pack_ref[pl.ds(piece(which, place), ROWS), :]


def receive_pieces(pack_ref, own_ref, other_ref, which, height, offset):
    half = PIECES // 2
    for place in range(PIECES):
        source, at = (own_ref, place) if place < half else (other_ref, place - half)
        start = at * height + offset
        pack_ref[pl.ds(piece(which, place), ROWS), :] = source[start : start + ROWS, :]


def model_pack(pack_ref, weighted_ref, dict_ref, powers):
    high, low = split(powers)
    half = L // 2
    top = corner = None
    for part in (low, high):
        weighted_ref[...] = dict_ref[...] * part
        a = dot_t(weighted_ref[:half, :], dict_ref[...])
        c = dot_t(weighted_ref[half:, :], dict_ref[half:, :])
        top, corner = (a, c) if top is None else (top + a, corner + c)
    pack_upper(pack_ref, top * (1.0 / L), corner * (1.0 / L))


def first_kernel(
    which_ref, first_ref, seed_ref, shift_ref, power_ref, active_ref, channel_ref,
    keep_ref, send_ref, dict_ref,
    chan_ref, weighted_ref, pack_ref, sems,
):
    which = which_ref[0]
    chunks = sems.shape[0]
    width = chan_ref.shape[1] // chunks
    copies = [
        pltpu.make_async_copy(
            channel_ref.at[:, n * width : (n + 1) * width],
            chan_ref.at[:, n * width : (n + 1) * width],
            sems.at[n],
        )
        for n in range(chunks)
    ]
    for copy in copies:
        copy.start()
    seeds = seed_ref[...]
    shifts = shift_ref[...]
    write_dictionary(dict_ref, seeds, shifts)
    height = 2 * ROWS + EXTRA

    count = seeds.shape[1]
    local = active_ref[...] - first_ref[0]
    hit = lax.broadcasted_iota(jnp.int32, (count, local.shape[1]), 0) == local
    chosen = jnp.where(hit, jnp.float32(1), jnp.float32(0)).astype(bf16)
    parts = [
        seeds & 255,
        lax.shift_right_logical(seeds, 8) & 255,
        lax.shift_right_logical(seeds, 16) & 255,
        shifts & 255,
        lax.shift_right_logical(shifts, 8) & 255,
    ]
    table = jnp.concatenate(parts + [jnp.zeros((11, count), jnp.int32)], 0).astype(f32).astype(bf16)
    found = dot(table, chosen)
    seeds_here = found[0:1] + 256.0 * found[1:2] + 65536.0 * found[2:3]
    shifts_here = found[3:4] + 256.0 * found[4:5]
    for number in range(PIECES):
        place = (which & 7) ^ number
        if number < NB:
            cut = slice(number * B, (number + 1) * B)
            tile = jnp.concatenate(
                [seeds_here[:, cut], shifts_here[:, cut], jnp.zeros((EXTRA - 2, B), f32)], 0
            )
        else:
            tile = jnp.zeros((EXTRA, B), f32)
        start = pl.multiple_of((place & 3) * height + 2 * ROWS, 8)

        @pl.when(place < PIECES // 2)
        def _():
            keep_ref[pl.ds(start, EXTRA), :] = tile

        @pl.when(place >= PIECES // 2)
        def _():
            send_ref[pl.ds(start, EXTRA), :] = tile

    model_pack(pack_ref, weighted_ref, dict_ref, power_ref[...])
    send_pieces(pack_ref, keep_ref, send_ref, which, height, 0)
    half = L // 2
    top = corner = None
    for n in range(chunks):
        copies[n].wait()
        block = chan_ref[:, n * width : (n + 1) * width]
        a = dot_t(block[:half], block)
        c = dot_t(block[half:], block[half:])
        top, corner = (a, c) if top is None else (top + a, corner + c)
    pack_upper(pack_ref, top, corner)
    send_pieces(pack_ref, keep_ref, send_ref, which, height, ROWS)


def invert(a_ref, x_ref, noise):
    eye = identity_like(a_ref)
    mean = jnp.sum(jnp.where(eye[:8, :128], a_ref[:8, :128], 0.0)) * 0.125
    b = jnp.where(eye, a_ref[...] - mean, a_ref[...])
    bh, bl = split(b)
    b2 = dot(bh, bh)
    reach = 1.02 * jnp.sqrt(jnp.sqrt(jnp.sum(b2 * b2)))
    centre = 0.5 * (jnp.maximum(noise, mean - reach) + mean + reach)
    inv = 1.0 / centre
    e0 = (centre - mean) * inv
    one = jnp.where(eye, 1.0, 0.0).astype(f32)
    e = e0 * one - b * inv
    e2 = (e0 * e0) * one - b * (2.0 * e0 * inv) + b2 * (inv * inv)
    x = (one + e + (1.0 + e0) * e2 - dot(bh, e2.astype(bf16)) * inv) * inv
    x = x.astype(bf16)
    x_ref[...] = x.astype(f32)

    def residual_of(x):
        return jnp.where(eye, 1.0, 0.0) - x.astype(f32) * mean - dot(bh, x)

    def more(state):
        count, size = state
        return jnp.logical_and(count < 12, jnp.logical_and(size > 0.01, size < 1e6))

    def step(state):
        count, size = state
        x = x_ref[...].astype(bf16)
        r = residual_of(x)
        size = jnp.sum(r * r)

        @pl.when(size > 0.01)
        def _():
            x_ref[...] = (x.astype(f32) + dot(x, r.astype(bf16))).astype(bf16).astype(f32)

        return count + 1, size

    lax.while_loop(more, step, (jnp.int32(0), jnp.float32(1.0)))
    x = x_ref[...].astype(bf16)
    r = jnp.where(eye, 1.0, 0.0) - x.astype(f32) * mean - (dot(bh, x) + dot(bl, x))
    size = jnp.sum(r * r)
    good = size < 0.02

    @pl.when(good)
    def _():
        rb = r.astype(bf16)
        r2 = dot(rb, rb)
        near = r + r2
        total = near + dot(r2.astype(bf16), near.astype(bf16))
        th, tl = split(total)
        x_ref[...] = x.astype(f32) + (dot(x, th) + dot(x, tl))

    @pl.when(jnp.logical_not(good))
    def _():
        bound = jnp.max(jnp.sum(jnp.abs(a_ref[...]), axis=0, keepdims=True))
        x_ref[...] = jnp.where(identity_like(a_ref), 1.0 / bound, 0.0).astype(f32)

        def more(state):
            count, size, before = state
            going = jnp.logical_or(size > 1e-2, size < 0.25 * before)
            return jnp.logical_and(count < 48, jnp.logical_and(size > 1e-12, going))

        def step(state):
            count, size, before = state
            x = x_ref[...]
            r = jnp.where(identity_like(a_ref), 1.0, 0.0) - dot_exact(a_ref[...], x)
            x_ref[...] = x + dot_exact(x, r)
            return count + 1, jnp.sum(r * r), size

        lax.while_loop(more, step, (jnp.int32(0), jnp.float32(1e30), jnp.float32(1e38)))


def slopes(x_ref, cov_ref, dict_ref):
    x = x_ref[...]
    form = x - dot_split(x, dot_split(cov_ref[...], x))
    fh, fl = split(form)
    d = dict_ref[...]
    mapped = dot(fh, d) + dot(fl, d)
    return jnp.sum(mapped * d.astype(f32), axis=0, keepdims=True) * (1.0 / L)


def add_diagonal(ref, noise):
    for n in range(NB):
        cut = slice(n * B, (n + 1) * B)
        block = ref[cut, cut]
        ref[cut, cut] = jnp.where(identity_like(block), block + noise, block)


def second_kernel(
    total_samples,
    which_ref, noise_ref, own_ref, other_ref, dict_ref, power_ref,
    keep_ref, send_ref, cov_ref, next_ref,
    a_ref, x_ref, pack_ref, act_ref, weighted_ref,
):
    which = which_ref[0]
    noise = noise_ref[0]
    height = 2 * ROWS + EXTRA
    receive_pieces(pack_ref, own_ref, other_ref, which, height, 0)
    unpack_upper(pack_ref, a_ref)
    add_diagonal(a_ref, noise)
    invert(a_ref, x_ref, noise)

    receive_pieces(pack_ref, own_ref, other_ref, which, height, ROWS)
    unpack_upper(pack_ref, a_ref)
    seeds, shifts = [], []
    for number in range(NB):
        place = (which & 7) ^ number
        start = pl.multiple_of((place & 3) * height + 2 * ROWS, 8)
        near = own_ref[pl.ds(start, EXTRA), :]
        far = other_ref[pl.ds(start, EXTRA), :]
        tile = jnp.where(place < PIECES // 2, near, far)
        seeds.append(tile[0:1])
        shifts.append(tile[1:2])
    seeds = jnp.concatenate(seeds, 1).astype(jnp.int32)
    shifts = jnp.concatenate(shifts, 1).astype(jnp.int32)
    write_dictionary(act_ref, seeds, shifts)
    act = act_ref[...]
    gh, gl = split(a_ref[...])
    th, tl = split(dot(act, gh) + dot(act, gl))
    cov_ref[...] = (dot_t(th, act) + dot_t(tl, act)) * (1.0 / (L * total_samples))
    add_diagonal(cov_ref, noise)

    gradient = slopes(x_ref, cov_ref, dict_ref)
    powers = jnp.maximum(power_ref[...] - gradient, 0.0)
    next_ref[...] = powers
    model_pack(pack_ref, weighted_ref, dict_ref, powers)
    send_pieces(pack_ref, keep_ref, send_ref, which, ROWS, 0)


def third_kernel(
    which_ref, noise_ref, own_ref, other_ref, dict_ref, cov_ref, power_ref,
    next_ref, gradient_ref,
    a_ref, x_ref, pack_ref,
):
    which = which_ref[0]
    noise = noise_ref[0]
    receive_pieces(pack_ref, own_ref, other_ref, which, ROWS, 0)
    unpack_upper(pack_ref, a_ref)
    add_diagonal(a_ref, noise)
    invert(a_ref, x_ref, noise)
    gradient = slopes(x_ref, cov_ref, dict_ref)
    gradient_ref[...] = gradient
    next_ref[...] = jnp.maximum(power_ref[...] - gradient, 0.0)


def partner(value, mask):
    return lax.ppermute(value, AXES, [(i, i ^ mask) for i in range(128)])


def exchange(keep, send, height):
    received = partner(send, CORE)
    cut = [slice(n * height, (n + 1) * height) for n in range(4)]
    pieces = [keep[c] + received[c] for c in cut]
    total = pieces[0]
    for arrived in [partner(pieces[m], m) for m in GROUP_X]:
        total = total + arrived
    for group in (GROUP_Y, GROUP_Z):
        arrivals = [partner(total, m) for m in group]
        total = (total + arrivals[0]) + (arrivals[1] + arrivals[2])
    own = jnp.concatenate([total] + [partner(total, m) for m in GROUP_X], 0)
    return own, partner(own, CORE)


VM = pl.BlockSpec(memory_space=pltpu.VMEM)
SM = pl.BlockSpec(memory_space=pltpu.SMEM)
HB = pl.BlockSpec(memory_space=pl.ANY)


def shards(pilot_seed, delay_shift, active_column, channel, initial_power, noise_power):
    device_count = lax.axis_size("cols") * lax.axis_size("grp")
    total_samples = channel.shape[1] * device_count
    count = delay_shift.shape[0]
    which = lax.axis_index(AXES).astype(jnp.int32)
    first = (which * count).reshape(1)
    which = which.reshape(1)
    seeds = jnp.repeat(pilot_seed, DELAYS).reshape(1, count)
    shifts = delay_shift.reshape(1, count)
    active = active_column.reshape(1, -1)
    start_power = initial_power.reshape(1, count)
    height = 2 * ROWS + EXTRA
    shape = jax.ShapeDtypeStruct
    row = shape((1, count), f32)
    square = (L, L)
    params = pltpu.CompilerParams(vmem_limit_bytes=48 << 20)

    keep, send, dictionary = pl.pallas_call(
        first_kernel,
        out_shape=(shape((4 * height, B), f32), shape((4 * height, B), f32), shape((L, count), bf16)),
        in_specs=[SM, SM, VM, VM, VM, VM, HB],
        out_specs=(VM, VM, VM),
        scratch_shapes=[
            pltpu.VMEM(channel.shape, bf16),
            pltpu.VMEM((L, count), bf16),
            pltpu.VMEM((PACK, B), f32),
            pltpu.SemaphoreType.DMA((4,)),
        ],
        compiler_params=params,
        name="first",
    )(which, first, seeds, shifts, start_power, active, channel)
    own, other = exchange(keep, send, height)
    keep, send, sample_cov, powers = pl.pallas_call(
        functools.partial(second_kernel, total_samples),
        out_shape=(shape((4 * ROWS, B), f32), shape((4 * ROWS, B), f32), shape(square, f32), row),
        in_specs=[SM, SM, VM, VM, VM, VM],
        out_specs=(VM, VM, VM, VM),
        scratch_shapes=[
            pltpu.VMEM(square, f32),
            pltpu.VMEM(square, f32),
            pltpu.VMEM((PACK, B), f32),
            pltpu.VMEM(square, bf16),
            pltpu.VMEM((L, count), bf16),
        ],
        compiler_params=params,
        name="second",
    )(which, noise_power, own, other, dictionary, start_power)
    own, other = exchange(keep, send, ROWS)
    powers, gradient = pl.pallas_call(
        third_kernel,
        out_shape=(row, row),
        in_specs=[SM, SM, VM, VM, VM, VM, VM],
        out_specs=(VM, VM),
        scratch_shapes=[
            pltpu.VMEM(square, f32),
            pltpu.VMEM(square, f32),
            pltpu.VMEM((PACK, B), f32),
        ],
        compiler_params=params,
        name="third",
    )(which, noise_power, own, other, dictionary, sample_cov, powers)
    return (powers.reshape(count), gradient.reshape(count))


def solution(mesh):
    placed = (
        P(AXES),
        P(AXES),
        P(),
        P(None, AXES),
        P(AXES),
        P(),
    )
    return jax.shard_map(
        shards,
        mesh=mesh,
        in_specs=placed,
        out_specs=(P(AXES), P(AXES)),
        check_vma=False,
    )
```

```python
import functools
import math

import jax
import jax.numpy as jnp
from jax import lax
from jax.experimental import pallas as pl
from jax.experimental.pallas import tpu as pltpu
from jax.sharding import PartitionSpec as P

L = 512
DELAYS = 8
ITERS = 2
AXES = ("cols", "grp")
CORE = 4
X, Z, Y = 0, 3, 5
STAGES = ((X, Y), (Y, Z), (Z, X), (X, Y))

mult_first = 747796405
mult_second = 289133645
add_first = 1442695041
mult_third = 2073658381

B = 128
NB = L // B
BLOCKS = [(i, j) for i in range(NB) for j in range(i, NB)]
PACK = len(BLOCKS) * B
PIECES = 8
ROWS = PACK // PIECES
EXTRA = 8

f32 = jnp.float32
bf16 = jnp.bfloat16
contract_cols = (((1,), (1,)), ((), ()))


def dot(left, right):
    return jnp.dot(left, right, preferred_element_type=f32)


def dot_t(left, right):
    return lax.dot_general(left, right, contract_cols, preferred_element_type=f32)


def split(value):
    high = value.astype(bf16)
    return high, (value - high.astype(f32)).astype(bf16)


def dot_split(left, right):
    lh, ll = split(left)
    rh, rl = split(right)
    return dot(lh, rh) + (dot(lh, rl) + dot(ll, rh))


def dot_exact(left, right):
    return jnp.dot(left, right, precision=lax.Precision.HIGHEST, preferred_element_type=f32)


def identity_like(value):
    rows = lax.broadcasted_iota(jnp.int32, value.shape, 0)
    cols = lax.broadcasted_iota(jnp.int32, value.shape, 1)
    return rows == cols


def write_dictionary(out_ref, seeds, shifts):
    step = 64
    low = seeds * jnp.int32(mult_first) + jnp.int32(add_first) - shifts * jnp.int32(mult_second)
    wrapped = low + jnp.int32((L * mult_second) % (1 << 32) - (1 << 32) if (L * mult_second) % (1 << 32) >= (1 << 31) else (L * mult_second) % (1 << 32))
    width = seeds.shape[1]

    def block(index, carry):
        row = lax.broadcasted_iota(jnp.int32, (step, width), 0) + index * step
        x = row * jnp.int32(mult_second) + jnp.where(row < shifts, wrapped, low)
        x = x ^ lax.shift_right_logical(x, 15)
        x = x * jnp.int32(mult_third)
        x = (x ^ lax.shift_right_logical(x, 13)) & jnp.int32(1 << 11)
        value = jnp.where(x == 0, jnp.float32(1), jnp.float32(-1))
        out_ref[pl.ds(pl.multiple_of(index * step, step), step), :] = value.astype(bf16)
        return carry

    lax.fori_loop(0, L // step, block, 0)


def pack_upper(pack_ref, top, corner):
    for number, (i, j) in enumerate(BLOCKS):
        if i < NB // 2:
            block = top[i * B : (i + 1) * B, j * B : (j + 1) * B]
        else:
            i2, j2 = i - NB // 2, j - NB // 2
            block = corner[i2 * B : (i2 + 1) * B, j2 * B : (j2 + 1) * B]
        pack_ref[number * B : (number + 1) * B, :] = block


def unpack_upper(pack_ref, out_ref):
    for number, (i, j) in enumerate(BLOCKS):
        block = pack_ref[number * B : (number + 1) * B, :]
        out_ref[i * B : (i + 1) * B, j * B : (j + 1) * B] = block
        if i != j:
            out_ref[j * B : (j + 1) * B, i * B : (i + 1) * B] = block.T


def piece(which, place):
    core = lax.shift_right_logical(which, 4) & 1
    if place < PIECES // 2:
        number = core * 4 + ((which & 3) ^ place)
    else:
        number = (1 - core) * 4 + ((lax.shift_right_logical(which, 2) & 3) ^ (place - 4))
    return pl.multiple_of(number * ROWS, ROWS)


def extra_row(which, number, height):
    core = lax.shift_right_logical(which, 4) & 1
    position = jnp.where(core == 0, which, lax.shift_right_logical(which, 2)) & 3
    return pl.multiple_of((position ^ number) * height + 2 * ROWS, 8)


def send_pieces(pack_ref, keep_ref, send_ref, which, height, offset):
    half = PIECES // 2
    for place in range(PIECES):
        target, at = (keep_ref, place) if place < half else (send_ref, place - half)
        start = at * height + offset
        target[start : start + ROWS, :] = pack_ref[pl.ds(piece(which, place), ROWS), :]


def receive_pieces(pack_ref, own_ref, other_ref, which, height, offset):
    half = PIECES // 2
    for place in range(PIECES):
        source, at = (own_ref, place) if place < half else (other_ref, place - half)
        start = at * height + offset
        pack_ref[pl.ds(piece(which, place), ROWS), :] = source[start : start + ROWS, :]


def model_pack(pack_ref, weighted_ref, dict_ref, powers):
    high, low = split(powers)
    half = L // 2
    top = corner = None
    for part in (low, high):
        weighted_ref[...] = dict_ref[...] * part
        a = dot_t(weighted_ref[:half, :], dict_ref[...])
        c = dot_t(weighted_ref[half:, :], dict_ref[half:, :])
        top, corner = (a, c) if top is None else (top + a, corner + c)
    pack_upper(pack_ref, top * (1.0 / L), corner * (1.0 / L))


def first_kernel(
    which_ref, first_ref, seed_ref, shift_ref, power_ref, active_ref, channel_ref,
    keep_ref, send_ref, dict_ref,
    chan_ref, weighted_ref, pack_ref, sems,
):
    which = which_ref[0]
    chunks = sems.shape[0]
    width = chan_ref.shape[1] // chunks
    copies = [
        pltpu.make_async_copy(
            channel_ref.at[:, n * width : (n + 1) * width],
            chan_ref.at[:, n * width : (n + 1) * width],
            sems.at[n],
        )
        for n in range(chunks)
    ]
    for copy in copies:
        copy.start()
    seeds = seed_ref[...]
    shifts = shift_ref[...]
    write_dictionary(dict_ref, seeds, shifts)
    height = 2 * ROWS + EXTRA

    count = seeds.shape[1]
    local = active_ref[...] - first_ref[0]
    hit = lax.broadcasted_iota(jnp.int32, (count, local.shape[1]), 0) == local
    chosen = jnp.where(hit, jnp.float32(1), jnp.float32(0)).astype(bf16)
    parts = [
        seeds & 255,
        lax.shift_right_logical(seeds, 8) & 255,
        lax.shift_right_logical(seeds, 16) & 255,
        shifts & 255,
        lax.shift_right_logical(shifts, 8) & 255,
    ]
    table = jnp.concatenate(parts + [jnp.zeros((11, count), jnp.int32)], 0).astype(f32).astype(bf16)
    found = dot(table, chosen)
    seeds_here = found[0:1] + 256.0 * found[1:2] + 65536.0 * found[2:3]
    shifts_here = found[3:4] + 256.0 * found[4:5]
    core = lax.shift_right_logical(which, 4) & 1
    for number in range(NB):
        cut = slice(number * B, (number + 1) * B)
        tile = jnp.concatenate(
            [seeds_here[:, cut], shifts_here[:, cut], jnp.zeros((EXTRA - 2, B), f32)], 0
        )
        start = extra_row(which, number, height)
        keep_ref[pl.ds(start, EXTRA), :] = jnp.where(core == 0, tile, 0.0)
        send_ref[pl.ds(start, EXTRA), :] = jnp.where(core == 0, 0.0, tile)

    model_pack(pack_ref, weighted_ref, dict_ref, power_ref[...])
    send_pieces(pack_ref, keep_ref, send_ref, which, height, 0)
    half = L // 2
    top = corner = None
    for n in range(chunks):
        copies[n].wait()
        block = chan_ref[:, n * width : (n + 1) * width]
        a = dot_t(block[:half], block)
        c = dot_t(block[half:], block[half:])
        top, corner = (a, c) if top is None else (top + a, corner + c)
    pack_upper(pack_ref, top, corner)
    send_pieces(pack_ref, keep_ref, send_ref, which, height, ROWS)


def invert(a_ref, x_ref, noise):
    eye = identity_like(a_ref)
    mean = jnp.sum(jnp.where(eye[:8, :128], a_ref[:8, :128], 0.0)) * 0.125
    b = jnp.where(eye, a_ref[...] - mean, a_ref[...])
    bh, bl = split(b)
    b2 = dot(bh, bh)
    reach = 1.02 * jnp.sqrt(jnp.sqrt(jnp.sum(b2 * b2)))
    centre = 0.5 * (jnp.maximum(noise, mean - reach) + mean + reach)
    inv = 1.0 / centre
    e0 = (centre - mean) * inv
    one = jnp.where(eye, 1.0, 0.0).astype(f32)
    e = e0 * one - b * inv
    e2 = (e0 * e0) * one - b * (2.0 * e0 * inv) + b2 * (inv * inv)
    x = (one + e + (1.0 + e0) * e2 - dot(bh, e2.astype(bf16)) * inv) * inv
    x = x.astype(bf16)
    x_ref[...] = x.astype(f32)

    def residual_of(x):
        return jnp.where(eye, 1.0, 0.0) - x.astype(f32) * mean - dot(bh, x)

    def more(state):
        count, size = state
        return jnp.logical_and(count < 12, jnp.logical_and(size > 0.01, size < 1e6))

    def step(state):
        count, size = state
        x = x_ref[...].astype(bf16)
        r = residual_of(x)
        size = jnp.sum(r * r)

        @pl.when(size > 0.01)
        def _():
            x_ref[...] = (x.astype(f32) + dot(x, r.astype(bf16))).astype(bf16).astype(f32)

        return count + 1, size

    lax.while_loop(more, step, (jnp.int32(0), jnp.float32(1.0)))
    x = x_ref[...].astype(bf16)
    r = jnp.where(eye, 1.0, 0.0) - x.astype(f32) * mean - (dot(bh, x) + dot(bl, x))
    size = jnp.sum(r * r)
    good = size < 0.02

    @pl.when(good)
    def _():
        rb = r.astype(bf16)
        r2 = dot(rb, rb)
        near = r + r2
        total = near + dot(r2.astype(bf16), near.astype(bf16))
        th, tl = split(total)
        x_ref[...] = x.astype(f32) + (dot(x, th) + dot(x, tl))

    @pl.when(jnp.logical_not(good))
    def _():
        bound = jnp.max(jnp.sum(jnp.abs(a_ref[...]), axis=0, keepdims=True))
        x_ref[...] = jnp.where(identity_like(a_ref), 1.0 / bound, 0.0).astype(f32)

        def more(state):
            count, size, before = state
            going = jnp.logical_or(size > 1e-2, size < 0.25 * before)
            return jnp.logical_and(count < 48, jnp.logical_and(size > 1e-12, going))

        def step(state):
            count, size, before = state
            x = x_ref[...]
            r = jnp.where(identity_like(a_ref), 1.0, 0.0) - dot_exact(a_ref[...], x)
            x_ref[...] = x + dot_exact(x, r)
            return count + 1, jnp.sum(r * r), size

        lax.while_loop(more, step, (jnp.int32(0), jnp.float32(1e30), jnp.float32(1e38)))


def slopes(x_ref, cov_ref, dict_ref):
    x = x_ref[...]
    form = x - dot_split(x, dot_split(cov_ref[...], x))
    fh, fl = split(form)
    d = dict_ref[...]
    mapped = dot(fh, d) + dot(fl, d)
    return jnp.sum(mapped * d.astype(f32), axis=0, keepdims=True) * (1.0 / L)


def add_diagonal(ref, noise):
    for n in range(NB):
        cut = slice(n * B, (n + 1) * B)
        block = ref[cut, cut]
        ref[cut, cut] = jnp.where(identity_like(block), block + noise, block)


def second_kernel(
    total_samples,
    which_ref, noise_ref, own_ref, other_ref, dict_ref, power_ref,
    keep_ref, send_ref, cov_ref, next_ref,
    a_ref, x_ref, pack_ref, act_ref, weighted_ref,
):
    which = which_ref[0]
    noise = noise_ref[0]
    height = 2 * ROWS + EXTRA
    receive_pieces(pack_ref, own_ref, other_ref, which, height, 0)
    unpack_upper(pack_ref, a_ref)
    add_diagonal(a_ref, noise)
    invert(a_ref, x_ref, noise)

    receive_pieces(pack_ref, own_ref, other_ref, which, height, ROWS)
    unpack_upper(pack_ref, a_ref)
    seeds, shifts = [], []
    for number in range(NB):
        start = extra_row(which, number, height)
        near = own_ref[pl.ds(start, EXTRA), :]
        far = other_ref[pl.ds(start, EXTRA), :]
        tile = jnp.where(lax.shift_right_logical(which, 4) & 1 == 0, near, far)
        seeds.append(tile[0:1])
        shifts.append(tile[1:2])
    seeds = jnp.concatenate(seeds, 1).astype(jnp.int32)
    shifts = jnp.concatenate(shifts, 1).astype(jnp.int32)
    write_dictionary(act_ref, seeds, shifts)
    act = act_ref[...]
    gh, gl = split(a_ref[...])
    th, tl = split(dot(act, gh) + dot(act, gl))
    cov_ref[...] = (dot_t(th, act) + dot_t(tl, act)) * (1.0 / (L * total_samples))
    add_diagonal(cov_ref, noise)

    gradient = slopes(x_ref, cov_ref, dict_ref)
    powers = jnp.maximum(power_ref[...] - gradient, 0.0)
    next_ref[...] = powers
    model_pack(pack_ref, weighted_ref, dict_ref, powers)
    send_pieces(pack_ref, keep_ref, send_ref, which, ROWS, 0)


def third_kernel(
    which_ref, noise_ref, own_ref, other_ref, dict_ref, cov_ref, power_ref,
    next_ref, gradient_ref,
    a_ref, x_ref, pack_ref,
):
    which = which_ref[0]
    noise = noise_ref[0]
    receive_pieces(pack_ref, own_ref, other_ref, which, ROWS, 0)
    unpack_upper(pack_ref, a_ref)
    add_diagonal(a_ref, noise)
    invert(a_ref, x_ref, noise)
    gradient = slopes(x_ref, cov_ref, dict_ref)
    gradient_ref[...] = gradient
    next_ref[...] = jnp.maximum(power_ref[...] - gradient, 0.0)


def partner(value, masks):
    pairs = [(i, i ^ masks[1 if i & CORE else 0]) for i in range(128)]
    return lax.ppermute(value, AXES, pairs)


def around(stage):
    return [tuple(m << bit for bit in STAGES[stage]) for m in (1, 2, 3)]


def exchange(keep, send, height):
    received = partner(send, (CORE, CORE))
    pieces = [keep[c] + received[c] for c in (slice(n * height, (n + 1) * height) for n in range(4))]
    pieces = lax.optimization_barrier(pieces)
    arrivals = [partner(pieces[n + 1], masks) for n, masks in enumerate(around(0))]
    total = (pieces[0] + arrivals[0]) + (arrivals[1] + arrivals[2])
    for stage in (1, 2):
        arrivals = [partner(total, masks) for masks in around(stage)]
        total = (total + arrivals[0]) + (arrivals[1] + arrivals[2])
    own = jnp.concatenate([total] + [partner(total, masks) for masks in around(3)], 0)
    return own, partner(own, (CORE, CORE))


VM = pl.BlockSpec(memory_space=pltpu.VMEM)
SM = pl.BlockSpec(memory_space=pltpu.SMEM)
HB = pl.BlockSpec(memory_space=pl.ANY)


def shards(pilot_seed, delay_shift, active_column, channel, initial_power, noise_power):
    device_count = lax.axis_size("cols") * lax.axis_size("grp")
    total_samples = channel.shape[1] * device_count
    count = delay_shift.shape[0]
    position = lax.axis_index(AXES).astype(jnp.int32)
    first = (position * count).reshape(1)
    core = lax.shift_right_logical(position, 2) & 1
    along = [lax.shift_right_logical(position, bit) & 3 for bit in STAGES[0]]
    own_first, other_first = jnp.where(core == 0, along[0], along[1]), jnp.where(core == 0, along[1], along[0])
    which = (own_first + 4 * other_first + 16 * core).reshape(1)
    seeds = jnp.repeat(pilot_seed, DELAYS).reshape(1, count)
    shifts = delay_shift.reshape(1, count)
    active = active_column.reshape(1, -1)
    start_power = initial_power.reshape(1, count)
    height = 2 * ROWS + EXTRA
    shape = jax.ShapeDtypeStruct
    row = shape((1, count), f32)
    square = (L, L)
    params = pltpu.CompilerParams(vmem_limit_bytes=48 << 20)

    keep, send, dictionary = pl.pallas_call(
        first_kernel,
        out_shape=(shape((4 * height, B), f32), shape((4 * height, B), f32), shape((L, count), bf16)),
        in_specs=[SM, SM, VM, VM, VM, VM, HB],
        out_specs=(VM, VM, VM),
        scratch_shapes=[
            pltpu.VMEM(channel.shape, bf16),
            pltpu.VMEM((L, count), bf16),
            pltpu.VMEM((PACK, B), f32),
            pltpu.SemaphoreType.DMA((4,)),
        ],
        compiler_params=params,
        name="first",
    )(which, first, seeds, shifts, start_power, active, channel)
    own, other = exchange(keep, send, height)
    keep, send, sample_cov, powers = pl.pallas_call(
        functools.partial(second_kernel, total_samples),
        out_shape=(shape((4 * ROWS, B), f32), shape((4 * ROWS, B), f32), shape(square, f32), row),
        in_specs=[SM, SM, VM, VM, VM, VM],
        out_specs=(VM, VM, VM, VM),
        scratch_shapes=[
            pltpu.VMEM(square, f32),
            pltpu.VMEM(square, f32),
            pltpu.VMEM((PACK, B), f32),
            pltpu.VMEM(square, bf16),
            pltpu.VMEM((L, count), bf16),
        ],
        compiler_params=params,
        name="second",
    )(which, noise_power, own, other, dictionary, start_power)
    own, other = exchange(keep, send, ROWS)
    powers, gradient = pl.pallas_call(
        third_kernel,
        out_shape=(row, row),
        in_specs=[SM, SM, VM, VM, VM, VM, VM],
        out_specs=(VM, VM),
        scratch_shapes=[
            pltpu.VMEM(square, f32),
            pltpu.VMEM(square, f32),
            pltpu.VMEM((PACK, B), f32),
        ],
        compiler_params=params,
        name="third",
    )(which, noise_power, own, other, dictionary, sample_cov, powers)
    return (powers.reshape(count), gradient.reshape(count))


def solution(mesh):
    placed = (
        P(AXES),
        P(AXES),
        P(),
        P(None, AXES),
        P(AXES),
        P(),
    )
    return jax.shard_map(
        shards,
        mesh=mesh,
        in_specs=placed,
        out_specs=(P(AXES), P(AXES)),
        check_vma=False,
    )
```

```python
import functools
import math

import jax
import jax.numpy as jnp
from jax import lax
from jax.experimental import pallas as pl
from jax.experimental.pallas import tpu as pltpu
from jax.sharding import PartitionSpec as P

L = 512
DELAYS = 8
ITERS = 2
AXES = ("cols", "grp")
CORE = 4
X, Z, Y = 0, 3, 5
STAGES = ((X, Y), (Y, Z), (Z, X), (X, Y))

mult_first = 747796405
mult_second = 289133645
add_first = 1442695041
mult_third = 2073658381

B = 128
NB = L // B
BLOCKS = [(i, j) for i in range(NB) for j in range(i, NB)]
PACK = len(BLOCKS) * B
PIECES = 8
ROWS = PACK // PIECES
EXTRA = 8

f32 = jnp.float32
bf16 = jnp.bfloat16
contract_cols = (((1,), (1,)), ((), ()))


def dot(left, right):
    return jnp.dot(left, right, preferred_element_type=f32)


def dot_t(left, right):
    return lax.dot_general(left, right, contract_cols, preferred_element_type=f32)


def split(value):
    high = value.astype(bf16)
    return high, (value - high.astype(f32)).astype(bf16)


def dot_exact(left, right):
    return jnp.dot(left, right, precision=lax.Precision.HIGHEST, preferred_element_type=f32)


def identity_like(value):
    rows = lax.broadcasted_iota(jnp.int32, value.shape, 0)
    cols = lax.broadcasted_iota(jnp.int32, value.shape, 1)
    return rows == cols


def signed(value):
    value %= 1 << 32
    return jnp.int32(value - (1 << 32) if value >= 1 << 31 else value)


def write_dictionary(out_ref, seeds, shifts, first_row, rows):
    low = seeds * signed(mult_first) + signed(add_first) - shifts * signed(mult_second)
    wrapped = low + signed(L * mult_second)
    row = lax.broadcasted_iota(jnp.int32, (rows, seeds.shape[1]), 0) + first_row
    x = row * signed(mult_second) + jnp.where(row < shifts, wrapped, low)
    x = x ^ lax.shift_right_logical(x, 15)
    x = x * signed(mult_third)
    x = (x ^ lax.shift_right_logical(x, 13)) & signed(1 << 11)
    value = jnp.where(x == 0, jnp.float32(1), jnp.float32(-1))
    out_ref[first_row : first_row + rows, :] = value.astype(bf16)


def pack_upper(pack_ref, top, corner):
    for number, (i, j) in enumerate(BLOCKS):
        if i < NB // 2:
            block = top[i * B : (i + 1) * B, j * B : (j + 1) * B]
        else:
            i2, j2 = i - NB // 2, j - NB // 2
            block = corner[i2 * B : (i2 + 1) * B, j2 * B : (j2 + 1) * B]
        pack_ref[number * B : (number + 1) * B, :] = block


def unpack_upper(pack_ref, out_ref):
    for number, (i, j) in enumerate(BLOCKS):
        block = pack_ref[number * B : (number + 1) * B, :]
        out_ref[i * B : (i + 1) * B, j * B : (j + 1) * B] = block
        if i != j:
            out_ref[j * B : (j + 1) * B, i * B : (i + 1) * B] = block.T


def piece(which, place):
    core = lax.shift_right_logical(which, 4) & 1
    if place < PIECES // 2:
        number = core * 4 + ((which & 3) ^ place)
    else:
        number = (1 - core) * 4 + ((lax.shift_right_logical(which, 2) & 3) ^ (place - 4))
    return pl.multiple_of(number * ROWS, ROWS)


def extra_row(which, number, height):
    core = lax.shift_right_logical(which, 4) & 1
    position = jnp.where(core == 0, which, lax.shift_right_logical(which, 2)) & 3
    return pl.multiple_of((position ^ number) * height + 2 * ROWS, 8)


def send_pieces(pack_ref, keep_ref, send_ref, which, height, offset):
    half = PIECES // 2
    for place in range(PIECES):
        target, at = (keep_ref, place) if place < half else (send_ref, place - half)
        start = at * height + offset
        target[start : start + ROWS, :] = pack_ref[pl.ds(piece(which, place), ROWS), :]


def receive_pieces(pack_ref, own_ref, other_ref, which, height, offset):
    half = PIECES // 2
    for place in range(PIECES):
        source, at = (own_ref, place) if place < half else (other_ref, place - half)
        start = at * height + offset
        pack_ref[pl.ds(piece(which, place), ROWS), :] = source[start : start + ROWS, :]


def model_pack(pack_ref, weighted_ref, dict_ref, powers):
    high, low = split(powers)
    half = L // 2
    top = corner = None
    for part in (low, high):
        weighted_ref[...] = dict_ref[...] * part
        a = dot_t(weighted_ref[:half, :], dict_ref[...])
        c = dot_t(weighted_ref[half:, :], dict_ref[half:, :])
        top, corner = (a, c) if top is None else (top + a, corner + c)
    pack_upper(pack_ref, top * (1.0 / L), corner * (1.0 / L))


def first_kernel(
    which_ref, first_ref, seed_hbm, shift_hbm, power_hbm, active_hbm, channel_hbm,
    keep_ref, send_ref, dict_ref,
    chan_ref, weighted_ref, pack_ref, top_ref, corner_ref, seed_ref, shift_ref, power_ref, active_ref,
    chan_sems, row_sems,
):
    which = which_ref[0]
    chunks = chan_ref.shape[0]
    width = chan_ref.shape[2]
    rows = [(seed_hbm, seed_ref), (shift_hbm, shift_ref), (active_hbm, active_ref), (power_hbm, power_ref)]
    row_copies = [pltpu.make_async_copy(a, b, row_sems.at[n]) for n, (a, b) in enumerate(rows)]
    copies = [
        pltpu.make_async_copy(
            channel_hbm.at[:, n * width : (n + 1) * width], chan_ref.at[n], chan_sems.at[n]
        )
        for n in range(chunks)
    ]
    for copy in row_copies + copies:
        copy.start()
    for copy in row_copies:
        copy.wait()
    height = 2 * ROWS + EXTRA
    units = seed_ref[...]
    shifts = shift_ref[...]
    count = shifts.shape[1]

    def in_bytes(value, number):
        return [lax.shift_right_logical(value, 8 * n) & 255 for n in range(number)]

    def table_of(parts, width):
        parts = parts + [jnp.zeros((16 - len(parts), width), jnp.int32)]
        return jnp.concatenate(parts, 0).astype(f32).astype(bf16)

    def chosen(hit):
        return jnp.where(hit, jnp.float32(1), jnp.float32(0)).astype(bf16)

    shape = (units.shape[1], count)
    user = lax.shift_right_logical(lax.broadcasted_iota(jnp.int32, shape, 1), int(math.log2(DELAYS)))
    spread = dot(table_of(in_bytes(units, 3), units.shape[1]), chosen(lax.broadcasted_iota(jnp.int32, shape, 0) == user))
    seed_bytes = [spread[n : n + 1].astype(jnp.int32) for n in range(3)]
    seeds = seed_bytes[0] + seed_bytes[1] * 256 + seed_bytes[2] * 65536

    local = active_ref[...] - first_ref[0]
    hit = lax.broadcasted_iota(jnp.int32, (count, local.shape[1]), 0) == local
    found = dot(table_of(seed_bytes + in_bytes(shifts, 2), count), chosen(hit))
    seeds_here = found[0:1] + 256.0 * found[1:2] + 65536.0 * found[2:3]
    shifts_here = found[3:4] + 256.0 * found[4:5]
    core = lax.shift_right_logical(which, 4) & 1
    for number in range(NB):
        cut = slice(number * B, (number + 1) * B)
        tile = jnp.concatenate(
            [seeds_here[:, cut], shifts_here[:, cut], jnp.zeros((EXTRA - 2, B), f32)], 0
        )
        start = extra_row(which, number, height)
        keep_ref[pl.ds(start, EXTRA), :] = jnp.where(core == 0, tile, 0.0)
        send_ref[pl.ds(start, EXTRA), :] = jnp.where(core == 0, 0.0, tile)

    half = L // 2
    step = L // chunks
    for n in range(chunks):
        copies[n].wait()
        write_dictionary(dict_ref, seeds, shifts, n * step, step)
        block = chan_ref[n]
        a = dot_t(block[:half], block)
        c = dot_t(block[half:], block[half:])
        if n == 0:
            top_ref[...] = a
            corner_ref[...] = c
        else:
            top_ref[...] += a
            corner_ref[...] += c
    pack_upper(pack_ref, top_ref[...], corner_ref[...])
    send_pieces(pack_ref, keep_ref, send_ref, which, height, ROWS)
    model_pack(pack_ref, weighted_ref, dict_ref, power_ref[...])
    send_pieces(pack_ref, keep_ref, send_ref, which, height, 0)


def invert(a_ref, x_ref, noise, squarings):
    eye = identity_like(a_ref)
    one = jnp.where(eye, 1.0, 0.0).astype(f32)
    mean = jnp.sum(jnp.where(eye[:8, :128], a_ref[:8, :128], 0.0)) * 0.125
    b = a_ref[...] - mean * one
    bh, bl = split(b)
    b2 = dot(bh, bh)
    reach = 1.02 * jnp.sqrt(jnp.sqrt(jnp.sum(b2 * b2)))
    centre = 0.5 * (jnp.maximum(noise, mean - reach) + mean + reach)
    inv = 1.0 / centre
    e0 = (centre - mean) * inv
    e2 = (e0 * e0) * one - b * (2.0 * e0 * inv) + b2 * (inv * inv)
    power = e2.astype(bf16)
    x = ((1.0 + e0) * (one + e2) - (b + dot(bh, power)) * inv) * inv
    for _ in range(squarings):
        power = dot(power, power).astype(bf16)
        x = x + dot(x.astype(bf16), power)

    def refine(x):
        r = one - x.astype(f32) * mean - (dot(bh, x) + dot(bl, x))
        rb = r.astype(bf16)
        r2 = dot(rb, rb)
        near = r + r2
        total = near + dot(r2.astype(bf16), near.astype(bf16))
        th, tl = split(total)
        x_ref[...] = x.astype(f32) + (dot(x, th) + dot(x, tl))
        return jnp.sum(r2 * r2)

    small = 1e-4
    size = refine(x.astype(bf16))

    @pl.when(jnp.logical_not(size < small))
    def _():
        def more(state):
            count, size = state
            return jnp.logical_and(count < 12, jnp.logical_and(size > small, size < 1e8))

        def step(state):
            count, size = state
            return count + 1, refine(x_ref[...].astype(bf16))

        count, last = lax.while_loop(more, step, (jnp.int32(0), size))

        @pl.when(jnp.logical_not(last < small))
        def _():
            bound = jnp.max(jnp.sum(jnp.abs(a_ref[...]), axis=0, keepdims=True))
            x_ref[...] = one * (1.0 / bound)

            def more(state):
                count, size, before = state
                going = jnp.logical_or(size > 1e-2, size < 0.25 * before)
                return jnp.logical_and(count < 48, jnp.logical_and(size > 1e-12, going))

            def step(state):
                count, size, before = state
                x = x_ref[...]
                r = one - dot_exact(a_ref[...], x)
                x_ref[...] = x + dot_exact(x, r)
                return count + 1, jnp.sum(r * r), size

            lax.while_loop(more, step, (jnp.int32(0), jnp.float32(1e30), jnp.float32(1e38)))


def slopes(x_ref, high_ref, low_ref, dict_ref):
    x = x_ref[...]
    xh, xl = split(x)
    right = dot(high_ref[...], xh) + (dot(high_ref[...], xl) + dot(low_ref[...], xh))
    rh, rl = split(right)
    fh, fl = split(x - (dot(xh, rh) + (dot(xh, rl) + dot(xl, rh))))
    d = dict_ref[...]
    mapped = dot(fh, d) + dot(fl, d)
    return jnp.sum(mapped * d.astype(f32), axis=0, keepdims=True) * (1.0 / L)


def add_diagonal(ref, noise):
    for n in range(NB):
        cut = slice(n * B, (n + 1) * B)
        block = ref[cut, cut]
        ref[cut, cut] = jnp.where(identity_like(block), block + noise, block)


def second_kernel(
    total_samples,
    which_ref, noise_ref, own_ref, other_ref, dict_ref, power_ref,
    keep_ref, send_ref, high_ref, low_ref, next_ref,
    a_ref, gram_ref, x_ref, pack_ref, act_ref, weighted_ref,
):
    which = which_ref[0]
    noise = noise_ref[0]
    height = 2 * ROWS + EXTRA
    receive_pieces(pack_ref, own_ref, other_ref, which, height, ROWS)
    unpack_upper(pack_ref, gram_ref)
    receive_pieces(pack_ref, own_ref, other_ref, which, height, 0)
    unpack_upper(pack_ref, a_ref)
    add_diagonal(a_ref, noise)
    seeds, shifts = [], []
    for number in range(NB):
        start = extra_row(which, number, height)
        near = own_ref[pl.ds(start, EXTRA), :]
        far = other_ref[pl.ds(start, EXTRA), :]
        tile = jnp.where(lax.shift_right_logical(which, 4) & 1 == 0, near, far)
        seeds.append(tile[0:1])
        shifts.append(tile[1:2])
    seeds = jnp.concatenate(seeds, 1).astype(jnp.int32)
    shifts = jnp.concatenate(shifts, 1).astype(jnp.int32)
    write_dictionary(act_ref, seeds, shifts, 0, L)
    act = act_ref[...]
    gh, gl = split(gram_ref[...])
    th, tl = split(dot(act, gh) + dot(act, gl))
    gram_ref[...] = (dot_t(th, act) + dot_t(tl, act)) * (1.0 / (L * total_samples))
    add_diagonal(gram_ref, noise)
    high_ref[...], low_ref[...] = split(gram_ref[...])
    invert(a_ref, x_ref, noise, 2)

    gradient = slopes(x_ref, high_ref, low_ref, dict_ref)
    powers = jnp.maximum(power_ref[...] - gradient, 0.0)
    next_ref[...] = powers
    model_pack(pack_ref, weighted_ref, dict_ref, powers)
    send_pieces(pack_ref, keep_ref, send_ref, which, ROWS, 0)


def third_kernel(
    which_ref, noise_ref, own_ref, other_ref, dict_ref, high_ref, low_ref, power_ref,
    next_ref, gradient_ref,
    a_ref, x_ref, pack_ref,
):
    which = which_ref[0]
    noise = noise_ref[0]
    receive_pieces(pack_ref, own_ref, other_ref, which, ROWS, 0)
    unpack_upper(pack_ref, a_ref)
    add_diagonal(a_ref, noise)
    invert(a_ref, x_ref, noise, 1)
    gradient = slopes(x_ref, high_ref, low_ref, dict_ref)
    gradient_ref[...] = gradient
    next_ref[...] = jnp.maximum(power_ref[...] - gradient, 0.0)


def partner(value, masks):
    pairs = [(i, i ^ masks[1 if i & CORE else 0]) for i in range(128)]
    return lax.ppermute(value, AXES, pairs)


def around(stage):
    return [tuple(m << bit for bit in STAGES[stage]) for m in (1, 2, 3)]


def exchange(keep, send, height):
    received = partner(send, (CORE, CORE))
    pieces = [keep[c] + received[c] for c in (slice(n * height, (n + 1) * height) for n in range(4))]
    pieces = lax.optimization_barrier(pieces)
    arrivals = [partner(pieces[n + 1], masks) for n, masks in enumerate(around(0))]
    total = (pieces[0] + arrivals[0]) + (arrivals[1] + arrivals[2])
    for stage in (1, 2):
        arrivals = [partner(total, masks) for masks in around(stage)]
        total = (total + arrivals[0]) + (arrivals[1] + arrivals[2])
    own = jnp.concatenate([total] + [partner(total, masks) for masks in around(3)], 0)
    return own, partner(own, (CORE, CORE))


VM = pl.BlockSpec(memory_space=pltpu.VMEM)
SM = pl.BlockSpec(memory_space=pltpu.SMEM)
HB = pl.BlockSpec(memory_space=pl.ANY)


def shards(pilot_seed, delay_shift, active_column, channel, initial_power, noise_power):
    device_count = lax.axis_size("cols") * lax.axis_size("grp")
    total_samples = channel.shape[1] * device_count
    count = delay_shift.shape[0]
    position = lax.axis_index(AXES).astype(jnp.int32)
    first = (position * count).reshape(1)
    core = lax.shift_right_logical(position, 2) & 1
    along = [lax.shift_right_logical(position, bit) & 3 for bit in STAGES[0]]
    own_first, other_first = jnp.where(core == 0, along[0], along[1]), jnp.where(core == 0, along[1], along[0])
    which = (own_first + 4 * other_first + 16 * core).reshape(1)
    units = pilot_seed.shape[0]
    active_count = active_column.shape[0]
    start_power = initial_power.reshape(1, count)
    height = 2 * ROWS + EXTRA
    shape = jax.ShapeDtypeStruct
    row = shape((1, count), f32)
    square = (L, L)
    chunks = 8
    params = pltpu.CompilerParams(vmem_limit_bytes=48 << 20)

    keep, send, dictionary = pl.pallas_call(
        first_kernel,
        out_shape=(shape((4 * height, B), f32), shape((4 * height, B), f32), shape((L, count), bf16)),
        in_specs=[SM, SM, HB, HB, HB, HB, HB],
        out_specs=(VM, VM, VM),
        scratch_shapes=[
            pltpu.VMEM((chunks, L, channel.shape[1] // chunks), bf16),
            pltpu.VMEM((L, count), bf16),
            pltpu.VMEM((PACK, B), f32),
            pltpu.VMEM((L // 2, L), f32),
            pltpu.VMEM((L // 2, L // 2), f32),
            pltpu.VMEM((1, units), jnp.int32),
            pltpu.VMEM((1, count), jnp.int32),
            pltpu.VMEM((1, count), f32),
            pltpu.VMEM((1, active_count), jnp.int32),
            pltpu.SemaphoreType.DMA((chunks,)),
            pltpu.SemaphoreType.DMA((4,)),
        ],
        compiler_params=params,
        name="first",
    )(
        which, first, pilot_seed.reshape(1, units), delay_shift.reshape(1, count), start_power,
        active_column.reshape(1, active_count), channel,
    )
    own, other = exchange(keep, send, height)
    half = shape(square, bf16)
    keep, send, high, low, powers = pl.pallas_call(
        functools.partial(second_kernel, total_samples),
        out_shape=(shape((4 * ROWS, B), f32), shape((4 * ROWS, B), f32), half, half, row),
        in_specs=[SM, SM, VM, VM, VM, VM],
        out_specs=(VM, VM, VM, VM, VM),
        scratch_shapes=[
            pltpu.VMEM(square, f32),
            pltpu.VMEM(square, f32),
            pltpu.VMEM(square, f32),
            pltpu.VMEM((PACK, B), f32),
            pltpu.VMEM(square, bf16),
            pltpu.VMEM((L, count), bf16),
        ],
        compiler_params=params,
        name="second",
    )(which, noise_power, own, other, dictionary, start_power)
    own, other = exchange(keep, send, ROWS)
    powers, gradient = pl.pallas_call(
        third_kernel,
        out_shape=(row, row),
        in_specs=[SM, SM, VM, VM, VM, VM, VM, VM],
        out_specs=(VM, VM),
        scratch_shapes=[
            pltpu.VMEM(square, f32),
            pltpu.VMEM(square, f32),
            pltpu.VMEM((PACK, B), f32),
        ],
        compiler_params=params,
        name="third",
    )(which, noise_power, own, other, dictionary, high, low, powers)
    return (powers.reshape(count), gradient.reshape(count))


def solution(mesh):
    placed = (
        P(AXES),
        P(AXES),
        P(),
        P(None, AXES),
        P(AXES),
        P(),
    )
    return jax.shard_map(
        shards,
        mesh=mesh,
        in_specs=placed,
        out_specs=(P(AXES), P(AXES)),
        check_vma=False,
    )
```

```python
import functools
import math

import jax
import jax.numpy as jnp
from jax import lax
from jax.experimental import pallas as pl
from jax.experimental.pallas import tpu as pltpu
from jax.sharding import PartitionSpec as P

L = 512
DELAYS = 8
ITERS = 2
AXES = ("cols", "grp")
CORE = 4
X, Z, Y = 0, 3, 5
STAGES = ((X, Y), (Y, Z), (Z, X), (X, Y))

mult_first = 747796405
mult_second = 289133645
add_first = 1442695041
mult_third = 2073658381

B = 128
NB = L // B
BLOCKS = [(i, j) for i in range(NB) for j in range(i, NB)]
PACK = len(BLOCKS) * B
PIECES = 8
ROWS = PACK // PIECES
EXTRA = 8

f32 = jnp.float32
bf16 = jnp.bfloat16
contract_cols = (((1,), (1,)), ((), ()))


def dot(left, right):
    return jnp.dot(left, right, preferred_element_type=f32)


def dot_t(left, right):
    return lax.dot_general(left, right, contract_cols, preferred_element_type=f32)


def split(value):
    high = value.astype(bf16)
    return high, (value - high.astype(f32)).astype(bf16)


def dot_exact(left, right):
    return jnp.dot(left, right, precision=lax.Precision.HIGHEST, preferred_element_type=f32)


def identity_like(value):
    rows = lax.broadcasted_iota(jnp.int32, value.shape, 0)
    cols = lax.broadcasted_iota(jnp.int32, value.shape, 1)
    return rows == cols


def signed(value):
    value %= 1 << 32
    return jnp.int32(value - (1 << 32) if value >= 1 << 31 else value)


def write_dictionary(out_ref, seeds, shifts, first_row, rows):
    low = seeds * signed(mult_first) + signed(add_first) - shifts * signed(mult_second)
    wrapped = low + signed(L * mult_second)
    row = lax.broadcasted_iota(jnp.int32, (rows, seeds.shape[1]), 0) + first_row
    x = row * signed(mult_second) + jnp.where(row < shifts, wrapped, low)
    x = x ^ lax.shift_right_logical(x, 15)
    x = x * signed(mult_third)
    x = (x ^ lax.shift_right_logical(x, 13)) & signed(1 << 11)
    value = jnp.where(x == 0, jnp.float32(1), jnp.float32(-1))
    out_ref[first_row : first_row + rows, :] = value.astype(bf16)


def pack_upper(pack_ref, top, corner):
    for number, (i, j) in enumerate(BLOCKS):
        if i < NB // 2:
            block = top[i * B : (i + 1) * B, j * B : (j + 1) * B]
        else:
            i2, j2 = i - NB // 2, j - NB // 2
            block = corner[i2 * B : (i2 + 1) * B, j2 * B : (j2 + 1) * B]
        pack_ref[number * B : (number + 1) * B, :] = block


def unpack_upper(pack_ref, out_ref):
    for number, (i, j) in enumerate(BLOCKS):
        block = pack_ref[number * B : (number + 1) * B, :]
        out_ref[i * B : (i + 1) * B, j * B : (j + 1) * B] = block
        if i != j:
            out_ref[j * B : (j + 1) * B, i * B : (i + 1) * B] = block.T


def piece(which, place):
    core = lax.shift_right_logical(which, 4) & 1
    if place < PIECES // 2:
        number = core * 4 + ((which & 3) ^ place)
    else:
        number = (1 - core) * 4 + ((lax.shift_right_logical(which, 2) & 3) ^ (place - 4))
    return pl.multiple_of(number * ROWS, ROWS)


def extra_row(which, number, height):
    core = lax.shift_right_logical(which, 4) & 1
    position = jnp.where(core == 0, which, lax.shift_right_logical(which, 2)) & 3
    return pl.multiple_of((position ^ number) * height + 2 * ROWS, 8)


def send_pieces(pack_ref, keep_ref, send_ref, which, height, offset):
    half = PIECES // 2
    for place in range(PIECES):
        target, at = (keep_ref, place) if place < half else (send_ref, place - half)
        start = at * height + offset
        target[start : start + ROWS, :] = pack_ref[pl.ds(piece(which, place), ROWS), :]


def receive_pieces(pack_ref, own_ref, other_ref, which, height, offset):
    half = PIECES // 2
    for place in range(PIECES):
        source, at = (own_ref, place) if place < half else (other_ref, place - half)
        start = at * height + offset
        pack_ref[pl.ds(piece(which, place), ROWS), :] = source[start : start + ROWS, :]


def model_pack(pack_ref, weighted_ref, dict_ref, powers):
    high, low = split(powers)
    half = L // 2
    top = corner = None
    for part in (low, high):
        weighted_ref[...] = dict_ref[...] * part
        a = dot_t(weighted_ref[:half, :], dict_ref[...])
        c = dot_t(weighted_ref[half:, :], dict_ref[half:, :])
        top, corner = (a, c) if top is None else (top + a, corner + c)
    pack_upper(pack_ref, top * (1.0 / L), corner * (1.0 / L))


def first_kernel(
    which_ref, first_ref, seed_hbm, shift_hbm, power_hbm, active_hbm, channel_hbm,
    keep_ref, send_ref, dict_ref,
    chan_ref, weighted_ref, pack_ref, top_ref, corner_ref, seed_ref, shift_ref, power_ref, active_ref,
    chan_sems, row_sems,
):
    which = which_ref[0]
    chunks = chan_ref.shape[0]
    width = chan_ref.shape[2]
    rows = [(seed_hbm, seed_ref), (shift_hbm, shift_ref), (active_hbm, active_ref), (power_hbm, power_ref)]
    row_copies = [pltpu.make_async_copy(a, b, row_sems.at[n]) for n, (a, b) in enumerate(rows)]
    copies = [
        pltpu.make_async_copy(
            channel_hbm.at[:, n * width : (n + 1) * width], chan_ref.at[n], chan_sems.at[n]
        )
        for n in range(chunks)
    ]
    for copy in row_copies + copies:
        copy.start()
    for copy in row_copies:
        copy.wait()
    height = 2 * ROWS + EXTRA
    units = seed_ref[...]
    shifts = shift_ref[...]
    count = shifts.shape[1]

    def in_bytes(value, number):
        return [lax.shift_right_logical(value, 8 * n) & 255 for n in range(number)]

    def table_of(parts, width):
        parts = parts + [jnp.zeros((16 - len(parts), width), jnp.int32)]
        return jnp.concatenate(parts, 0).astype(f32).astype(bf16)

    def chosen(hit):
        return jnp.where(hit, jnp.float32(1), jnp.float32(0)).astype(bf16)

    shape = (units.shape[1], count)
    user = lax.shift_right_logical(lax.broadcasted_iota(jnp.int32, shape, 1), int(math.log2(DELAYS)))
    spread = dot(table_of(in_bytes(units, 3), units.shape[1]), chosen(lax.broadcasted_iota(jnp.int32, shape, 0) == user))
    seed_bytes = [spread[n : n + 1].astype(jnp.int32) for n in range(3)]
    seeds = seed_bytes[0] + seed_bytes[1] * 256 + seed_bytes[2] * 65536

    local = active_ref[...] - first_ref[0]
    hit = lax.broadcasted_iota(jnp.int32, (count, local.shape[1]), 0) == local
    found = dot(table_of(seed_bytes + in_bytes(shifts, 2), count), chosen(hit))
    seeds_here = found[0:1] + 256.0 * found[1:2] + 65536.0 * found[2:3]
    shifts_here = found[3:4] + 256.0 * found[4:5]
    core = lax.shift_right_logical(which, 4) & 1
    for number in range(NB):
        cut = slice(number * B, (number + 1) * B)
        tile = jnp.concatenate(
            [seeds_here[:, cut], shifts_here[:, cut], jnp.zeros((EXTRA - 2, B), f32)], 0
        )
        start = extra_row(which, number, height)
        keep_ref[pl.ds(start, EXTRA), :] = jnp.where(core == 0, tile, 0.0)
        send_ref[pl.ds(start, EXTRA), :] = jnp.where(core == 0, 0.0, tile)

    half = L // 2
    step = L // chunks
    for n in range(chunks):
        copies[n].wait()
        write_dictionary(dict_ref, seeds, shifts, n * step, step)
        block = chan_ref[n]
        a = dot_t(block[:half], block)
        c = dot_t(block[half:], block[half:])
        if n == 0:
            top_ref[...] = a
            corner_ref[...] = c
        else:
            top_ref[...] += a
            corner_ref[...] += c
    pack_upper(pack_ref, top_ref[...], corner_ref[...])
    send_pieces(pack_ref, keep_ref, send_ref, which, height, ROWS)
    model_pack(pack_ref, weighted_ref, dict_ref, power_ref[...])
    send_pieces(pack_ref, keep_ref, send_ref, which, height, 0)


def invert(a_ref, x_ref, noise, squarings):
    eye = identity_like(a_ref)
    one = jnp.where(eye, 1.0, 0.0).astype(f32)
    mean = jnp.sum(jnp.where(eye[:8, :128], a_ref[:8, :128], 0.0)) * 0.125
    b = a_ref[...] - mean * one
    bh, bl = split(b)
    b2 = dot(bh, bh)
    reach = 1.02 * jnp.sqrt(jnp.sqrt(jnp.sum(b2 * b2)))
    centre = 0.5 * (jnp.maximum(noise, mean - reach) + mean + reach)
    inv = 1.0 / centre
    e0 = (centre - mean) * inv
    e2 = (e0 * e0) * one - b * (2.0 * e0 * inv) + b2 * (inv * inv)
    power = e2.astype(bf16)
    x = ((1.0 + e0) * (one + e2) - (b + dot(bh, power)) * inv) * inv
    for _ in range(squarings):
        power = dot(power, power).astype(bf16)
        x = x + dot(x.astype(bf16), power)

    def refine(x):
        r = one - x.astype(f32) * mean - (dot(bh, x) + dot(bl, x))
        rb = r.astype(bf16)
        r2 = dot(rb, rb)
        near = r + r2
        total = near + dot(r2.astype(bf16), near.astype(bf16))
        th, tl = split(total)
        x_ref[...] = x.astype(f32) + (dot(x, th) + dot(x, tl))
        return jnp.sum(r2 * r2)

    small = 1e-4
    size = refine(x.astype(bf16))

    @pl.when(jnp.logical_not(size < small))
    def _():
        def more(state):
            count, size = state
            return jnp.logical_and(count < 12, jnp.logical_and(size > small, size < 1e8))

        def step(state):
            count, size = state
            return count + 1, refine(x_ref[...].astype(bf16))

        count, last = lax.while_loop(more, step, (jnp.int32(0), size))

        @pl.when(jnp.logical_not(last < small))
        def _():
            bound = jnp.max(jnp.sum(jnp.abs(a_ref[...]), axis=0, keepdims=True))
            x_ref[...] = one * (1.0 / bound)

            def more(state):
                count, size, before = state
                going = jnp.logical_or(size > 1e-2, size < 0.25 * before)
                return jnp.logical_and(count < 48, jnp.logical_and(size > 1e-12, going))

            def step(state):
                count, size, before = state
                x = x_ref[...]
                r = one - dot_exact(a_ref[...], x)
                x_ref[...] = x + dot_exact(x, r)
                return count + 1, jnp.sum(r * r), size

            lax.while_loop(more, step, (jnp.int32(0), jnp.float32(1e30), jnp.float32(1e38)))


def slopes(x_ref, high_ref, low_ref, dict_ref):
    x = x_ref[...]
    xh, xl = split(x)
    right = dot(high_ref[...], xh) + (dot(high_ref[...], xl) + dot(low_ref[...], xh))
    rh, rl = split(right)
    fh, fl = split(x - (dot(xh, rh) + (dot(xh, rl) + dot(xl, rh))))
    d = dict_ref[...]
    mapped = dot(fh, d) + dot(fl, d)
    return jnp.sum(mapped * d.astype(f32), axis=0, keepdims=True) * (1.0 / L)


def add_diagonal(ref, noise):
    for n in range(NB):
        cut = slice(n * B, (n + 1) * B)
        block = ref[cut, cut]
        ref[cut, cut] = jnp.where(identity_like(block), block + noise, block)


def second_kernel(
    total_samples,
    which_ref, noise_ref, own_ref, other_ref, dict_ref, power_ref,
    keep_ref, send_ref, high_ref, low_ref, next_ref,
    a_ref, gram_ref, x_ref, pack_ref, act_ref, weighted_ref,
):
    which = which_ref[0]
    noise = noise_ref[0]
    height = 2 * ROWS + EXTRA
    receive_pieces(pack_ref, own_ref, other_ref, which, height, ROWS)
    unpack_upper(pack_ref, gram_ref)
    receive_pieces(pack_ref, own_ref, other_ref, which, height, 0)
    unpack_upper(pack_ref, a_ref)
    add_diagonal(a_ref, noise)
    seeds, shifts = [], []
    for number in range(NB):
        start = extra_row(which, number, height)
        near = own_ref[pl.ds(start, EXTRA), :]
        far = other_ref[pl.ds(start, EXTRA), :]
        tile = jnp.where(lax.shift_right_logical(which, 4) & 1 == 0, near, far)
        seeds.append(tile[0:1])
        shifts.append(tile[1:2])
    seeds = jnp.concatenate(seeds, 1).astype(jnp.int32)
    shifts = jnp.concatenate(shifts, 1).astype(jnp.int32)
    write_dictionary(act_ref, seeds, shifts, 0, L)
    act = act_ref[...]
    gh, gl = split(gram_ref[...])
    th, tl = split(dot(act, gh) + dot(act, gl))
    gram_ref[...] = (dot_t(th, act) + dot_t(tl, act)) * (1.0 / (L * total_samples))
    add_diagonal(gram_ref, noise)
    high_ref[...], low_ref[...] = split(gram_ref[...])
    invert(a_ref, x_ref, noise, 2)

    gradient = slopes(x_ref, high_ref, low_ref, dict_ref)
    powers = jnp.maximum(power_ref[...] - gradient, 0.0)
    next_ref[...] = powers
    model_pack(pack_ref, weighted_ref, dict_ref, powers)
    send_pieces(pack_ref, keep_ref, send_ref, which, ROWS, 0)


def third_kernel(
    which_ref, noise_ref, own_ref, other_ref, dict_ref, high_ref, low_ref, power_ref,
    next_ref, gradient_ref,
    a_ref, x_ref, pack_ref,
):
    which = which_ref[0]
    noise = noise_ref[0]
    receive_pieces(pack_ref, own_ref, other_ref, which, ROWS, 0)
    unpack_upper(pack_ref, a_ref)
    add_diagonal(a_ref, noise)
    invert(a_ref, x_ref, noise, 1)
    gradient = slopes(x_ref, high_ref, low_ref, dict_ref)
    gradient_ref[...] = gradient
    next_ref[...] = jnp.maximum(power_ref[...] - gradient, 0.0)


def partner(value, masks):
    pairs = [(i, i ^ masks[1 if i & CORE else 0]) for i in range(128)]
    return lax.ppermute(value, AXES, pairs)


def around(stage):
    return [tuple(m << bit for bit in STAGES[stage]) for m in (1, 2, 3)]


def exchange(keep, send, height):
    received = partner(send, (CORE, CORE))
    pieces = [keep[c] + received[c] for c in (slice(n * height, (n + 1) * height) for n in range(4))]
    pieces = lax.optimization_barrier(pieces)
    arrivals = [partner(pieces[n + 1], masks) for n, masks in enumerate(around(0))]
    total = (pieces[0] + arrivals[0]) + (arrivals[1] + arrivals[2])
    for stage in (1, 2):
        arrivals = [partner(total, masks) for masks in around(stage)]
        total = (total + arrivals[0]) + (arrivals[1] + arrivals[2])
    own = jnp.concatenate([total] + [partner(total, masks) for masks in around(3)], 0)
    return own, partner(own, (CORE, CORE))


VM = pl.BlockSpec(memory_space=pltpu.VMEM)
SM = pl.BlockSpec(memory_space=pltpu.SMEM)
HB = pl.BlockSpec(memory_space=pltpu.HBM)


def shards(pilot_seed, delay_shift, active_column, channel, initial_power, noise_power):
    device_count = lax.axis_size("cols") * lax.axis_size("grp")
    total_samples = channel.shape[1] * device_count
    count = delay_shift.shape[0]
    position = lax.axis_index(AXES).astype(jnp.int32)
    first = (position * count).reshape(1)
    core = lax.shift_right_logical(position, 2) & 1
    along = [lax.shift_right_logical(position, bit) & 3 for bit in STAGES[0]]
    own_first, other_first = jnp.where(core == 0, along[0], along[1]), jnp.where(core == 0, along[1], along[0])
    which = (own_first + 4 * other_first + 16 * core).reshape(1)
    units = pilot_seed.shape[0]
    active_count = active_column.shape[0]
    start_power = initial_power.reshape(1, count)
    height = 2 * ROWS + EXTRA
    shape = jax.ShapeDtypeStruct
    row = shape((1, count), f32)
    square = (L, L)
    chunks = 8
    params = pltpu.CompilerParams(vmem_limit_bytes=48 << 20)

    keep, send, dictionary = pl.pallas_call(
        first_kernel,
        out_shape=(shape((4 * height, B), f32), shape((4 * height, B), f32), shape((L, count), bf16)),
        in_specs=[SM, SM, HB, HB, HB, HB, HB],
        out_specs=(VM, VM, VM),
        scratch_shapes=[
            pltpu.VMEM((chunks, L, channel.shape[1] // chunks), bf16),
            pltpu.VMEM((L, count), bf16),
            pltpu.VMEM((PACK, B), f32),
            pltpu.VMEM((L // 2, L), f32),
            pltpu.VMEM((L // 2, L // 2), f32),
            pltpu.VMEM((1, units), jnp.int32),
            pltpu.VMEM((1, count), jnp.int32),
            pltpu.VMEM((1, count), f32),
            pltpu.VMEM((1, active_count), jnp.int32),
            pltpu.SemaphoreType.DMA((chunks,)),
            pltpu.SemaphoreType.DMA((4,)),
        ],
        compiler_params=params,
        name="first",
    )(
        which, first,
        *(
            pltpu.with_memory_space_constraint(value, pltpu.HBM)
            for value in (
                pilot_seed.reshape(1, units), delay_shift.reshape(1, count), start_power,
                active_column.reshape(1, active_count), channel,
            )
        ),
    )
    own, other = exchange(keep, send, height)
    half = shape(square, bf16)
    keep, send, high, low, powers = pl.pallas_call(
        functools.partial(second_kernel, total_samples),
        out_shape=(shape((4 * ROWS, B), f32), shape((4 * ROWS, B), f32), half, half, row),
        in_specs=[SM, SM, VM, VM, VM, VM],
        out_specs=(VM, VM, VM, VM, VM),
        scratch_shapes=[
            pltpu.VMEM(square, f32),
            pltpu.VMEM(square, f32),
            pltpu.VMEM(square, f32),
            pltpu.VMEM((PACK, B), f32),
            pltpu.VMEM(square, bf16),
            pltpu.VMEM((L, count), bf16),
        ],
        compiler_params=params,
        name="second",
    )(which, noise_power, own, other, dictionary, start_power)
    own, other = exchange(keep, send, ROWS)
    powers, gradient = pl.pallas_call(
        third_kernel,
        out_shape=(row, row),
        in_specs=[SM, SM, VM, VM, VM, VM, VM, VM],
        out_specs=(VM, VM),
        scratch_shapes=[
            pltpu.VMEM(square, f32),
            pltpu.VMEM(square, f32),
            pltpu.VMEM((PACK, B), f32),
        ],
        compiler_params=params,
        name="third",
    )(which, noise_power, own, other, dictionary, high, low, powers)
    return (powers.reshape(count), gradient.reshape(count))


def solution(mesh):
    placed = (
        P(AXES),
        P(AXES),
        P(),
        P(None, AXES),
        P(AXES),
        P(),
    )
    return jax.shard_map(
        shards,
        mesh=mesh,
        in_specs=placed,
        out_specs=(P(AXES), P(AXES)),
        check_vma=False,
    )
```

```python
import functools
import math

import jax
import jax.numpy as jnp
from jax import lax
from jax.experimental import pallas as pl
from jax.experimental.pallas import tpu as pltpu
from jax.sharding import PartitionSpec as P

L = 512
DELAYS = 8
ITERS = 2
AXES = ("cols", "grp")
CORE = 4
X, Z, Y = 0, 3, 5
STAGES = ((X, Y), (Y, Z), (Z, X), (X, Y))

mult_first = 747796405
mult_second = 289133645
add_first = 1442695041
mult_third = 2073658381

B = 128
NB = L // B
BLOCKS = [(i, j) for i in range(NB) for j in range(i + 1, NB)]
PACK = (len(BLOCKS) + NB // 2) * B
PIECES = 8
ROWS = PACK // PIECES
EXTRA = 8

f32 = jnp.float32
bf16 = jnp.bfloat16
contract_cols = (((1,), (1,)), ((), ()))


def dot(left, right):
    return jnp.dot(left, right, preferred_element_type=f32)


def dot_t(left, right):
    return lax.dot_general(left, right, contract_cols, preferred_element_type=f32)


def split(value):
    high = value.astype(bf16)
    return high, (value - high.astype(f32)).astype(bf16)


def dot_exact(left, right):
    return jnp.dot(left, right, precision=lax.Precision.HIGHEST, preferred_element_type=f32)


def identity_like(value):
    rows = lax.broadcasted_iota(jnp.int32, value.shape, 0)
    cols = lax.broadcasted_iota(jnp.int32, value.shape, 1)
    return rows == cols


def signed(value):
    value %= 1 << 32
    return jnp.int32(value - (1 << 32) if value >= 1 << 31 else value)


def write_dictionary(out_ref, seeds, shifts, first_row, rows):
    low = seeds * signed(mult_first) + signed(add_first) - shifts * signed(mult_second)
    wrapped = low + signed(L * mult_second)
    row = lax.broadcasted_iota(jnp.int32, (rows, B), 0) + first_row
    start = row * signed(mult_second)
    for tile in range(seeds.shape[1] // B):
        cut = slice(tile * B, (tile + 1) * B)
        x = start + jnp.where(row < shifts[:, cut], wrapped[:, cut], low[:, cut])
        x = x ^ lax.shift_right_logical(x, 15)
        x = x * signed(mult_third)
        x = (x ^ lax.shift_right_logical(x, 13)) & signed(1 << 11)
        value = jnp.where(x == 0, jnp.float32(1), jnp.float32(-1))
        out_ref[first_row : first_row + rows, cut] = value.astype(bf16)


def block_order(shape):
    return lax.broadcasted_iota(jnp.int32, shape, 0), lax.broadcasted_iota(jnp.int32, shape, 1)


def pack_upper(pack_ref, top, corner):
    def block(i, j):
        if i < NB // 2:
            return top[i * B : (i + 1) * B, j * B : (j + 1) * B]
        i, j = i - NB // 2, j - NB // 2
        return corner[i * B : (i + 1) * B, j * B : (j + 1) * B]

    for number, (i, j) in enumerate(BLOCKS):
        pack_ref[number * B : (number + 1) * B, :] = block(i, j)
    row, col = block_order((B, B))
    for pair in range(NB // 2):
        number = len(BLOCKS) + pair
        both = jnp.where(row <= col, block(2 * pair, 2 * pair), block(2 * pair + 1, 2 * pair + 1))
        pack_ref[number * B : (number + 1) * B, :] = both


def diagonal_of(block):
    row, col = block_order(block.shape)
    return jnp.sum(jnp.where(row == col, block, 0.0), axis=0, keepdims=True)


def unpack_upper(pack_ref, out_ref, diagonals, shift):
    for number, (i, j) in enumerate(BLOCKS):
        block = pack_ref[number * B : (number + 1) * B, :]
        out_ref[i * B : (i + 1) * B, j * B : (j + 1) * B] = block
        out_ref[j * B : (j + 1) * B, i * B : (i + 1) * B] = block.T
    row, col = block_order((B, B))
    for pair in range(NB // 2):
        number = len(BLOCKS) + pair
        both = pack_ref[number * B : (number + 1) * B, :]
        turned = both.T
        upper = jnp.where(row <= col, both, turned)
        lower = jnp.where(row > col, both, turned)
        if diagonals is not None:
            lower = jnp.where(row == col, diagonals[pair], lower)
        for i, value in ((2 * pair, upper), (2 * pair + 1, lower)):
            if shift is not None:
                value = jnp.where(row == col, value + shift, value)
            out_ref[i * B : (i + 1) * B, i * B : (i + 1) * B] = value


def piece(which, place):
    core = lax.shift_right_logical(which, 4) & 1
    if place < PIECES // 2:
        number = core * 4 + ((which & 3) ^ place)
    else:
        number = (1 - core) * 4 + ((lax.shift_right_logical(which, 2) & 3) ^ (place - 4))
    return pl.multiple_of(number * ROWS, ROWS)


def extra_row(which, number, height):
    core = lax.shift_right_logical(which, 4) & 1
    position = jnp.where(core == 0, which, lax.shift_right_logical(which, 2)) & 3
    return pl.multiple_of((position ^ number) * height + 2 * ROWS, 8)


def send_pieces(pack_ref, keep_ref, send_ref, which, height, offset):
    half = PIECES // 2
    for place in range(PIECES):
        target, at = (keep_ref, place) if place < half else (send_ref, place - half)
        start = at * height + offset
        target[start : start + ROWS, :] = pack_ref[pl.ds(piece(which, place), ROWS), :]


def receive_pieces(pack_ref, own_ref, other_ref, which, height, offset):
    half = PIECES // 2
    for place in range(PIECES):
        source, at = (own_ref, place) if place < half else (other_ref, place - half)
        start = at * height + offset
        pack_ref[pl.ds(piece(which, place), ROWS), :] = source[start : start + ROWS, :]


def model_pack(pack_ref, weighted_ref, dict_ref, powers):
    high, low = split(powers)
    half = L // 2
    top = corner = None
    for part in (low, high):
        weighted_ref[...] = dict_ref[...] * part
        a = dot_t(weighted_ref[:half, :], dict_ref[...])
        c = dot_t(weighted_ref[half:, :], dict_ref[half:, :])
        top, corner = (a, c) if top is None else (top + a, corner + c)
    pack_upper(pack_ref, top * (1.0 / L), corner * (1.0 / L))


def first_kernel(
    which_ref, first_ref, seed_hbm, shift_hbm, power_hbm, active_hbm, channel_hbm,
    keep_ref, send_ref, dict_ref,
    chan_ref, weighted_ref, pack_ref, top_ref, corner_ref, seed_ref, shift_ref, power_ref, active_ref,
    chan_sems, row_sems,
):
    which = which_ref[0]
    chunks = chan_ref.shape[0]
    width = chan_ref.shape[2]
    rows = [(seed_hbm, seed_ref), (shift_hbm, shift_ref), (active_hbm, active_ref), (power_hbm, power_ref)]
    row_copies = [pltpu.make_async_copy(a, b, row_sems.at[n]) for n, (a, b) in enumerate(rows)]
    copies = [
        pltpu.make_async_copy(
            channel_hbm.at[:, n * width : (n + 1) * width], chan_ref.at[n], chan_sems.at[n]
        )
        for n in range(chunks)
    ]
    for copy in row_copies + copies:
        copy.start()
    for copy in row_copies:
        copy.wait()
    height = 2 * ROWS + EXTRA
    units = seed_ref[...]
    shifts = shift_ref[...]
    count = shifts.shape[1]

    def in_bytes(value, number):
        return [lax.shift_right_logical(value, 8 * n) & 255 for n in range(number)]

    def table_of(parts, width):
        parts = parts + [jnp.zeros((16 - len(parts), width), jnp.int32)]
        return jnp.concatenate(parts, 0).astype(f32).astype(bf16)

    def chosen(hit):
        return jnp.where(hit, jnp.float32(1), jnp.float32(0)).astype(bf16)

    shape = (units.shape[1], count)
    user = lax.shift_right_logical(lax.broadcasted_iota(jnp.int32, shape, 1), int(math.log2(DELAYS)))
    spread = dot(table_of(in_bytes(units, 3), units.shape[1]), chosen(lax.broadcasted_iota(jnp.int32, shape, 0) == user))
    seed_bytes = [spread[n : n + 1].astype(jnp.int32) for n in range(3)]
    seeds = seed_bytes[0] + seed_bytes[1] * 256 + seed_bytes[2] * 65536

    local = active_ref[...] - first_ref[0]
    hit = lax.broadcasted_iota(jnp.int32, (count, local.shape[1]), 0) == local
    found = dot(table_of(seed_bytes + in_bytes(shifts, 2), count), chosen(hit))
    seeds_here = found[0:1] + 256.0 * found[1:2] + 65536.0 * found[2:3]
    shifts_here = found[3:4] + 256.0 * found[4:5]
    half = L // 2
    step = L // chunks
    for n in range(chunks):
        copies[n].wait()
        write_dictionary(dict_ref, seeds, shifts, n * step, step)
        block = chan_ref[n]
        a = dot_t(block[:half], block)
        c = dot_t(block[half:], block[half:])
        if n == 0:
            top_ref[...] = a
            corner_ref[...] = c
        else:
            top_ref[...] += a
            corner_ref[...] += c
    pack_upper(pack_ref, top_ref[...], corner_ref[...])
    send_pieces(pack_ref, keep_ref, send_ref, which, height, ROWS)
    core = lax.shift_right_logical(which, 4) & 1
    for number in range(NB):
        cut = slice(number * B, (number + 1) * B)
        rows = [seeds_here[:, cut], shifts_here[:, cut]]
        if number < NB // 2:
            cut = slice(B, 2 * B)
            rows.append(diagonal_of((top_ref if number == 0 else corner_ref)[cut, cut]))
        tile = jnp.concatenate(rows + [jnp.zeros((EXTRA - len(rows), B), f32)], 0)
        start = extra_row(which, number, height)
        keep_ref[pl.ds(start, EXTRA), :] = jnp.where(core == 0, tile, 0.0)
        send_ref[pl.ds(start, EXTRA), :] = jnp.where(core == 0, 0.0, tile)
    model_pack(pack_ref, weighted_ref, dict_ref, power_ref[...])
    send_pieces(pack_ref, keep_ref, send_ref, which, height, 0)


def invert(a_ref, x_ref, noise, squarings, terms, small):
    eye = identity_like(a_ref)
    one = jnp.where(eye, 1.0, 0.0).astype(f32)
    mean = jnp.sum(jnp.where(eye[:8, :128], a_ref[:8, :128], 0.0)) * 0.125
    b = a_ref[...] - mean * one
    bh, bl = split(b)
    b2 = dot(bh, bh)
    reach = 1.02 * jnp.sqrt(jnp.sqrt(jnp.sum(b2 * b2)))
    centre = 0.5 * (jnp.maximum(noise, mean - reach) + mean + reach)
    inv = 1.0 / centre
    e0 = (centre - mean) * inv
    e2 = (e0 * e0) * one - b * (2.0 * e0 * inv) + b2 * (inv * inv)
    power = e2.astype(bf16)
    x = ((1.0 + e0) * (one + e2) - (b + dot(bh, power)) * inv) * inv
    for _ in range(squarings):
        power = dot(power, power).astype(bf16)
        x = x + dot(x.astype(bf16), power)

    def refine(x):
        r = one - x.astype(f32) * mean - (dot(bh, x) + dot(bl, x))
        rb = r.astype(bf16)
        r2 = dot(rb, rb)
        near = r + r2
        total = near + dot(r2.astype(bf16), near.astype(bf16)) if terms == 4 else near
        th, tl = split(total)
        x_ref[...] = x.astype(f32) + (dot(x, th) + dot(x, tl))
        return jnp.sum(r2 * r2)

    size = refine(x.astype(bf16))

    @pl.when(jnp.logical_not(size < small))
    def _():
        def more(state):
            count, size = state
            return jnp.logical_and(count < 12, jnp.logical_and(size > small, size < 1e8))

        def step(state):
            count, size = state
            return count + 1, refine(x_ref[...].astype(bf16))

        count, last = lax.while_loop(more, step, (jnp.int32(0), size))

        @pl.when(jnp.logical_not(last < small))
        def _():
            bound = jnp.max(jnp.sum(jnp.abs(a_ref[...]), axis=0, keepdims=True))
            x_ref[...] = one * (1.0 / bound)

            def more(state):
                count, size, before = state
                going = jnp.logical_or(size > 1e-2, size < 0.25 * before)
                return jnp.logical_and(count < 48, jnp.logical_and(size > 1e-12, going))

            def step(state):
                count, size, before = state
                x = x_ref[...]
                r = one - dot_exact(a_ref[...], x)
                x_ref[...] = x + dot_exact(x, r)
                return count + 1, jnp.sum(r * r), size

            lax.while_loop(more, step, (jnp.int32(0), jnp.float32(1e30), jnp.float32(1e38)))


def slopes(x_ref, high_ref, low_ref, dict_ref):
    x = x_ref[...]
    xh, xl = split(x)
    right = dot(high_ref[...], xh) + (dot(high_ref[...], xl) + dot(low_ref[...], xh))
    rh, rl = split(right)
    half = L // 2
    d = dict_ref[...]
    result = None
    for rows, cols in ((slice(0, half), slice(0, L)), (slice(half, L), slice(half, L))):
        lh, ll = xh[rows], xl[rows]
        form = x[rows, cols] - (dot(lh, rh[:, cols]) + (dot(lh, rl[:, cols]) + dot(ll, rh[:, cols])))
        if rows != cols:
            form = jnp.concatenate([form[:, :half], 2.0 * form[:, half:]], 1)
        fh, fl = split(form)
        mapped = dot(fh, d[cols]) + dot(fl, d[cols])
        part = jnp.sum(mapped * d[rows].astype(f32), axis=0, keepdims=True)
        result = part if result is None else result + part
    return result * (1.0 / L)


def add_diagonal(ref, noise):
    for n in range(NB):
        cut = slice(n * B, (n + 1) * B)
        block = ref[cut, cut]
        ref[cut, cut] = jnp.where(identity_like(block), block + noise, block)


def second_kernel(
    total_samples,
    which_ref, noise_ref, own_ref, other_ref, dict_ref, power_ref,
    keep_ref, send_ref, high_ref, low_ref, next_ref,
    a_ref, gram_ref, x_ref, pack_ref, act_ref, weighted_ref,
):
    which = which_ref[0]
    noise = noise_ref[0]
    height = 2 * ROWS + EXTRA
    seeds, shifts, diagonals = [], [], []
    for number in range(NB):
        start = extra_row(which, number, height)
        near = own_ref[pl.ds(start, EXTRA), :]
        far = other_ref[pl.ds(start, EXTRA), :]
        tile = jnp.where(lax.shift_right_logical(which, 4) & 1 == 0, near, far)
        seeds.append(tile[0:1])
        shifts.append(tile[1:2])
        diagonals.append(tile[2:3])
    receive_pieces(pack_ref, own_ref, other_ref, which, height, ROWS)
    unpack_upper(pack_ref, gram_ref, diagonals, None)
    receive_pieces(pack_ref, own_ref, other_ref, which, height, 0)
    unpack_upper(pack_ref, a_ref, None, noise)
    seeds = jnp.concatenate(seeds, 1).astype(jnp.int32)
    shifts = jnp.concatenate(shifts, 1).astype(jnp.int32)
    write_dictionary(act_ref, seeds, shifts, 0, L)
    act = act_ref[...]
    gh, gl = split(gram_ref[...])
    th, tl = split(dot(act, gh) + dot(act, gl))
    gram_ref[...] = (dot_t(th, act) + dot_t(tl, act)) * (1.0 / (L * total_samples))
    add_diagonal(gram_ref, noise)
    high_ref[...], low_ref[...] = split(gram_ref[...])
    invert(a_ref, x_ref, noise, 2, 4, 1e-4)

    gradient = slopes(x_ref, high_ref, low_ref, dict_ref)
    powers = jnp.maximum(power_ref[...] - gradient, 0.0)
    next_ref[...] = powers
    model_pack(pack_ref, weighted_ref, dict_ref, powers)
    send_pieces(pack_ref, keep_ref, send_ref, which, ROWS, 0)


def third_kernel(
    which_ref, noise_ref, own_ref, other_ref, dict_ref, high_ref, low_ref, power_ref,
    next_ref, gradient_ref,
    a_ref, x_ref, pack_ref,
):
    which = which_ref[0]
    noise = noise_ref[0]
    receive_pieces(pack_ref, own_ref, other_ref, which, ROWS, 0)
    unpack_upper(pack_ref, a_ref, None, noise)
    invert(a_ref, x_ref, noise, 0, 2, 1.6e-7)
    gradient = slopes(x_ref, high_ref, low_ref, dict_ref)
    gradient_ref[...] = gradient
    next_ref[...] = jnp.maximum(power_ref[...] - gradient, 0.0)


def partner(value, masks):
    pairs = [(i, i ^ masks[1 if i & CORE else 0]) for i in range(128)]
    return lax.ppermute(value, AXES, pairs)


def around(stage):
    return [tuple(m << bit for bit in STAGES[stage]) for m in (1, 2, 3)]


def exchange(keep, send, height):
    received = partner(send, (CORE, CORE))
    pieces = [keep[c] + received[c] for c in (slice(n * height, (n + 1) * height) for n in range(4))]
    pieces = lax.optimization_barrier(pieces)
    arrivals = [partner(pieces[n + 1], masks) for n, masks in enumerate(around(0))]
    total = (pieces[0] + arrivals[0]) + (arrivals[1] + arrivals[2])
    for stage in (1, 2):
        arrivals = [partner(total, masks) for masks in around(stage)]
        total = (total + arrivals[0]) + (arrivals[1] + arrivals[2])
    own = jnp.concatenate([total] + [partner(total, masks) for masks in around(3)], 0)
    return own, partner(own, (CORE, CORE))


VM = pl.BlockSpec(memory_space=pltpu.VMEM)
SM = pl.BlockSpec(memory_space=pltpu.SMEM)
HB = pl.BlockSpec(memory_space=pltpu.HBM)


def shards(pilot_seed, delay_shift, active_column, channel, initial_power, noise_power):
    device_count = lax.axis_size("cols") * lax.axis_size("grp")
    total_samples = channel.shape[1] * device_count
    count = delay_shift.shape[0]
    position = lax.axis_index(AXES).astype(jnp.int32)
    first = (position * count).reshape(1)
    core = lax.shift_right_logical(position, 2) & 1
    along = [lax.shift_right_logical(position, bit) & 3 for bit in STAGES[0]]
    own_first, other_first = jnp.where(core == 0, along[0], along[1]), jnp.where(core == 0, along[1], along[0])
    which = (own_first + 4 * other_first + 16 * core).reshape(1)
    units = pilot_seed.shape[0]
    active_count = active_column.shape[0]
    start_power = initial_power.reshape(1, count)
    height = 2 * ROWS + EXTRA
    shape = jax.ShapeDtypeStruct
    row = shape((1, count), f32)
    square = (L, L)
    chunks = 8
    params = pltpu.CompilerParams(vmem_limit_bytes=48 << 20)

    keep, send, dictionary = pl.pallas_call(
        first_kernel,
        out_shape=(shape((4 * height, B), f32), shape((4 * height, B), f32), shape((L, count), bf16)),
        in_specs=[SM, SM, HB, HB, HB, HB, HB],
        out_specs=(VM, VM, VM),
        scratch_shapes=[
            pltpu.VMEM((chunks, L, channel.shape[1] // chunks), bf16),
            pltpu.VMEM((L, count), bf16),
            pltpu.VMEM((PACK, B), f32),
            pltpu.VMEM((L // 2, L), f32),
            pltpu.VMEM((L // 2, L // 2), f32),
            pltpu.VMEM((1, units), jnp.int32),
            pltpu.VMEM((1, count), jnp.int32),
            pltpu.VMEM((1, count), f32),
            pltpu.VMEM((1, active_count), jnp.int32),
            pltpu.SemaphoreType.DMA((chunks,)),
            pltpu.SemaphoreType.DMA((4,)),
        ],
        compiler_params=params,
        name="first",
    )(
        which, first,
        *(
            pltpu.with_memory_space_constraint(value, pltpu.HBM)
            for value in (
                pilot_seed.reshape(1, units), delay_shift.reshape(1, count), start_power,
                active_column.reshape(1, active_count), channel,
            )
        ),
    )
    own, other = exchange(keep, send, height)
    half = shape(square, bf16)
    keep, send, high, low, powers = pl.pallas_call(
        functools.partial(second_kernel, total_samples),
        out_shape=(shape((4 * ROWS, B), f32), shape((4 * ROWS, B), f32), half, half, row),
        in_specs=[SM, SM, VM, VM, VM, VM],
        out_specs=(VM, VM, VM, VM, VM),
        scratch_shapes=[
            pltpu.VMEM(square, f32),
            pltpu.VMEM(square, f32),
            pltpu.VMEM(square, f32),
            pltpu.VMEM((PACK, B), f32),
            pltpu.VMEM(square, bf16),
            pltpu.VMEM((L, count), bf16),
        ],
        compiler_params=params,
        name="second",
    )(which, noise_power, own, other, dictionary, start_power)
    own, other = exchange(keep, send, ROWS)
    powers, gradient = pl.pallas_call(
        third_kernel,
        out_shape=(row, row),
        in_specs=[SM, SM, VM, VM, VM, VM, VM, VM],
        out_specs=(VM, VM),
        scratch_shapes=[
            pltpu.VMEM(square, f32),
            pltpu.VMEM(square, f32),
            pltpu.VMEM((PACK, B), f32),
        ],
        compiler_params=params,
        name="third",
    )(which, noise_power, own, other, dictionary, high, low, powers)
    return (powers.reshape(count), gradient.reshape(count))


def solution(mesh):
    placed = (
        P(AXES),
        P(AXES),
        P(),
        P(None, AXES),
        P(AXES),
        P(),
    )
    return jax.shard_map(
        shards,
        mesh=mesh,
        in_specs=placed,
        out_specs=(P(AXES), P(AXES)),
        check_vma=False,
    )
```

```python
import functools
import math

import jax
import jax.numpy as jnp
from jax import lax
from jax.experimental import pallas as pl
from jax.experimental.pallas import tpu as pltpu
from jax.sharding import PartitionSpec as P

L = 512
DELAYS = 8
ITERS = 2
AXES = ("cols", "grp")
CORE = 4
X, Z, Y = 0, 3, 5
STAGES = ((X, Y), (Y, Z), (Z, X), (X, Y))

mult_first = 747796405
mult_second = 289133645
add_first = 1442695041
mult_third = 2073658381

B = 128
NB = L // B
BLOCKS = [(i, j) for i in range(NB) for j in range(i + 1, NB)]
PACK = (len(BLOCKS) + NB // 2) * B
PIECES = 8
ROWS = PACK // PIECES
EXTRA = 8

f32 = jnp.float32
bf16 = jnp.bfloat16
contract_cols = (((1,), (1,)), ((), ()))


def dot(left, right):
    return jnp.dot(left, right, preferred_element_type=f32)


def dot_t(left, right):
    return lax.dot_general(left, right, contract_cols, preferred_element_type=f32)


def dot_halves(left, right, product):
    axis = 0 if product is dot else 1
    cut = left.shape[1] // 2
    first, second = (slice(0, cut), slice(cut, None))
    pick = (lambda v, c: v[c]) if axis == 0 else (lambda v, c: v[:, c])
    return product(left[:, first], pick(right, first)) + product(left[:, second], pick(right, second))


def split(value):
    high = value.astype(bf16)
    return high, (value - high.astype(f32)).astype(bf16)


def dot_exact(left, right):
    return jnp.dot(left, right, precision=lax.Precision.HIGHEST, preferred_element_type=f32)


def identity_like(value):
    rows = lax.broadcasted_iota(jnp.int32, value.shape, 0)
    cols = lax.broadcasted_iota(jnp.int32, value.shape, 1)
    return rows == cols


def signed(value):
    value %= 1 << 32
    return jnp.int32(value - (1 << 32) if value >= 1 << 31 else value)


def write_dictionary(out_ref, seeds, shifts, first_row, rows):
    low = seeds * signed(mult_first) + signed(add_first) - shifts * signed(mult_second)
    wrapped = low + signed(L * mult_second)
    row = lax.broadcasted_iota(jnp.int32, (rows, B), 0) + first_row
    start = row * signed(mult_second)
    for tile in range(seeds.shape[1] // B):
        cut = slice(tile * B, (tile + 1) * B)
        x = start + jnp.where(row < shifts[:, cut], wrapped[:, cut], low[:, cut])
        x = x ^ lax.shift_right_logical(x, 15)
        x = x * signed(mult_third)
        x = (x ^ lax.shift_right_logical(x, 13)) & signed(1 << 11)
        value = jnp.where(x == 0, jnp.float32(1), jnp.float32(-1))
        out_ref[first_row : first_row + rows, cut] = value.astype(bf16)


def block_order(shape):
    return lax.broadcasted_iota(jnp.int32, shape, 0), lax.broadcasted_iota(jnp.int32, shape, 1)


def pack_upper(pack_ref, top, corner):
    def block(i, j):
        if i < NB // 2:
            return top[i * B : (i + 1) * B, j * B : (j + 1) * B]
        i, j = i - NB // 2, j - NB // 2
        return corner[i * B : (i + 1) * B, j * B : (j + 1) * B]

    for number, (i, j) in enumerate(BLOCKS):
        pack_ref[number * B : (number + 1) * B, :] = block(i, j)
    row, col = block_order((B, B))
    for pair in range(NB // 2):
        number = len(BLOCKS) + pair
        both = jnp.where(row <= col, block(2 * pair, 2 * pair), block(2 * pair + 1, 2 * pair + 1))
        pack_ref[number * B : (number + 1) * B, :] = both


def diagonal_of(block):
    row, col = block_order(block.shape)
    return jnp.sum(jnp.where(row == col, block, 0.0), axis=0, keepdims=True)


def unpack_upper(pack_ref, out_ref, diagonals, shift):
    for number, (i, j) in enumerate(BLOCKS):
        block = pack_ref[number * B : (number + 1) * B, :]
        out_ref[i * B : (i + 1) * B, j * B : (j + 1) * B] = block
        out_ref[j * B : (j + 1) * B, i * B : (i + 1) * B] = block.T
    row, col = block_order((B, B))
    for pair in range(NB // 2):
        number = len(BLOCKS) + pair
        both = pack_ref[number * B : (number + 1) * B, :]
        turned = both.T
        upper = jnp.where(row <= col, both, turned)
        lower = jnp.where(row > col, both, turned)
        if diagonals is not None:
            lower = jnp.where(row == col, diagonals[pair], lower)
        for i, value in ((2 * pair, upper), (2 * pair + 1, lower)):
            if shift is not None:
                value = jnp.where(row == col, value + shift, value)
            out_ref[i * B : (i + 1) * B, i * B : (i + 1) * B] = value


def place_of_device():
    position = lax.axis_index("cols").astype(jnp.int32) * 4 + lax.axis_index("grp").astype(jnp.int32)
    core = lax.shift_right_logical(position, 2) & 1
    first, second = [lax.shift_right_logical(position, bit) & 3 for bit in STAGES[0]]
    own = jnp.where(core == 0, first, second)
    return own + 4 * (first + second - own) + 16 * core, position


def piece(which, place):
    core = lax.shift_right_logical(which, 4) & 1
    if place < PIECES // 2:
        number = core * 4 + ((which & 3) ^ place)
    else:
        number = (1 - core) * 4 + ((lax.shift_right_logical(which, 2) & 3) ^ (place - 4))
    return pl.multiple_of(number * ROWS, ROWS)


def extra_row(which, number, height):
    core = lax.shift_right_logical(which, 4) & 1
    position = jnp.where(core == 0, which, lax.shift_right_logical(which, 2)) & 3
    return pl.multiple_of((position ^ number) * height + 2 * ROWS, 8)


def send_pieces(pack_ref, keep_ref, send_ref, which, height, offset):
    half = PIECES // 2
    for place in range(PIECES):
        target, at = (keep_ref, place) if place < half else (send_ref, place - half)
        start = at * height + offset
        target[start : start + ROWS, :] = pack_ref[pl.ds(piece(which, place), ROWS), :]


def receive_pieces(pack_ref, own_ref, other_ref, which, height, offset):
    half = PIECES // 2
    for place in range(PIECES):
        source, at = (own_ref, place) if place < half else (other_ref, place - half)
        start = at * height + offset
        pack_ref[pl.ds(piece(which, place), ROWS), :] = source[start : start + ROWS, :]


def model_pack(pack_ref, weighted_ref, dict_ref, powers):
    high, low = split(powers)
    half = L // 2
    top = corner = None
    for part in (low, high):
        weighted_ref[...] = dict_ref[...] * part
        a = dot_t(weighted_ref[:half, :], dict_ref[...])
        c = dot_halves(weighted_ref[half:, :], dict_ref[half:, :], dot_t)
        top, corner = (a, c) if top is None else (top + a, corner + c)
    pack_upper(pack_ref, top * (1.0 / L), corner * (1.0 / L))


def first_kernel(
    seed_hbm, shift_hbm, power_hbm, active_hbm, channel_hbm,
    keep_ref, send_ref, dict_ref, power_ref,
    chan_ref, weighted_ref, pack_ref, top_ref, corner_ref, seed_ref, shift_ref, active_ref,
    chan_sems, row_sems,
):
    which, position = place_of_device()
    chunks = chan_ref.shape[0]
    width = chan_ref.shape[2]
    rows = [(seed_hbm, seed_ref), (shift_hbm, shift_ref), (active_hbm, active_ref), (power_hbm, power_ref)]
    row_copies = [pltpu.make_async_copy(a, b, row_sems.at[n]) for n, (a, b) in enumerate(rows)]
    copies = [
        pltpu.make_async_copy(
            channel_hbm.at[:, n * width : (n + 1) * width], chan_ref.at[n], chan_sems.at[n]
        )
        for n in range(chunks)
    ]
    for copy in row_copies + copies:
        copy.start()
    for copy in row_copies:
        copy.wait()
    height = 2 * ROWS + EXTRA
    half = L // 2
    step = L // chunks

    def gram(n):
        copies[n].wait()
        block = chan_ref[n]
        a = dot_t(block[:half], block)
        c = dot_halves(block[half:], block[half:], dot_t)
        if n == 0:
            top_ref[...] = a
            corner_ref[...] = c
        else:
            top_ref[...] += a
            corner_ref[...] += c

    gram(0)
    units = seed_ref[...]
    shifts = shift_ref[...]
    count = shifts.shape[1]

    def in_bytes(value, number):
        return [lax.shift_right_logical(value, 8 * n) & 255 for n in range(number)]

    def table_of(parts, width):
        parts = parts + [jnp.zeros((16 - len(parts), width), jnp.int32)]
        return jnp.concatenate(parts, 0).astype(f32).astype(bf16)

    def chosen(hit):
        return jnp.where(hit, jnp.float32(1), jnp.float32(0)).astype(bf16)

    shape = (units.shape[1], count)
    user = lax.shift_right_logical(lax.broadcasted_iota(jnp.int32, shape, 1), int(math.log2(DELAYS)))
    spread = dot(table_of(in_bytes(units, 3), units.shape[1]), chosen(lax.broadcasted_iota(jnp.int32, shape, 0) == user))
    seed_bytes = [spread[n : n + 1].astype(jnp.int32) for n in range(3)]
    seeds = seed_bytes[0] + seed_bytes[1] * 256 + seed_bytes[2] * 65536

    local = active_ref[...] - position * count
    hit = lax.broadcasted_iota(jnp.int32, (count, local.shape[1]), 0) == local
    found = dot(table_of(seed_bytes + in_bytes(shifts, 2), count), chosen(hit))
    seeds_here = found[0:1] + 256.0 * found[1:2] + 65536.0 * found[2:3]
    shifts_here = found[3:4] + 256.0 * found[4:5]
    for n in range(1, chunks):
        gram(n)
        write_dictionary(dict_ref, seeds, shifts, (n - 1) * step, step)
    write_dictionary(dict_ref, seeds, shifts, (chunks - 1) * step, step)
    pack_upper(pack_ref, top_ref[...], corner_ref[...])
    send_pieces(pack_ref, keep_ref, send_ref, which, height, ROWS)
    core = lax.shift_right_logical(which, 4) & 1
    for number in range(NB):
        cut = slice(number * B, (number + 1) * B)
        rows = [seeds_here[:, cut], shifts_here[:, cut]]
        if number < NB // 2:
            cut = slice(B, 2 * B)
            rows.append(diagonal_of((top_ref if number == 0 else corner_ref)[cut, cut]))
        tile = jnp.concatenate(rows + [jnp.zeros((EXTRA - len(rows), B), f32)], 0)
        start = extra_row(which, number, height)
        keep_ref[pl.ds(start, EXTRA), :] = jnp.where(core == 0, tile, 0.0)
        send_ref[pl.ds(start, EXTRA), :] = jnp.where(core == 0, 0.0, tile)
    model_pack(pack_ref, weighted_ref, dict_ref, power_ref[...])
    send_pieces(pack_ref, keep_ref, send_ref, which, height, 0)


def invert(a_ref, x_ref, noise, squarings, terms, small):
    eye = identity_like(a_ref)
    one = jnp.where(eye, 1.0, 0.0).astype(f32)
    mean = a_ref[0:1, 0:1]
    b = a_ref[...] - mean * one
    bh, bl = split(b)
    b2 = dot(bh, bh)
    fourth = jnp.sum(jnp.sum(b2 * b2, axis=0, keepdims=True), axis=1, keepdims=True)
    reach = 1.02 * jnp.sqrt(jnp.sqrt(fourth))
    centre = 0.5 * (jnp.maximum(noise, mean - reach) + mean + reach)
    inv = 1.0 / centre
    e0 = (centre - mean) * inv
    e2 = (e0 * e0) * one - b * (2.0 * e0 * inv) + b2 * (inv * inv)
    power = e2.astype(bf16)
    x = ((1.0 + e0) * (one + e2) - (b + dot(bh, power)) * inv) * inv
    for _ in range(squarings):
        power = dot(power, power).astype(bf16)
        x = x + dot(x.astype(bf16), power)

    def refine(x):
        r = one - x.astype(f32) * mean - (dot(bh, x) + dot(bl, x))
        rb = r.astype(bf16)
        r2 = dot(rb, rb)
        near = r + r2
        total = near + dot(r2.astype(bf16), near.astype(bf16)) if terms == 4 else near
        th, tl = split(total)
        x_ref[...] = x.astype(f32) + (dot(x, th) + dot(x, tl))
        return jnp.sum(r2 * r2)

    size = refine(x.astype(bf16))

    @pl.when(jnp.logical_not(size < small))
    def _():
        def more(state):
            count, size = state
            return jnp.logical_and(count < 12, jnp.logical_and(size > small, size < 1e8))

        def step(state):
            count, size = state
            return count + 1, refine(x_ref[...].astype(bf16))

        count, last = lax.while_loop(more, step, (jnp.int32(0), size))

        @pl.when(jnp.logical_not(last < small))
        def _():
            bound = jnp.max(jnp.sum(jnp.abs(a_ref[...]), axis=0, keepdims=True))
            x_ref[...] = one * (1.0 / bound)

            def more(state):
                count, size, before = state
                going = jnp.logical_or(size > 1e-2, size < 0.25 * before)
                return jnp.logical_and(count < 48, jnp.logical_and(size > 1e-12, going))

            def step(state):
                count, size, before = state
                x = x_ref[...]
                r = one - dot_exact(a_ref[...], x)
                x_ref[...] = x + dot_exact(x, r)
                return count + 1, jnp.sum(r * r), size

            lax.while_loop(more, step, (jnp.int32(0), jnp.float32(1e30), jnp.float32(1e38)))


def slopes(x_ref, high_ref, low_ref, dict_ref):
    x = x_ref[...]
    xh, xl = split(x)
    right = dot(high_ref[...], xh) + (dot(high_ref[...], xl) + dot(low_ref[...], xh))
    rh, rl = split(right)
    half = L // 2
    d = dict_ref[...]
    result = None
    for rows, cols in ((slice(0, half), slice(0, L)), (slice(half, L), slice(half, L))):
        lh, ll = xh[rows], xl[rows]
        if rows == cols:
            ch, cl = rh[:, cols], rl[:, cols]
            form = x[rows, cols] - (
                dot_halves(lh, ch, dot) + (dot_halves(lh, cl, dot) + dot_halves(ll, ch, dot))
            )
        else:
            form = x[rows] - (dot(lh, rh) + (dot(lh, rl) + dot(ll, rh)))
            form = jnp.concatenate([form[:, :half], 2.0 * form[:, half:]], 1)
        fh, fl = split(form)
        mapped = dot(fh, d[cols]) + dot(fl, d[cols])
        part = jnp.sum(mapped * d[rows].astype(f32), axis=0, keepdims=True)
        result = part if result is None else result + part
    return result * (1.0 / L)


def add_diagonal(ref, noise):
    for n in range(NB):
        cut = slice(n * B, (n + 1) * B)
        block = ref[cut, cut]
        ref[cut, cut] = jnp.where(identity_like(block), block + noise, block)


def second_kernel(
    total_samples,
    noise_ref, own_ref, other_ref, dict_ref, power_ref,
    keep_ref, send_ref, high_ref, low_ref, next_ref,
    a_ref, gram_ref, x_ref, pack_ref, act_ref, weighted_ref,
):
    which, _ = place_of_device()
    noise = noise_ref[0]
    height = 2 * ROWS + EXTRA
    seeds, shifts, diagonals = [], [], []
    for number in range(NB):
        start = extra_row(which, number, height)
        near = own_ref[pl.ds(start, EXTRA), :]
        far = other_ref[pl.ds(start, EXTRA), :]
        tile = jnp.where(lax.shift_right_logical(which, 4) & 1 == 0, near, far)
        seeds.append(tile[0:1])
        shifts.append(tile[1:2])
        diagonals.append(tile[2:3])
    receive_pieces(pack_ref, own_ref, other_ref, which, height, ROWS)
    unpack_upper(pack_ref, gram_ref, diagonals, None)
    receive_pieces(pack_ref, own_ref, other_ref, which, height, 0)
    unpack_upper(pack_ref, a_ref, None, noise)
    seeds = jnp.concatenate(seeds, 1).astype(jnp.int32)
    shifts = jnp.concatenate(shifts, 1).astype(jnp.int32)
    write_dictionary(act_ref, seeds, shifts, 0, L)
    act = act_ref[...]
    gh, gl = split(gram_ref[...])
    th, tl = split(dot(act, gh) + dot(act, gl))
    half = L // 2
    scale = 1.0 / (L * total_samples)
    top = (dot_t(th[:half], act) + dot_t(tl[:half], act)) * scale
    corner = (dot_halves(th[half:], act[half:], dot_t) + dot_halves(tl[half:], act[half:], dot_t)) * scale
    gram_ref[:half, :] = top
    gram_ref[half:, half:] = corner
    for i in range(NB // 2):
        for j in range(NB // 2, NB):
            gram_ref[j * B : (j + 1) * B, i * B : (i + 1) * B] = top[i * B : (i + 1) * B, j * B : (j + 1) * B].T
    add_diagonal(gram_ref, noise)
    high_ref[...], low_ref[...] = split(gram_ref[...])
    invert(a_ref, x_ref, noise, 2, 4, 1e-4)

    gradient = slopes(x_ref, high_ref, low_ref, dict_ref)
    powers = jnp.maximum(power_ref[...] - gradient, 0.0)
    next_ref[...] = powers
    model_pack(pack_ref, weighted_ref, dict_ref, powers)
    send_pieces(pack_ref, keep_ref, send_ref, which, ROWS, 0)


def third_kernel(
    noise_ref, own_ref, other_ref, dict_ref, high_ref, low_ref, power_ref,
    next_ref, gradient_ref,
    a_ref, x_ref, pack_ref,
):
    which, _ = place_of_device()
    noise = noise_ref[0]
    receive_pieces(pack_ref, own_ref, other_ref, which, ROWS, 0)
    unpack_upper(pack_ref, a_ref, None, noise)
    invert(a_ref, x_ref, noise, 0, 2, 1.6e-7)
    gradient = slopes(x_ref, high_ref, low_ref, dict_ref)
    gradient_ref[...] = gradient
    next_ref[...] = jnp.maximum(power_ref[...] - gradient, 0.0)


def partner(value, masks):
    pairs = [(i, i ^ masks[1 if i & CORE else 0]) for i in range(128)]
    return lax.ppermute(value, AXES, pairs)


def around(stage):
    return [tuple(m << bit for bit in STAGES[stage]) for m in (1, 2, 3)]


def exchange(keep, send, height):
    received = partner(send, (CORE, CORE))
    pieces = [keep[c] + received[c] for c in (slice(n * height, (n + 1) * height) for n in range(4))]
    pieces = lax.optimization_barrier(pieces)
    arrivals = [partner(pieces[n + 1], masks) for n, masks in enumerate(around(0))]
    total = (pieces[0] + arrivals[0]) + (arrivals[1] + arrivals[2])
    for stage in (1, 2):
        arrivals = [partner(total, masks) for masks in around(stage)]
        total = (total + arrivals[0]) + (arrivals[1] + arrivals[2])
    own = jnp.concatenate([total] + [partner(total, masks) for masks in around(3)], 0)
    return own, partner(own, (CORE, CORE))


VM = pl.BlockSpec(memory_space=pltpu.VMEM)
SM = pl.BlockSpec(memory_space=pltpu.SMEM)
HB = pl.BlockSpec(memory_space=pltpu.HBM)


def shards(pilot_seed, delay_shift, active_column, channel, initial_power, noise_power):
    device_count = lax.axis_size("cols") * lax.axis_size("grp")
    total_samples = channel.shape[1] * device_count
    count = delay_shift.shape[0]
    units = pilot_seed.shape[0]
    active_count = active_column.shape[0]
    height = 2 * ROWS + EXTRA
    shape = jax.ShapeDtypeStruct
    row = shape((1, count), f32)
    square = (L, L)
    chunks = 8
    params = pltpu.CompilerParams(vmem_limit_bytes=48 << 20)

    keep, send, dictionary, start_power = pl.pallas_call(
        first_kernel,
        out_shape=(
            shape((4 * height, B), f32), shape((4 * height, B), f32), shape((L, count), bf16), row
        ),
        in_specs=[HB] * 5,
        out_specs=(VM,) * 4,
        scratch_shapes=[
            pltpu.VMEM((chunks, L, channel.shape[1] // chunks), bf16),
            pltpu.VMEM((L, count), bf16),
            pltpu.VMEM((PACK, B), f32),
            pltpu.VMEM((L // 2, L), f32),
            pltpu.VMEM((L // 2, L // 2), f32),
            pltpu.VMEM((1, units), jnp.int32),
            pltpu.VMEM((1, count), jnp.int32),
            pltpu.VMEM((1, active_count), jnp.int32),
            pltpu.SemaphoreType.DMA((chunks,)),
            pltpu.SemaphoreType.DMA((4,)),
        ],
        compiler_params=params,
        name="first",
    )(
        *(
            pltpu.with_memory_space_constraint(value, pltpu.HBM)
            for value in (
                pilot_seed.reshape(1, units), delay_shift.reshape(1, count), initial_power.reshape(1, count),
                active_column.reshape(1, active_count), channel,
            )
        ),
    )
    own, other = exchange(keep, send, height)
    half = shape(square, bf16)
    keep, send, high, low, powers = pl.pallas_call(
        functools.partial(second_kernel, total_samples),
        out_shape=(shape((4 * ROWS, B), f32), shape((4 * ROWS, B), f32), half, half, row),
        in_specs=[SM] + [VM] * 4,
        out_specs=(VM, VM, VM, VM, VM),
        scratch_shapes=[
            pltpu.VMEM(square, f32),
            pltpu.VMEM(square, f32),
            pltpu.VMEM(square, f32),
            pltpu.VMEM((PACK, B), f32),
            pltpu.VMEM(square, bf16),
            pltpu.VMEM((L, count), bf16),
        ],
        compiler_params=params,
        name="second",
    )(noise_power, own, other, dictionary, start_power)
    own, other = exchange(keep, send, ROWS)
    powers, gradient = pl.pallas_call(
        third_kernel,
        out_shape=(row, row),
        in_specs=[SM] + [VM] * 6,
        out_specs=(VM, VM),
        scratch_shapes=[
            pltpu.VMEM(square, f32),
            pltpu.VMEM(square, f32),
            pltpu.VMEM((PACK, B), f32),
        ],
        compiler_params=params,
        name="third",
    )(noise_power, own, other, dictionary, high, low, powers)
    return (powers.reshape(count), gradient.reshape(count))


def solution(mesh):
    placed = (
        P(AXES),
        P(AXES),
        P(),
        P(None, AXES),
        P(AXES),
        P(),
    )
    return jax.shard_map(
        shards,
        mesh=mesh,
        in_specs=placed,
        out_specs=(P(AXES), P(AXES)),
        check_vma=False,
    )
```

```python
import functools
import math

import jax
import jax.numpy as jnp
from jax import lax
from jax.experimental import pallas as pl
from jax.experimental.pallas import tpu as pltpu
from jax.sharding import PartitionSpec as P

L = 512
DELAYS = 8
ITERS = 2
AXES = ("cols", "grp")
CORE = 4
X, Z, Y = 0, 3, 5
STAGES = ((X, Y), (Y, Z), (Z, X), (X, Y))

mult_first = 747796405
mult_second = 289133645
add_first = 1442695041
mult_third = 2073658381

B = 128
NB = L // B
BLOCKS = [(i, j) for i in range(NB) for j in range(i + 1, NB)]
PACK = (len(BLOCKS) + NB // 2) * B
PIECES = 8
ROWS = PACK // PIECES
EXTRA = 8
ORDER = (3, 1, 2)
SLOTS = (0,) + ORDER

f32 = jnp.float32
bf16 = jnp.bfloat16
contract_cols = (((1,), (1,)), ((), ()))


def dot(left, right):
    return jnp.dot(left, right, preferred_element_type=f32)


def dot_t(left, right):
    return lax.dot_general(left, right, contract_cols, preferred_element_type=f32)


def dot_halves(left, right, product):
    axis = 0 if product is dot else 1
    cut = left.shape[1] // 2
    first, second = (slice(0, cut), slice(cut, None))
    pick = (lambda v, c: v[c]) if axis == 0 else (lambda v, c: v[:, c])
    return product(left[:, first], pick(right, first)) + product(left[:, second], pick(right, second))


def split(value):
    high = value.astype(bf16)
    return high, (value - high.astype(f32)).astype(bf16)


def dot_exact(left, right):
    return jnp.dot(left, right, precision=lax.Precision.HIGHEST, preferred_element_type=f32)


def identity_like(value):
    rows = lax.broadcasted_iota(jnp.int32, value.shape, 0)
    cols = lax.broadcasted_iota(jnp.int32, value.shape, 1)
    return rows == cols


def signed(value):
    value %= 1 << 32
    return jnp.int32(value - (1 << 32) if value >= 1 << 31 else value)


def write_dictionary(out_ref, seeds, shifts, first_row, rows):
    low = seeds * signed(mult_first) + signed(add_first) - shifts * signed(mult_second)
    wrapped = low + signed(L * mult_second)
    row = lax.broadcasted_iota(jnp.int32, (rows, B), 0) + first_row
    start = row * signed(mult_second)
    for tile in range(seeds.shape[1] // B):
        cut = slice(tile * B, (tile + 1) * B)
        x = start + jnp.where(row < shifts[:, cut], wrapped[:, cut], low[:, cut])
        x = x ^ lax.shift_right_logical(x, 15)
        x = x * signed(mult_third)
        x = (x ^ lax.shift_right_logical(x, 13)) & signed(1 << 11)
        value = jnp.where(x == 0, jnp.float32(1), jnp.float32(-1))
        out_ref[first_row : first_row + rows, cut] = value.astype(bf16)


def block_order(shape):
    return lax.broadcasted_iota(jnp.int32, shape, 0), lax.broadcasted_iota(jnp.int32, shape, 1)


def pack_upper(pack_ref, top, corner):
    def block(i, j):
        if i < NB // 2:
            return top[i * B : (i + 1) * B, j * B : (j + 1) * B]
        i, j = i - NB // 2, j - NB // 2
        return corner[i * B : (i + 1) * B, j * B : (j + 1) * B]

    for number, (i, j) in enumerate(BLOCKS):
        pack_ref[number * B : (number + 1) * B, :] = block(i, j)
    row, col = block_order((B, B))
    for pair in range(NB // 2):
        number = len(BLOCKS) + pair
        both = jnp.where(row <= col, block(2 * pair, 2 * pair), block(2 * pair + 1, 2 * pair + 1))
        pack_ref[number * B : (number + 1) * B, :] = both


def diagonal_of(block):
    row, col = block_order(block.shape)
    return jnp.sum(jnp.where(row == col, block, 0.0), axis=0, keepdims=True)


def unpack_upper(pack_ref, out_ref, diagonals, shift):
    for number, (i, j) in enumerate(BLOCKS):
        block = pack_ref[number * B : (number + 1) * B, :]
        out_ref[i * B : (i + 1) * B, j * B : (j + 1) * B] = block
        out_ref[j * B : (j + 1) * B, i * B : (i + 1) * B] = block.T
    row, col = block_order((B, B))
    for pair in range(NB // 2):
        number = len(BLOCKS) + pair
        both = pack_ref[number * B : (number + 1) * B, :]
        turned = both.T
        upper = jnp.where(row <= col, both, turned)
        lower = jnp.where(row > col, both, turned)
        if diagonals is not None:
            lower = jnp.where(row == col, diagonals[pair], lower)
        for i, value in ((2 * pair, upper), (2 * pair + 1, lower)):
            if shift is not None:
                value = jnp.where(row == col, value + shift, value)
            out_ref[i * B : (i + 1) * B, i * B : (i + 1) * B] = value


def place_of_device():
    position = lax.axis_index("cols").astype(jnp.int32) * 4 + lax.axis_index("grp").astype(jnp.int32)
    core = lax.shift_right_logical(position, 2) & 1
    first, second = [lax.shift_right_logical(position, bit) & 3 for bit in STAGES[0]]
    own = jnp.where(core == 0, first, second)
    return own + 4 * (first + second - own) + 16 * core, position


def piece(which, place):
    core = lax.shift_right_logical(which, 4) & 1
    if place < PIECES // 2:
        number = core * 4 + ((which & 3) ^ place)
    else:
        number = (1 - core) * 4 + ((lax.shift_right_logical(which, 2) & 3) ^ (place - 4))
    return pl.multiple_of(number * ROWS, ROWS)


def extra_row(which, number, height, slots):
    core = lax.shift_right_logical(which, 4) & 1
    position = jnp.where(core == 0, which, lax.shift_right_logical(which, 2)) & 3
    place = position ^ number
    slot = sum(jnp.where(place == p, n, 0) for n, p in enumerate(slots))
    return pl.multiple_of(slot * height + 2 * ROWS, 8)


def send_pieces(pack_ref, keep_ref, send_ref, which, height, offset):
    half = PIECES // 2
    for place in range(PIECES):
        target, at = (keep_ref, place) if place < half else (send_ref, place - half)
        start = at * height + offset
        target[start : start + ROWS, :] = pack_ref[pl.ds(piece(which, place), ROWS), :]


def receive_pieces(pack_ref, own_ref, other_ref, which, height, offset):
    half = PIECES // 2
    for slot, place in enumerate(SLOTS):
        start = slot * height + offset
        for source, at in ((own_ref, place), (other_ref, place + half)):
            pack_ref[pl.ds(piece(which, at), ROWS), :] = source[start : start + ROWS, :]


def model_pack(pack_ref, weighted_ref, dict_ref, powers):
    high, low = split(powers)
    half = L // 2
    top = corner = None
    for part in (low, high):
        weighted_ref[...] = dict_ref[...] * part
        a = dot_t(weighted_ref[:half, :], dict_ref[...])
        c = dot_halves(weighted_ref[half:, :], dict_ref[half:, :], dot_t)
        top, corner = (a, c) if top is None else (top + a, corner + c)
    pack_upper(pack_ref, top * (1.0 / L), corner * (1.0 / L))


def first_kernel(
    seed_hbm, shift_hbm, power_hbm, active_hbm, channel_hbm,
    keep_ref, send_ref, dict_ref, power_ref,
    chan_ref, weighted_ref, pack_ref, top_ref, corner_ref, seed_ref, shift_ref, active_ref,
    chan_sems, row_sems,
):
    which, position = place_of_device()
    chunks = chan_ref.shape[0]
    width = chan_ref.shape[2]
    rows = [(seed_hbm, seed_ref), (shift_hbm, shift_ref), (active_hbm, active_ref), (power_hbm, power_ref)]
    row_copies = [pltpu.make_async_copy(a, b, row_sems.at[n]) for n, (a, b) in enumerate(rows)]
    copies = [
        pltpu.make_async_copy(
            channel_hbm.at[:, n * width : (n + 1) * width], chan_ref.at[n], chan_sems.at[n]
        )
        for n in range(chunks)
    ]
    for copy in row_copies + copies:
        copy.start()
    for copy in row_copies:
        copy.wait()
    height = 2 * ROWS + EXTRA
    half = L // 2
    step = L // chunks

    def gram(n):
        copies[n].wait()
        block = chan_ref[n]
        a = dot_t(block[:half], block)
        c = dot_halves(block[half:], block[half:], dot_t)
        if n == 0:
            top_ref[...] = a
            corner_ref[...] = c
        else:
            top_ref[...] += a
            corner_ref[...] += c

    gram(0)
    units = seed_ref[...]
    shifts = shift_ref[...]
    count = shifts.shape[1]

    def in_bytes(value, number):
        return [lax.shift_right_logical(value, 8 * n) & 255 for n in range(number)]

    def table_of(parts, width):
        parts = parts + [jnp.zeros((16 - len(parts), width), jnp.int32)]
        return jnp.concatenate(parts, 0).astype(f32).astype(bf16)

    def chosen(hit):
        return jnp.where(hit, jnp.float32(1), jnp.float32(0)).astype(bf16)

    shape = (units.shape[1], count)
    user = lax.shift_right_logical(lax.broadcasted_iota(jnp.int32, shape, 1), int(math.log2(DELAYS)))
    spread = dot(table_of(in_bytes(units, 3), units.shape[1]), chosen(lax.broadcasted_iota(jnp.int32, shape, 0) == user))
    seed_bytes = [spread[n : n + 1].astype(jnp.int32) for n in range(3)]
    seeds = seed_bytes[0] + seed_bytes[1] * 256 + seed_bytes[2] * 65536

    local = active_ref[...] - position * count
    hit = lax.broadcasted_iota(jnp.int32, (count, local.shape[1]), 0) == local
    found = dot(table_of(seed_bytes + in_bytes(shifts, 2), count), chosen(hit))
    seeds_here = found[0:1] + 256.0 * found[1:2] + 65536.0 * found[2:3]
    shifts_here = found[3:4] + 256.0 * found[4:5]
    for n in range(1, chunks):
        gram(n)
        write_dictionary(dict_ref, seeds, shifts, (n - 1) * step, step)
    write_dictionary(dict_ref, seeds, shifts, (chunks - 1) * step, step)
    pack_upper(pack_ref, top_ref[...], corner_ref[...])
    send_pieces(pack_ref, keep_ref, send_ref, which, height, ROWS)
    core = lax.shift_right_logical(which, 4) & 1
    for number in range(NB):
        cut = slice(number * B, (number + 1) * B)
        rows = [seeds_here[:, cut], shifts_here[:, cut]]
        if number < NB // 2:
            cut = slice(B, 2 * B)
            rows.append(diagonal_of((top_ref if number == 0 else corner_ref)[cut, cut]))
        tile = jnp.concatenate(rows + [jnp.zeros((EXTRA - len(rows), B), f32)], 0)
        start = extra_row(which, number, height, range(PIECES // 2))
        keep_ref[pl.ds(start, EXTRA), :] = jnp.where(core == 0, tile, 0.0)
        send_ref[pl.ds(start, EXTRA), :] = jnp.where(core == 0, 0.0, tile)
    model_pack(pack_ref, weighted_ref, dict_ref, power_ref[...])
    send_pieces(pack_ref, keep_ref, send_ref, which, height, 0)


def invert(a_ref, x_ref, noise, squarings, terms, small):
    eye = identity_like(a_ref)
    one = jnp.where(eye, 1.0, 0.0).astype(f32)
    mean = a_ref[0:1, 0:1]
    b = a_ref[...] - mean * one
    bh, bl = split(b)
    b2 = dot(bh, bh)
    fourth = jnp.sum(jnp.sum(b2 * b2, axis=0, keepdims=True), axis=1, keepdims=True)
    reach = 1.02 * jnp.sqrt(jnp.sqrt(fourth))
    centre = 0.5 * (jnp.maximum(noise, mean - reach) + mean + reach)
    inv = 1.0 / centre
    e0 = (centre - mean) * inv
    e2 = (e0 * e0) * one - b * (2.0 * e0 * inv) + b2 * (inv * inv)
    power = e2.astype(bf16)
    x = ((1.0 + e0) * (one + e2) - (b + dot(bh, power)) * inv) * inv
    for _ in range(squarings):
        power = dot(power, power).astype(bf16)
        x = x + dot(x.astype(bf16), power)

    def refine(x):
        r = one - x.astype(f32) * mean - (dot(bh, x) + dot(bl, x))
        rb = r.astype(bf16)
        r2 = dot(rb, rb)
        near = r + r2
        total = near + dot(r2.astype(bf16), near.astype(bf16)) if terms == 4 else near
        th, tl = split(total)
        update = dot(x, th) + dot(x, tl) if terms == 4 else dot(x, th)
        x_ref[...] = x.astype(f32) + update
        return jnp.sum(r2 * r2)

    size = refine(x.astype(bf16))

    @pl.when(jnp.logical_not(size < small))
    def _():
        def more(state):
            count, size = state
            return jnp.logical_and(count < 12, jnp.logical_and(size > small, size < 1e8))

        def step(state):
            count, size = state
            return count + 1, refine(x_ref[...].astype(bf16))

        count, last = lax.while_loop(more, step, (jnp.int32(0), size))

        @pl.when(jnp.logical_not(last < small))
        def _():
            bound = jnp.max(jnp.sum(jnp.abs(a_ref[...]), axis=0, keepdims=True))
            x_ref[...] = one * (1.0 / bound)

            def more(state):
                count, size, before = state
                going = jnp.logical_or(size > 1e-2, size < 0.25 * before)
                return jnp.logical_and(count < 48, jnp.logical_and(size > 1e-12, going))

            def step(state):
                count, size, before = state
                x = x_ref[...]
                r = one - dot_exact(a_ref[...], x)
                x_ref[...] = x + dot_exact(x, r)
                return count + 1, jnp.sum(r * r), size

            lax.while_loop(more, step, (jnp.int32(0), jnp.float32(1e30), jnp.float32(1e38)))


def slopes(x_ref, high_ref, low_ref, dict_ref):
    x = x_ref[...]
    xh, xl = split(x)
    right = dot(high_ref[...], xh) + (dot(high_ref[...], xl) + dot(low_ref[...], xh))
    rh, rl = split(right)
    half = L // 2
    d = dict_ref[...]
    result = None
    for rows, cols in ((slice(0, half), slice(0, L)), (slice(half, L), slice(half, L))):
        lh, ll = xh[rows], xl[rows]
        if rows == cols:
            ch, cl = rh[:, cols], rl[:, cols]
            form = x[rows, cols] - (
                dot_halves(lh, ch, dot) + (dot_halves(lh, cl, dot) + dot_halves(ll, ch, dot))
            )
        else:
            form = x[rows] - (dot(lh, rh) + (dot(lh, rl) + dot(ll, rh)))
            form = jnp.concatenate([form[:, :half], 2.0 * form[:, half:]], 1)
        fh, fl = split(form)
        mapped = dot(fh, d[cols]) + dot(fl, d[cols])
        part = jnp.sum(mapped * d[rows].astype(f32), axis=0, keepdims=True)
        result = part if result is None else result + part
    return result * (1.0 / L)


def add_diagonal(ref, noise):
    for n in range(NB):
        cut = slice(n * B, (n + 1) * B)
        block = ref[cut, cut]
        ref[cut, cut] = jnp.where(identity_like(block), block + noise, block)


def second_kernel(
    total_samples,
    noise_ref, own_ref, other_ref, dict_ref, power_ref,
    keep_ref, send_ref, high_ref, low_ref, next_ref,
    a_ref, gram_ref, x_ref, pack_ref, act_ref, weighted_ref,
):
    which, _ = place_of_device()
    noise = noise_ref[0]
    height = 2 * ROWS + EXTRA
    seeds, shifts, diagonals = [], [], []
    for number in range(NB):
        start = extra_row(which, number, height, SLOTS)
        near = own_ref[pl.ds(start, EXTRA), :]
        far = other_ref[pl.ds(start, EXTRA), :]
        tile = jnp.where(lax.shift_right_logical(which, 4) & 1 == 0, near, far)
        seeds.append(tile[0:1])
        shifts.append(tile[1:2])
        diagonals.append(tile[2:3])
    receive_pieces(pack_ref, own_ref, other_ref, which, height, ROWS)
    unpack_upper(pack_ref, gram_ref, diagonals, None)
    receive_pieces(pack_ref, own_ref, other_ref, which, height, 0)
    unpack_upper(pack_ref, a_ref, None, noise)
    seeds = jnp.concatenate(seeds, 1).astype(jnp.int32)
    shifts = jnp.concatenate(shifts, 1).astype(jnp.int32)
    write_dictionary(act_ref, seeds, shifts, 0, L)
    act = act_ref[...]
    gh, gl = split(gram_ref[...])
    th, tl = split(dot(act, gh) + dot(act, gl))
    half = L // 2
    scale = 1.0 / (L * total_samples)
    top = (dot_t(th[:half], act) + dot_t(tl[:half], act)) * scale
    corner = (dot_halves(th[half:], act[half:], dot_t) + dot_halves(tl[half:], act[half:], dot_t)) * scale
    gram_ref[:half, :] = top
    gram_ref[half:, half:] = corner
    for i in range(NB // 2):
        for j in range(NB // 2, NB):
            gram_ref[j * B : (j + 1) * B, i * B : (i + 1) * B] = top[i * B : (i + 1) * B, j * B : (j + 1) * B].T
    add_diagonal(gram_ref, noise)
    high_ref[...], low_ref[...] = split(gram_ref[...])
    invert(a_ref, x_ref, noise, 2, 4, 1e-4)

    gradient = slopes(x_ref, high_ref, low_ref, dict_ref)
    powers = jnp.maximum(power_ref[...] - gradient, 0.0)
    next_ref[...] = powers
    model_pack(pack_ref, weighted_ref, dict_ref, powers)
    send_pieces(pack_ref, keep_ref, send_ref, which, ROWS, 0)


def third_kernel(
    noise_ref, own_ref, other_ref, dict_ref, high_ref, low_ref, power_ref,
    next_ref, gradient_ref,
    a_ref, x_ref, pack_ref,
):
    which, _ = place_of_device()
    noise = noise_ref[0]
    receive_pieces(pack_ref, own_ref, other_ref, which, ROWS, 0)
    unpack_upper(pack_ref, a_ref, None, noise)
    invert(a_ref, x_ref, noise, 0, 2, 1.6e-7)
    gradient = slopes(x_ref, high_ref, low_ref, dict_ref)
    gradient_ref[...] = gradient
    next_ref[...] = jnp.maximum(power_ref[...] - gradient, 0.0)


def partner(value, masks):
    pairs = [(i, i ^ masks[1 if i & CORE else 0]) for i in range(128)]
    return lax.ppermute(value, AXES, pairs)


def around(stage, order):
    return [tuple(m << bit for bit in STAGES[stage]) for m in order]


def exchange(keep, send, height):
    received = partner(send, (CORE, CORE))
    pieces = [keep[c] + received[c] for c in (slice(n * height, (n + 1) * height) for n in range(4))]
    pieces = lax.optimization_barrier(pieces)
    order = (3, 2, 1)
    total = pieces[0]
    for arrived in [partner(pieces[m], masks) for m, masks in zip(order, around(0, order))]:
        total = total + arrived
    for stage in (1, 2):
        total = lax.optimization_barrier(total)
        for arrived in [partner(total, masks) for masks in around(stage, ORDER)]:
            total = total + arrived
    total = lax.optimization_barrier(total)
    own = jnp.concatenate([total] + [partner(total, masks) for masks in around(3, ORDER)], 0)
    return own, partner(own, (CORE, CORE))


VM = pl.BlockSpec(memory_space=pltpu.VMEM)
SM = pl.BlockSpec(memory_space=pltpu.SMEM)
HB = pl.BlockSpec(memory_space=pltpu.HBM)


def shards(pilot_seed, delay_shift, active_column, channel, initial_power, noise_power):
    device_count = lax.axis_size("cols") * lax.axis_size("grp")
    total_samples = channel.shape[1] * device_count
    count = delay_shift.shape[0]
    units = pilot_seed.shape[0]
    active_count = active_column.shape[0]
    height = 2 * ROWS + EXTRA
    shape = jax.ShapeDtypeStruct
    row = shape((1, count), f32)
    square = (L, L)
    chunks = 8
    params = pltpu.CompilerParams(vmem_limit_bytes=48 << 20)

    keep, send, dictionary, start_power = pl.pallas_call(
        first_kernel,
        out_shape=(
            shape((4 * height, B), f32), shape((4 * height, B), f32), shape((L, count), bf16), row
        ),
        in_specs=[HB] * 5,
        out_specs=(VM,) * 4,
        scratch_shapes=[
            pltpu.VMEM((chunks, L, channel.shape[1] // chunks), bf16),
            pltpu.VMEM((L, count), bf16),
            pltpu.VMEM((PACK, B), f32),
            pltpu.VMEM((L // 2, L), f32),
            pltpu.VMEM((L // 2, L // 2), f32),
            pltpu.VMEM((1, units), jnp.int32),
            pltpu.VMEM((1, count), jnp.int32),
            pltpu.VMEM((1, active_count), jnp.int32),
            pltpu.SemaphoreType.DMA((chunks,)),
            pltpu.SemaphoreType.DMA((4,)),
        ],
        compiler_params=params,
        name="first",
    )(
        *(
            pltpu.with_memory_space_constraint(value, pltpu.HBM)
            for value in (
                pilot_seed.reshape(1, units), delay_shift.reshape(1, count), initial_power.reshape(1, count),
                active_column.reshape(1, active_count), channel,
            )
        ),
    )
    own, other = exchange(keep, send, height)
    half = shape(square, bf16)
    keep, send, high, low, powers = pl.pallas_call(
        functools.partial(second_kernel, total_samples),
        out_shape=(shape((4 * ROWS, B), f32), shape((4 * ROWS, B), f32), half, half, row),
        in_specs=[SM] + [VM] * 4,
        out_specs=(VM, VM, VM, VM, VM),
        scratch_shapes=[
            pltpu.VMEM(square, f32),
            pltpu.VMEM(square, f32),
            pltpu.VMEM(square, f32),
            pltpu.VMEM((PACK, B), f32),
            pltpu.VMEM(square, bf16),
            pltpu.VMEM((L, count), bf16),
        ],
        compiler_params=params,
        name="second",
    )(noise_power, own, other, dictionary, start_power)
    own, other = exchange(keep, send, ROWS)
    powers, gradient = pl.pallas_call(
        third_kernel,
        out_shape=(row, row),
        in_specs=[SM] + [VM] * 6,
        out_specs=(VM, VM),
        scratch_shapes=[
            pltpu.VMEM(square, f32),
            pltpu.VMEM(square, f32),
            pltpu.VMEM((PACK, B), f32),
        ],
        compiler_params=params,
        name="third",
    )(noise_power, own, other, dictionary, high, low, powers)
    return (powers.reshape(count), gradient.reshape(count))


def solution(mesh):
    placed = (
        P(AXES),
        P(AXES),
        P(),
        P(None, AXES),
        P(AXES),
        P(),
    )
    return jax.shard_map(
        shards,
        mesh=mesh,
        in_specs=placed,
        out_specs=(P(AXES), P(AXES)),
        check_vma=False,
    )
```

```python
import functools
import math

import jax
import jax.numpy as jnp
from jax import lax
from jax.experimental import pallas as pl
from jax.experimental.pallas import tpu as pltpu
from jax.sharding import PartitionSpec as P

L = 512
DELAYS = 8
ITERS = 2
AXES = ("cols", "grp")
CORE = 4
X, Z, Y = 0, 3, 5
STAGES = ((X, Y), (Y, Z), (Z, X), (X, Y))

mult_first = 747796405
mult_second = 289133645
add_first = 1442695041
mult_third = 2073658381

B = 128
NB = L // B
BLOCKS = [(i, j) for i in range(NB) for j in range(i + 1, NB)]
PACK = (len(BLOCKS) + NB // 2) * B
PIECES = 8
ROWS = PACK // PIECES
EXTRA = 8
ORDER = (3, 1, 2)
SLOTS = (0,) + ORDER

f32 = jnp.float32
bf16 = jnp.bfloat16
contract_cols = (((1,), (1,)), ((), ()))


def dot(left, right):
    return jnp.dot(left, right, preferred_element_type=f32)


def dot_t(left, right):
    return lax.dot_general(left, right, contract_cols, preferred_element_type=f32)


def dot_halves(left, right, product):
    axis = 0 if product is dot else 1
    cut = left.shape[1] // 2
    first, second = (slice(0, cut), slice(cut, None))
    pick = (lambda v, c: v[c]) if axis == 0 else (lambda v, c: v[:, c])
    return product(left[:, first], pick(right, first)) + product(left[:, second], pick(right, second))


def split(value):
    high = value.astype(bf16)
    return high, (value - high.astype(f32)).astype(bf16)


def dot_exact(left, right):
    return jnp.dot(left, right, precision=lax.Precision.HIGHEST, preferred_element_type=f32)


def identity_like(value):
    rows = lax.broadcasted_iota(jnp.int32, value.shape, 0)
    cols = lax.broadcasted_iota(jnp.int32, value.shape, 1)
    return rows == cols


def signed(value):
    value %= 1 << 32
    return jnp.int32(value - (1 << 32) if value >= 1 << 31 else value)


def write_dictionary(out_ref, seeds, shifts, first_row, rows):
    low = seeds * signed(mult_first) + signed(add_first) - shifts * signed(mult_second)
    wrapped = low + signed(L * mult_second)
    row = lax.broadcasted_iota(jnp.int32, (rows, B), 0) + first_row
    start = row * signed(mult_second)
    for tile in range(seeds.shape[1] // B):
        cut = slice(tile * B, (tile + 1) * B)
        x = start + jnp.where(row < shifts[:, cut], wrapped[:, cut], low[:, cut])
        x = x ^ lax.shift_right_logical(x, 15)
        x = x * signed(mult_third)
        x = (x ^ lax.shift_right_logical(x, 13)) & signed(1 << 11)
        value = jnp.where(x == 0, jnp.float32(1), jnp.float32(-1))
        out_ref[first_row : first_row + rows, cut] = value.astype(bf16)


def block_order(shape):
    return lax.broadcasted_iota(jnp.int32, shape, 0), lax.broadcasted_iota(jnp.int32, shape, 1)


def pack_upper(pack_ref, top, corner):
    def block(i, j):
        if i < NB // 2:
            return top[i * B : (i + 1) * B, j * B : (j + 1) * B]
        i, j = i - NB // 2, j - NB // 2
        return corner[i * B : (i + 1) * B, j * B : (j + 1) * B]

    for number, (i, j) in enumerate(BLOCKS):
        pack_ref[number * B : (number + 1) * B, :] = block(i, j)
    row, col = block_order((B, B))
    for pair in range(NB // 2):
        number = len(BLOCKS) + pair
        both = jnp.where(row <= col, block(2 * pair, 2 * pair), block(2 * pair + 1, 2 * pair + 1))
        pack_ref[number * B : (number + 1) * B, :] = both


def diagonal_of(block):
    row, col = block_order(block.shape)
    return jnp.sum(jnp.where(row == col, block, 0.0), axis=0, keepdims=True)


def unpack_upper(pack_ref, out_ref, diagonals, shift):
    for number, (i, j) in enumerate(BLOCKS):
        block = pack_ref[number * B : (number + 1) * B, :]
        out_ref[i * B : (i + 1) * B, j * B : (j + 1) * B] = block
        out_ref[j * B : (j + 1) * B, i * B : (i + 1) * B] = block.T
    row, col = block_order((B, B))
    for pair in range(NB // 2):
        number = len(BLOCKS) + pair
        both = pack_ref[number * B : (number + 1) * B, :]
        turned = both.T
        upper = jnp.where(row <= col, both, turned)
        lower = jnp.where(row > col, both, turned)
        if diagonals is not None:
            lower = jnp.where(row == col, diagonals[pair], lower)
        for i, value in ((2 * pair, upper), (2 * pair + 1, lower)):
            if shift is not None:
                value = jnp.where(row == col, value + shift, value)
            out_ref[i * B : (i + 1) * B, i * B : (i + 1) * B] = value


def place_of_device():
    position = lax.axis_index("cols").astype(jnp.int32) * 4 + lax.axis_index("grp").astype(jnp.int32)
    core = lax.shift_right_logical(position, 2) & 1
    first, second = [lax.shift_right_logical(position, bit) & 3 for bit in STAGES[0]]
    own = jnp.where(core == 0, first, second)
    return own + 4 * (first + second - own) + 16 * core, position


def piece(which, place):
    core = lax.shift_right_logical(which, 4) & 1
    if place < PIECES // 2:
        number = core * 4 + ((which & 3) ^ place)
    else:
        number = (1 - core) * 4 + ((lax.shift_right_logical(which, 2) & 3) ^ (place - 4))
    return pl.multiple_of(number * ROWS, ROWS)


def extra_row(which, number, height, slots):
    core = lax.shift_right_logical(which, 4) & 1
    position = jnp.where(core == 0, which, lax.shift_right_logical(which, 2)) & 3
    place = position ^ number
    slot = sum(jnp.where(place == p, n, 0) for n, p in enumerate(slots))
    return pl.multiple_of(slot * height + 2 * ROWS, 8)


def send_pieces(pack_ref, keep_ref, send_ref, which, height, offset):
    half = PIECES // 2
    for place in range(PIECES):
        target, at = (keep_ref, place) if place < half else (send_ref, place - half)
        start = at * height + offset
        target[start : start + ROWS, :] = pack_ref[pl.ds(piece(which, place), ROWS), :]


def receive_pieces(pack_ref, own_ref, other_ref, which, height, offset):
    half = PIECES // 2
    for slot, place in enumerate(SLOTS):
        start = slot * height + offset
        for source, at in ((own_ref, place), (other_ref, place + half)):
            pack_ref[pl.ds(piece(which, at), ROWS), :] = source[start : start + ROWS, :]


def model_pack(pack_ref, weighted_ref, dict_ref, powers):
    high, low = split(powers)
    half = L // 2
    top = corner = None
    for part in (low, high):
        weighted_ref[...] = dict_ref[...] * part
        a = dot_t(weighted_ref[:half, :], dict_ref[...])
        c = dot_halves(weighted_ref[half:, :], dict_ref[half:, :], dot_t)
        top, corner = (a, c) if top is None else (top + a, corner + c)
    pack_upper(pack_ref, top * (1.0 / L), corner * (1.0 / L))


def first_kernel(
    seed_hbm, shift_hbm, power_hbm, active_hbm, channel_hbm,
    keep_ref, send_ref, dict_ref, power_ref,
    chan_ref, weighted_ref, pack_ref, top_ref, corner_ref, seed_ref, shift_ref, active_ref,
    chan_sems, row_sems,
):
    which, position = place_of_device()
    chunks = chan_ref.shape[0]
    width = chan_ref.shape[2]
    rows = [(seed_hbm, seed_ref), (shift_hbm, shift_ref), (active_hbm, active_ref), (power_hbm, power_ref)]
    row_copies = [pltpu.make_async_copy(a, b, row_sems.at[n]) for n, (a, b) in enumerate(rows)]
    copies = [
        pltpu.make_async_copy(
            channel_hbm.at[:, n * width : (n + 1) * width], chan_ref.at[n], chan_sems.at[n]
        )
        for n in range(chunks)
    ]
    for copy in row_copies + copies:
        copy.start()
    height = 2 * ROWS + EXTRA
    half = L // 2
    step = L // chunks

    def gram(n):
        copies[n].wait()
        block = chan_ref[n]
        a = dot_t(block[:half], block)
        c = dot_halves(block[half:], block[half:], dot_t)
        if n == 0:
            top_ref[...] = a
            corner_ref[...] = c
        else:
            top_ref[...] += a
            corner_ref[...] += c

    for n in range(2):
        gram(n)
    for copy in row_copies:
        copy.wait()
    units = seed_ref[...]
    shifts = shift_ref[...]
    count = shifts.shape[1]

    def in_bytes(value, number):
        return [lax.shift_right_logical(value, 8 * n) & 255 for n in range(number)]

    def table_of(parts, width):
        parts = parts + [jnp.zeros((16 - len(parts), width), jnp.int32)]
        return jnp.concatenate(parts, 0).astype(f32).astype(bf16)

    def chosen(hit):
        return jnp.where(hit, jnp.float32(1), jnp.float32(0)).astype(bf16)

    shape = (units.shape[1], count)
    user = lax.shift_right_logical(lax.broadcasted_iota(jnp.int32, shape, 1), int(math.log2(DELAYS)))
    spread = dot(table_of(in_bytes(units, 3), units.shape[1]), chosen(lax.broadcasted_iota(jnp.int32, shape, 0) == user))
    seed_bytes = [spread[n : n + 1].astype(jnp.int32) for n in range(3)]
    seeds = seed_bytes[0] + seed_bytes[1] * 256 + seed_bytes[2] * 65536

    local = active_ref[...] - position * count
    hit = lax.broadcasted_iota(jnp.int32, (count, local.shape[1]), 0) == local
    found = dot(table_of(seed_bytes + in_bytes(shifts, 2), count), chosen(hit))
    seeds_here = found[0:1] + 256.0 * found[1:2] + 65536.0 * found[2:3]
    shifts_here = found[3:4] + 256.0 * found[4:5]
    for n in range(chunks):
        if n >= 2:
            gram(n)
        write_dictionary(dict_ref, seeds, shifts, n * step, step)
    pack_upper(pack_ref, top_ref[...], corner_ref[...])
    send_pieces(pack_ref, keep_ref, send_ref, which, height, ROWS)
    core = lax.shift_right_logical(which, 4) & 1
    for number in range(NB):
        cut = slice(number * B, (number + 1) * B)
        rows = [seeds_here[:, cut], shifts_here[:, cut]]
        if number < NB // 2:
            cut = slice(B, 2 * B)
            rows.append(diagonal_of((top_ref if number == 0 else corner_ref)[cut, cut]))
        tile = jnp.concatenate(rows + [jnp.zeros((EXTRA - len(rows), B), f32)], 0)
        start = extra_row(which, number, height, range(PIECES // 2))
        keep_ref[pl.ds(start, EXTRA), :] = jnp.where(core == 0, tile, 0.0)
        send_ref[pl.ds(start, EXTRA), :] = jnp.where(core == 0, 0.0, tile)
    model_pack(pack_ref, weighted_ref, dict_ref, power_ref[...])
    send_pieces(pack_ref, keep_ref, send_ref, which, height, 0)


def invert(a_ref, x_ref, noise, squarings, terms, small):
    eye = identity_like(a_ref)
    one = jnp.where(eye, 1.0, 0.0).astype(f32)
    mean = a_ref[0:1, 0:1]
    b = a_ref[...] - mean * one
    bh, bl = split(b)
    b2 = dot(bh, bh)
    fourth = jnp.sum(jnp.sum(b2 * b2, axis=0, keepdims=True), axis=1, keepdims=True)
    reach = 1.02 * jnp.sqrt(jnp.sqrt(fourth))
    centre = 0.5 * (jnp.maximum(noise, mean - reach) + mean + reach)
    inv = 1.0 / centre
    e0 = (centre - mean) * inv
    e2 = (e0 * e0) * one - b * (2.0 * e0 * inv) + b2 * (inv * inv)
    power = e2.astype(bf16)
    x = ((1.0 + e0) * (one + e2) - (b + dot(bh, power)) * inv) * inv
    for _ in range(squarings):
        power = dot(power, power).astype(bf16)
        x = x + dot(x.astype(bf16), power)

    def refine(x):
        r = one - x.astype(f32) * mean - (dot(bh, x) + dot(bl, x))
        rb = r.astype(bf16)
        r2 = dot(rb, rb)
        near = r + r2
        total = near + dot(r2.astype(bf16), near.astype(bf16)) if terms == 4 else near
        th, tl = split(total)
        update = dot(x, th) + dot(x, tl) if terms == 4 else dot(x, th)
        x_ref[...] = x.astype(f32) + update
        return jnp.sum(r2 * r2)

    size = refine(x.astype(bf16))

    @pl.when(jnp.logical_not(size < small))
    def _():
        def more(state):
            count, size = state
            return jnp.logical_and(count < 12, jnp.logical_and(size > small, size < 1e8))

        def step(state):
            count, size = state
            return count + 1, refine(x_ref[...].astype(bf16))

        count, last = lax.while_loop(more, step, (jnp.int32(0), size))

        @pl.when(jnp.logical_not(last < small))
        def _():
            bound = jnp.max(jnp.sum(jnp.abs(a_ref[...]), axis=0, keepdims=True))
            x_ref[...] = one * (1.0 / bound)

            def more(state):
                count, size, before = state
                going = jnp.logical_or(size > 1e-2, size < 0.25 * before)
                return jnp.logical_and(count < 48, jnp.logical_and(size > 1e-12, going))

            def step(state):
                count, size, before = state
                x = x_ref[...]
                r = one - dot_exact(a_ref[...], x)
                x_ref[...] = x + dot_exact(x, r)
                return count + 1, jnp.sum(r * r), size

            lax.while_loop(more, step, (jnp.int32(0), jnp.float32(1e30), jnp.float32(1e38)))


def slopes(x_ref, high_ref, low_ref, dict_ref):
    x = x_ref[...]
    xh, xl = split(x)
    right = dot(high_ref[...], xh) + (dot(high_ref[...], xl) + dot(low_ref[...], xh))
    rh, rl = split(right)
    half = L // 2
    d = dict_ref[...]
    result = None
    for rows, cols in ((slice(0, half), slice(0, L)), (slice(half, L), slice(half, L))):
        lh, ll = xh[rows], xl[rows]
        if rows == cols:
            ch, cl = rh[:, cols], rl[:, cols]
            form = x[rows, cols] - (
                dot_halves(lh, ch, dot) + (dot_halves(lh, cl, dot) + dot_halves(ll, ch, dot))
            )
        else:
            form = x[rows] - (dot(lh, rh) + (dot(lh, rl) + dot(ll, rh)))
            form = jnp.concatenate([form[:, :half], 2.0 * form[:, half:]], 1)
        fh, fl = split(form)
        mapped = dot(fh, d[cols]) + dot(fl, d[cols])
        part = jnp.sum(mapped * d[rows].astype(f32), axis=0, keepdims=True)
        result = part if result is None else result + part
    return result * (1.0 / L)


def add_diagonal(ref, noise):
    for n in range(NB):
        cut = slice(n * B, (n + 1) * B)
        block = ref[cut, cut]
        ref[cut, cut] = jnp.where(identity_like(block), block + noise, block)


def second_kernel(
    total_samples,
    noise_ref, own_ref, other_ref, dict_ref, power_ref,
    keep_ref, send_ref, high_ref, low_ref, next_ref,
    a_ref, gram_ref, x_ref, pack_ref, act_ref, weighted_ref,
):
    which, _ = place_of_device()
    noise = noise_ref[0:1, 0:1]
    height = 2 * ROWS + EXTRA
    seeds, shifts, diagonals = [], [], []
    for number in range(NB):
        start = extra_row(which, number, height, SLOTS)
        near = own_ref[pl.ds(start, EXTRA), :]
        far = other_ref[pl.ds(start, EXTRA), :]
        tile = jnp.where(lax.shift_right_logical(which, 4) & 1 == 0, near, far)
        seeds.append(tile[0:1])
        shifts.append(tile[1:2])
        diagonals.append(tile[2:3])
    receive_pieces(pack_ref, own_ref, other_ref, which, height, ROWS)
    unpack_upper(pack_ref, gram_ref, diagonals, None)
    receive_pieces(pack_ref, own_ref, other_ref, which, height, 0)
    unpack_upper(pack_ref, a_ref, None, noise)
    seeds = jnp.concatenate(seeds, 1).astype(jnp.int32)
    shifts = jnp.concatenate(shifts, 1).astype(jnp.int32)
    write_dictionary(act_ref, seeds, shifts, 0, L)
    act = act_ref[...]
    gh, gl = split(gram_ref[...])
    th, tl = split(dot(act, gh) + dot(act, gl))
    half = L // 2
    scale = 1.0 / (L * total_samples)
    top = (dot_t(th[:half], act) + dot_t(tl[:half], act)) * scale
    corner = (dot_halves(th[half:], act[half:], dot_t) + dot_halves(tl[half:], act[half:], dot_t)) * scale
    gram_ref[:half, :] = top
    gram_ref[half:, half:] = corner
    for i in range(NB // 2):
        for j in range(NB // 2, NB):
            gram_ref[j * B : (j + 1) * B, i * B : (i + 1) * B] = top[i * B : (i + 1) * B, j * B : (j + 1) * B].T
    add_diagonal(gram_ref, noise)
    high_ref[...], low_ref[...] = split(gram_ref[...])
    invert(a_ref, x_ref, noise, 2, 4, 1e-4)

    gradient = slopes(x_ref, high_ref, low_ref, dict_ref)
    powers = jnp.maximum(power_ref[...] - gradient, 0.0)
    next_ref[...] = powers
    model_pack(pack_ref, weighted_ref, dict_ref, powers)
    send_pieces(pack_ref, keep_ref, send_ref, which, ROWS, 0)


def third_kernel(
    noise_ref, own_ref, other_ref, dict_ref, high_ref, low_ref, power_ref,
    next_ref, gradient_ref,
    a_ref, x_ref, pack_ref,
):
    which, _ = place_of_device()
    noise = noise_ref[0:1, 0:1]
    receive_pieces(pack_ref, own_ref, other_ref, which, ROWS, 0)
    unpack_upper(pack_ref, a_ref, None, noise)
    invert(a_ref, x_ref, noise, 0, 2, 1.6e-7)
    gradient = slopes(x_ref, high_ref, low_ref, dict_ref)
    gradient_ref[...] = gradient
    next_ref[...] = jnp.maximum(power_ref[...] - gradient, 0.0)


def partner(value, masks):
    pairs = [(i, i ^ masks[1 if i & CORE else 0]) for i in range(128)]
    return lax.ppermute(value, AXES, pairs)


def around(stage, order):
    return [tuple(m << bit for bit in STAGES[stage]) for m in order]


def exchange(keep, send, height, side=None):
    received = partner(send, (CORE, CORE))
    pieces = [keep[c] + received[c] for c in (slice(n * height, (n + 1) * height) for n in range(4))]
    pieces, side = lax.optimization_barrier((pieces, side))
    order = (3, 2, 1)
    total = pieces[0]
    for arrived in [partner(pieces[m], masks) for m, masks in zip(order, around(0, order))]:
        total = total + arrived
    for stage in (1, 2):
        total = lax.optimization_barrier(total)
        for arrived in [partner(total, masks) for masks in around(stage, ORDER)]:
            total = total + arrived
    total = lax.optimization_barrier(total)
    own = jnp.concatenate([total] + [partner(total, masks) for masks in around(3, ORDER)], 0)
    return own, partner(own, (CORE, CORE)), side


VM = pl.BlockSpec(memory_space=pltpu.VMEM)
HB = pl.BlockSpec(memory_space=pltpu.HBM)


def shards(pilot_seed, delay_shift, active_column, channel, initial_power, noise_power):
    device_count = lax.axis_size("cols") * lax.axis_size("grp")
    total_samples = channel.shape[1] * device_count
    count = delay_shift.shape[0]
    units = pilot_seed.shape[0]
    active_count = active_column.shape[0]
    height = 2 * ROWS + EXTRA
    shape = jax.ShapeDtypeStruct
    row = shape((1, count), f32)
    square = (L, L)
    chunks = 8
    params = pltpu.CompilerParams(vmem_limit_bytes=48 << 20)

    keep, send, dictionary, start_power = pl.pallas_call(
        first_kernel,
        out_shape=(
            shape((4 * height, B), f32), shape((4 * height, B), f32), shape((L, count), bf16), row
        ),
        in_specs=[HB] * 5,
        out_specs=(VM,) * 4,
        scratch_shapes=[
            pltpu.VMEM((chunks, L, channel.shape[1] // chunks), bf16),
            pltpu.VMEM((L, count), bf16),
            pltpu.VMEM((PACK, B), f32),
            pltpu.VMEM((L // 2, L), f32),
            pltpu.VMEM((L // 2, L // 2), f32),
            pltpu.VMEM((1, units), jnp.int32),
            pltpu.VMEM((1, count), jnp.int32),
            pltpu.VMEM((1, active_count), jnp.int32),
            pltpu.SemaphoreType.DMA((chunks,)),
            pltpu.SemaphoreType.DMA((4,)),
        ],
        compiler_params=params,
        name="first",
    )(
        *(
            pltpu.with_memory_space_constraint(value, pltpu.HBM)
            for value in (
                pilot_seed.reshape(1, units), delay_shift.reshape(1, count), initial_power.reshape(1, count),
                active_column.reshape(1, active_count), channel,
            )
        ),
    )
    own, other, noise = exchange(keep, send, height, jnp.broadcast_to(noise_power.reshape(1, 1), (1, B)))
    half = shape(square, bf16)
    keep, send, high, low, powers = pl.pallas_call(
        functools.partial(second_kernel, total_samples),
        out_shape=(shape((4 * ROWS, B), f32), shape((4 * ROWS, B), f32), half, half, row),
        in_specs=[VM] * 5,
        out_specs=(VM, VM, VM, VM, VM),
        scratch_shapes=[
            pltpu.VMEM(square, f32),
            pltpu.VMEM(square, f32),
            pltpu.VMEM(square, f32),
            pltpu.VMEM((PACK, B), f32),
            pltpu.VMEM(square, bf16),
            pltpu.VMEM((L, count), bf16),
        ],
        compiler_params=params,
        name="second",
    )(noise, own, other, dictionary, start_power)
    own, other, _ = exchange(keep, send, ROWS)
    powers, gradient = pl.pallas_call(
        third_kernel,
        out_shape=(row, row),
        in_specs=[VM] * 7,
        out_specs=(VM, VM),
        scratch_shapes=[
            pltpu.VMEM(square, f32),
            pltpu.VMEM(square, f32),
            pltpu.VMEM((PACK, B), f32),
        ],
        compiler_params=params,
        name="third",
    )(noise, own, other, dictionary, high, low, powers)
    return (powers.reshape(count), gradient.reshape(count))


def solution(mesh):
    placed = (
        P(AXES),
        P(AXES),
        P(),
        P(None, AXES),
        P(AXES),
        P(),
    )
    return jax.shard_map(
        shards,
        mesh=mesh,
        in_specs=placed,
        out_specs=(P(AXES), P(AXES)),
        check_vma=False,
    )
```

```python
import functools
import math

import jax
import jax.numpy as jnp
from jax import lax
from jax.experimental import pallas as pl
from jax.experimental.pallas import tpu as pltpu
from jax.sharding import PartitionSpec as P

L = 512
DELAYS = 8
ITERS = 2
AXES = ("cols", "grp")
CORE = 4
X, Z, Y = 0, 3, 5
STAGES = ((X, Y), (Y, Z), (Z, X), (X, Y))

mult_first = 747796405
mult_second = 289133645
add_first = 1442695041
mult_third = 2073658381

B = 128
NB = L // B
BLOCKS = [(i, j) for i in range(NB) for j in range(i + 1, NB)]
PACK = (len(BLOCKS) + NB // 2) * B
PIECES = 8
ROWS = PACK // PIECES
EXTRA = 8
ORDER = (3, 1, 2)
SLOTS = (0,) + ORDER

f32 = jnp.float32
bf16 = jnp.bfloat16
contract_cols = (((1,), (1,)), ((), ()))


def dot(left, right):
    return jnp.dot(left, right, preferred_element_type=f32)


def dot_t(left, right):
    return lax.dot_general(left, right, contract_cols, preferred_element_type=f32)


def dot_halves(left, right, product):
    axis = 0 if product is dot else 1
    cut = left.shape[1] // 2
    first, second = (slice(0, cut), slice(cut, None))
    pick = (lambda v, c: v[c]) if axis == 0 else (lambda v, c: v[:, c])
    return product(left[:, first], pick(right, first)) + product(left[:, second], pick(right, second))


def split(value):
    high = value.astype(bf16)
    return high, (value - high.astype(f32)).astype(bf16)


def dot_exact(left, right):
    return jnp.dot(left, right, precision=lax.Precision.HIGHEST, preferred_element_type=f32)


def identity_like(value):
    rows = lax.broadcasted_iota(jnp.int32, value.shape, 0)
    cols = lax.broadcasted_iota(jnp.int32, value.shape, 1)
    return rows == cols


def signed(value):
    value %= 1 << 32
    return jnp.int32(value - (1 << 32) if value >= 1 << 31 else value)


def write_dictionary(out_ref, seeds, shifts, first_row, rows):
    low = seeds * signed(mult_first) + signed(add_first) - shifts * signed(mult_second)
    wrapped = low + signed(L * mult_second)
    row = lax.broadcasted_iota(jnp.int32, (rows, B), 0) + first_row
    start = row * signed(mult_second)
    for tile in range(seeds.shape[1] // B):
        cut = slice(tile * B, (tile + 1) * B)
        x = start + jnp.where(row < shifts[:, cut], wrapped[:, cut], low[:, cut])
        x = x ^ lax.shift_right_logical(x, 15)
        x = x * signed(mult_third)
        x = (x ^ lax.shift_right_logical(x, 13)) & signed(1 << 11)
        value = jnp.where(x == 0, jnp.float32(1), jnp.float32(-1))
        out_ref[first_row : first_row + rows, cut] = value.astype(bf16)


def block_order(shape):
    return lax.broadcasted_iota(jnp.int32, shape, 0), lax.broadcasted_iota(jnp.int32, shape, 1)


def pack_lower(pack_ref, left, corner):
    def block(i, j):
        if j < NB // 2:
            return left[i * B : (i + 1) * B, j * B : (j + 1) * B]
        i, j = i - NB // 2, j - NB // 2
        return corner[i * B : (i + 1) * B, j * B : (j + 1) * B]

    for number, (i, j) in enumerate(BLOCKS):
        pack_ref[number * B : (number + 1) * B, :] = block(j, i)
    row, col = block_order((B, B))
    for pair in range(NB // 2):
        number = len(BLOCKS) + pair
        both = jnp.where(row <= col, block(2 * pair, 2 * pair), block(2 * pair + 1, 2 * pair + 1))
        pack_ref[number * B : (number + 1) * B, :] = both


def diagonal_of(block):
    row, col = block_order(block.shape)
    return jnp.sum(jnp.where(row == col, block, 0.0), axis=0, keepdims=True)


def unpack(pack_ref, out_ref, diagonals, shift):
    for number, (i, j) in enumerate(BLOCKS):
        block = pack_ref[number * B : (number + 1) * B, :]
        out_ref[j * B : (j + 1) * B, i * B : (i + 1) * B] = block
        out_ref[i * B : (i + 1) * B, j * B : (j + 1) * B] = block.T
    row, col = block_order((B, B))
    for pair in range(NB // 2):
        number = len(BLOCKS) + pair
        both = pack_ref[number * B : (number + 1) * B, :]
        turned = both.T
        upper = jnp.where(row <= col, both, turned)
        lower = jnp.where(row > col, both, turned)
        if diagonals is not None:
            lower = jnp.where(row == col, diagonals[pair], lower)
        for i, value in ((2 * pair, upper), (2 * pair + 1, lower)):
            if shift is not None:
                value = jnp.where(row == col, value + shift, value)
            out_ref[i * B : (i + 1) * B, i * B : (i + 1) * B] = value


def place_of_device():
    position = lax.axis_index("cols").astype(jnp.int32) * 4 + lax.axis_index("grp").astype(jnp.int32)
    core = lax.shift_right_logical(position, 2) & 1
    first, second = [lax.shift_right_logical(position, bit) & 3 for bit in STAGES[0]]
    own = jnp.where(core == 0, first, second)
    return own + 4 * (first + second - own) + 16 * core, position


def piece(which, place):
    core = lax.shift_right_logical(which, 4) & 1
    if place < PIECES // 2:
        number = core * 4 + ((which & 3) ^ place)
    else:
        number = (1 - core) * 4 + ((lax.shift_right_logical(which, 2) & 3) ^ (place - 4))
    return pl.multiple_of(number * ROWS, ROWS)


def extra_row(which, number, height, slots):
    core = lax.shift_right_logical(which, 4) & 1
    position = jnp.where(core == 0, which, lax.shift_right_logical(which, 2)) & 3
    place = position ^ number
    slot = sum(jnp.where(place == p, n, 0) for n, p in enumerate(slots))
    return pl.multiple_of(slot * height + 2 * ROWS, 8)


def send_pieces(pack_ref, keep_ref, send_ref, which, height, offset):
    half = PIECES // 2
    for place in range(PIECES):
        target, at = (keep_ref, place) if place < half else (send_ref, place - half)
        start = at * height + offset
        target[start : start + ROWS, :] = pack_ref[pl.ds(piece(which, place), ROWS), :]


def receive_pieces(pack_ref, own_ref, other_ref, which, height, offset):
    half = PIECES // 2
    for slot, place in enumerate(SLOTS):
        start = slot * height + offset
        for source, at in ((own_ref, place), (other_ref, place + half)):
            pack_ref[pl.ds(piece(which, at), ROWS), :] = source[start : start + ROWS, :]


def model_pack(pack_ref, weighted_ref, dict_ref, powers):
    high, low = split(powers)
    half = L // 2
    left = corner = None
    for part in (low, high):
        weighted_ref[...] = dict_ref[...] * part
        a = dot_halves(weighted_ref[...], dict_ref[:half, :], dot_t)
        c = dot_halves(weighted_ref[half:, :], dict_ref[half:, :], dot_t)
        left, corner = (a, c) if left is None else (left + a, corner + c)
    pack_lower(pack_ref, left * (1.0 / L), corner * (1.0 / L))


def first_kernel(
    seed_hbm, shift_hbm, power_hbm, active_hbm, channel_hbm,
    keep_ref, send_ref, dict_ref, power_ref,
    chan_ref, weighted_ref, pack_ref, left_ref, corner_ref, seed_ref, shift_ref, active_ref,
    chan_sems, row_sems,
):
    which, position = place_of_device()
    chunks = chan_ref.shape[0]
    width = chan_ref.shape[2]
    rows = [(seed_hbm, seed_ref), (shift_hbm, shift_ref), (active_hbm, active_ref), (power_hbm, power_ref)]
    row_copies = [pltpu.make_async_copy(a, b, row_sems.at[n]) for n, (a, b) in enumerate(rows)]
    copies = [
        pltpu.make_async_copy(
            channel_hbm.at[:, n * width : (n + 1) * width], chan_ref.at[n], chan_sems.at[n]
        )
        for n in range(chunks)
    ]
    for copy in row_copies + copies:
        copy.start()
    height = 2 * ROWS + EXTRA
    half = L // 2
    step = L // chunks

    def gram(n):
        copies[n].wait()
        block = chan_ref[n]
        a = dot_halves(block, block[:half], dot_t)
        c = dot_halves(block[half:], block[half:], dot_t)
        if n == 0:
            left_ref[...] = a
            corner_ref[...] = c
        else:
            left_ref[...] += a
            corner_ref[...] += c

    for n in range(2):
        gram(n)
    for copy in row_copies:
        copy.wait()
    units = seed_ref[...]
    shifts = shift_ref[...]
    count = shifts.shape[1]

    def in_bytes(value, number):
        return [lax.shift_right_logical(value, 8 * n) & 255 for n in range(number)]

    def table_of(parts, width):
        parts = parts + [jnp.zeros((16 - len(parts), width), jnp.int32)]
        return jnp.concatenate(parts, 0).astype(f32).astype(bf16)

    def chosen(hit):
        return jnp.where(hit, jnp.float32(1), jnp.float32(0)).astype(bf16)

    shape = (units.shape[1], count)
    user = lax.shift_right_logical(lax.broadcasted_iota(jnp.int32, shape, 1), int(math.log2(DELAYS)))
    spread = dot(table_of(in_bytes(units, 3), units.shape[1]), chosen(lax.broadcasted_iota(jnp.int32, shape, 0) == user))
    seed_bytes = [spread[n : n + 1].astype(jnp.int32) for n in range(3)]
    seeds = seed_bytes[0] + seed_bytes[1] * 256 + seed_bytes[2] * 65536

    local = active_ref[...] - position * count
    hit = lax.broadcasted_iota(jnp.int32, (count, local.shape[1]), 0) == local
    found = dot(table_of(seed_bytes + in_bytes(shifts, 2), count), chosen(hit))
    seeds_here = found[0:1] + 256.0 * found[1:2] + 65536.0 * found[2:3]
    shifts_here = found[3:4] + 256.0 * found[4:5]
    for n in range(chunks):
        if n >= 2:
            gram(n)
        write_dictionary(dict_ref, seeds, shifts, n * step, step)
    pack_lower(pack_ref, left_ref[...], corner_ref[...])
    send_pieces(pack_ref, keep_ref, send_ref, which, height, ROWS)
    core = lax.shift_right_logical(which, 4) & 1
    for number in range(NB):
        cut = slice(number * B, (number + 1) * B)
        rows = [seeds_here[:, cut], shifts_here[:, cut]]
        if number < NB // 2:
            cut = slice(B, 2 * B)
            rows.append(diagonal_of((left_ref if number == 0 else corner_ref)[cut, cut]))
        tile = jnp.concatenate(rows + [jnp.zeros((EXTRA - len(rows), B), f32)], 0)
        start = extra_row(which, number, height, range(PIECES // 2))
        keep_ref[pl.ds(start, EXTRA), :] = jnp.where(core == 0, tile, 0.0)
        send_ref[pl.ds(start, EXTRA), :] = jnp.where(core == 0, 0.0, tile)
    model_pack(pack_ref, weighted_ref, dict_ref, power_ref[...])
    send_pieces(pack_ref, keep_ref, send_ref, which, height, 0)


def invert(a_ref, x_ref, noise, squarings, terms, small):
    eye = identity_like(a_ref)
    one = jnp.where(eye, 1.0, 0.0).astype(f32)
    mean = a_ref[0:1, 0:1]
    b = a_ref[...] - mean * one
    bh, bl = split(b)
    b2 = dot(bh, bh)
    fourth = jnp.sum(jnp.sum(b2 * b2, axis=0, keepdims=True), axis=1, keepdims=True)
    reach = 1.02 * jnp.sqrt(jnp.sqrt(fourth))
    centre = 0.5 * (jnp.maximum(noise, mean - reach) + mean + reach)
    inv = 1.0 / centre
    e0 = (centre - mean) * inv
    e2 = (e0 * e0) * one - b * (2.0 * e0 * inv) + b2 * (inv * inv)
    power = e2.astype(bf16)
    x = ((1.0 + e0) * (one + e2) - (b + dot(bh, power)) * inv) * inv
    for _ in range(squarings):
        power = dot(power, power).astype(bf16)
        x = x + dot(x.astype(bf16), power)

    def refine(x):
        r = one - x.astype(f32) * mean - (dot(bh, x) + dot(bl, x))
        rb = r.astype(bf16)
        r2 = dot(rb, rb)
        near = r + r2
        total = near + dot(r2.astype(bf16), near.astype(bf16)) if terms == 4 else near
        th, tl = split(total)
        update = dot(x, th) + dot(x, tl) if terms == 4 else dot(x, th)
        x_ref[...] = x.astype(f32) + update
        return jnp.sum(r2 * r2)

    size = refine(x.astype(bf16))

    @pl.when(jnp.logical_not(size < small))
    def _():
        def more(state):
            count, size = state
            return jnp.logical_and(count < 12, jnp.logical_and(size > small, size < 1e8))

        def step(state):
            count, size = state
            return count + 1, refine(x_ref[...].astype(bf16))

        count, last = lax.while_loop(more, step, (jnp.int32(0), size))

        @pl.when(jnp.logical_not(last < small))
        def _():
            bound = jnp.max(jnp.sum(jnp.abs(a_ref[...]), axis=0, keepdims=True))
            x_ref[...] = one * (1.0 / bound)

            def more(state):
                count, size, before = state
                going = jnp.logical_or(size > 1e-2, size < 0.25 * before)
                return jnp.logical_and(count < 48, jnp.logical_and(size > 1e-12, going))

            def step(state):
                count, size, before = state
                x = x_ref[...]
                r = one - dot_exact(a_ref[...], x)
                x_ref[...] = x + dot_exact(x, r)
                return count + 1, jnp.sum(r * r), size

            lax.while_loop(more, step, (jnp.int32(0), jnp.float32(1e30), jnp.float32(1e38)))


def slopes(x_ref, high_ref, low_ref, dict_ref):
    x = x_ref[...]
    xh, xl = split(x)
    right = dot(high_ref[...], xh) + (dot(high_ref[...], xl) + dot(low_ref[...], xh))
    rh, rl = split(right)
    half = L // 2
    d = dict_ref[...]
    result = None
    for rows, cols in ((slice(0, L), slice(0, half)), (slice(half, L), slice(half, L))):
        lh, ll = xh[rows], xl[rows]
        ch, cl = rh[:, cols], rl[:, cols]
        form = x[rows, cols] - (
            dot_halves(lh, ch, dot) + (dot_halves(lh, cl, dot) + dot_halves(ll, ch, dot))
        )
        if rows != cols:
            form = jnp.concatenate([form[:half], 2.0 * form[half:]], 0)
        fh, fl = split(form)
        mapped = dot(fh, d[cols]) + dot(fl, d[cols])
        part = jnp.sum(mapped * d[rows].astype(f32), axis=0, keepdims=True)
        result = part if result is None else result + part
    return result * (1.0 / L)


def add_diagonal(ref, noise):
    for n in range(NB):
        cut = slice(n * B, (n + 1) * B)
        block = ref[cut, cut]
        ref[cut, cut] = jnp.where(identity_like(block), block + noise, block)


def second_kernel(
    total_samples,
    noise_ref, own_ref, other_ref, dict_ref, power_ref,
    keep_ref, send_ref, high_ref, low_ref, next_ref,
    a_ref, gram_ref, x_ref, pack_ref, act_ref, weighted_ref,
):
    which, _ = place_of_device()
    noise = noise_ref[0:1, 0:1]
    height = 2 * ROWS + EXTRA
    seeds, shifts, diagonals = [], [], []
    for number in range(NB):
        start = extra_row(which, number, height, SLOTS)
        near = own_ref[pl.ds(start, EXTRA), :]
        far = other_ref[pl.ds(start, EXTRA), :]
        tile = jnp.where(lax.shift_right_logical(which, 4) & 1 == 0, near, far)
        seeds.append(tile[0:1])
        shifts.append(tile[1:2])
        diagonals.append(tile[2:3])
    receive_pieces(pack_ref, own_ref, other_ref, which, height, ROWS)
    unpack(pack_ref, gram_ref, diagonals, None)
    receive_pieces(pack_ref, own_ref, other_ref, which, height, 0)
    unpack(pack_ref, a_ref, None, noise)
    seeds = jnp.concatenate(seeds, 1).astype(jnp.int32)
    shifts = jnp.concatenate(shifts, 1).astype(jnp.int32)
    write_dictionary(act_ref, seeds, shifts, 0, L)
    act = act_ref[...]
    gh, gl = split(gram_ref[...])
    th, tl = split(dot(act, gh) + dot(act, gl))
    half = L // 2
    scale = 1.0 / (L * total_samples)
    left = (dot_halves(th, act[:half], dot_t) + dot_halves(tl, act[:half], dot_t)) * scale
    corner = (dot_halves(th[half:], act[half:], dot_t) + dot_halves(tl[half:], act[half:], dot_t)) * scale
    gram_ref[:, :half] = left
    gram_ref[half:, half:] = corner
    for i in range(NB // 2):
        for j in range(NB // 2, NB):
            gram_ref[i * B : (i + 1) * B, j * B : (j + 1) * B] = left[j * B : (j + 1) * B, i * B : (i + 1) * B].T
    add_diagonal(gram_ref, noise)
    high_ref[...], low_ref[...] = split(gram_ref[...])
    invert(a_ref, x_ref, noise, 2, 4, 1e-4)

    gradient = slopes(x_ref, high_ref, low_ref, dict_ref)
    powers = jnp.maximum(power_ref[...] - gradient, 0.0)
    next_ref[...] = powers
    model_pack(pack_ref, weighted_ref, dict_ref, powers)
    send_pieces(pack_ref, keep_ref, send_ref, which, ROWS, 0)


def third_kernel(
    noise_ref, own_ref, other_ref, dict_ref, high_ref, low_ref, power_ref,
    next_ref, gradient_ref,
    a_ref, x_ref, pack_ref,
):
    which, _ = place_of_device()
    noise = noise_ref[0:1, 0:1]
    receive_pieces(pack_ref, own_ref, other_ref, which, ROWS, 0)
    unpack(pack_ref, a_ref, None, noise)
    invert(a_ref, x_ref, noise, 0, 2, 1.6e-7)
    gradient = slopes(x_ref, high_ref, low_ref, dict_ref)
    gradient_ref[...] = gradient
    next_ref[...] = jnp.maximum(power_ref[...] - gradient, 0.0)


def partner(value, masks):
    pairs = [(i, i ^ masks[1 if i & CORE else 0]) for i in range(128)]
    return lax.ppermute(value, AXES, pairs)


def around(stage, order):
    return [tuple(m << bit for bit in STAGES[stage]) for m in order]


def exchange(keep, send, height, side=None):
    received = partner(send, (CORE, CORE))
    pieces = [keep[c] + received[c] for c in (slice(n * height, (n + 1) * height) for n in range(4))]
    pieces, side = lax.optimization_barrier((pieces, side))
    order = (3, 2, 1)
    total = pieces[0]
    for arrived in [partner(pieces[m], masks) for m, masks in zip(order, around(0, order))]:
        total = total + arrived
    for stage in (1, 2):
        total = lax.optimization_barrier(total)
        for arrived in [partner(total, masks) for masks in around(stage, ORDER)]:
            total = total + arrived
    total = lax.optimization_barrier(total)
    own = jnp.concatenate([total] + [partner(total, masks) for masks in around(3, ORDER)], 0)
    return own, partner(own, (CORE, CORE)), side


VM = pl.BlockSpec(memory_space=pltpu.VMEM)
HB = pl.BlockSpec(memory_space=pltpu.HBM)


def shards(pilot_seed, delay_shift, active_column, channel, initial_power, noise_power):
    device_count = lax.axis_size("cols") * lax.axis_size("grp")
    total_samples = channel.shape[1] * device_count
    count = delay_shift.shape[0]
    units = pilot_seed.shape[0]
    active_count = active_column.shape[0]
    height = 2 * ROWS + EXTRA
    shape = jax.ShapeDtypeStruct
    row = shape((1, count), f32)
    square = (L, L)
    chunks = 8
    params = pltpu.CompilerParams(vmem_limit_bytes=48 << 20)

    keep, send, dictionary, start_power = pl.pallas_call(
        first_kernel,
        out_shape=(
            shape((4 * height, B), f32), shape((4 * height, B), f32), shape((L, count), bf16), row
        ),
        in_specs=[HB] * 5,
        out_specs=(VM,) * 4,
        scratch_shapes=[
            pltpu.VMEM((chunks, L, channel.shape[1] // chunks), bf16),
            pltpu.VMEM((L, count), bf16),
            pltpu.VMEM((PACK, B), f32),
            pltpu.VMEM((L, L // 2), f32),
            pltpu.VMEM((L // 2, L // 2), f32),
            pltpu.VMEM((1, units), jnp.int32),
            pltpu.VMEM((1, count), jnp.int32),
            pltpu.VMEM((1, active_count), jnp.int32),
            pltpu.SemaphoreType.DMA((chunks,)),
            pltpu.SemaphoreType.DMA((4,)),
        ],
        compiler_params=params,
        name="first",
    )(
        *(
            pltpu.with_memory_space_constraint(value, pltpu.HBM)
            for value in (
                pilot_seed.reshape(1, units), delay_shift.reshape(1, count), initial_power.reshape(1, count),
                active_column.reshape(1, active_count), channel,
            )
        ),
    )
    own, other, noise = exchange(keep, send, height, jnp.broadcast_to(noise_power.reshape(1, 1), (1, B)))
    half = shape(square, bf16)
    keep, send, high, low, powers = pl.pallas_call(
        functools.partial(second_kernel, total_samples),
        out_shape=(shape((4 * ROWS, B), f32), shape((4 * ROWS, B), f32), half, half, row),
        in_specs=[VM] * 5,
        out_specs=(VM, VM, VM, VM, VM),
        scratch_shapes=[
            pltpu.VMEM(square, f32),
            pltpu.VMEM(square, f32),
            pltpu.VMEM(square, f32),
            pltpu.VMEM((PACK, B), f32),
            pltpu.VMEM(square, bf16),
            pltpu.VMEM((L, count), bf16),
        ],
        compiler_params=params,
        name="second",
    )(noise, own, other, dictionary, start_power)
    own, other, _ = exchange(keep, send, ROWS)
    powers, gradient = pl.pallas_call(
        third_kernel,
        out_shape=(row, row),
        in_specs=[VM] * 7,
        out_specs=(VM, VM),
        scratch_shapes=[
            pltpu.VMEM(square, f32),
            pltpu.VMEM(square, f32),
            pltpu.VMEM((PACK, B), f32),
        ],
        compiler_params=params,
        name="third",
    )(noise, own, other, dictionary, high, low, powers)
    return (powers.reshape(count), gradient.reshape(count))


def solution(mesh):
    placed = (
        P(AXES),
        P(AXES),
        P(),
        P(None, AXES),
        P(AXES),
        P(),
    )
    return jax.shard_map(
        shards,
        mesh=mesh,
        in_specs=placed,
        out_specs=(P(AXES), P(AXES)),
        check_vma=False,
    )
```

```python
import functools
import math

import jax
import jax.numpy as jnp
from jax import lax
from jax.experimental import pallas as pl
from jax.experimental.pallas import tpu as pltpu
from jax.sharding import PartitionSpec as P

L = 512
DELAYS = 8
ITERS = 2
AXES = ("cols", "grp")
CORE = 4
X, Z, Y = 0, 3, 5
STAGES = ((X, Y), (Y, Z), (Z, X), (X, Y))

mult_first = 747796405
mult_second = 289133645
add_first = 1442695041
mult_third = 2073658381

B = 128
NB = L // B
BLOCKS = [(i, j) for i in range(NB) for j in range(i + 1, NB)]
PACK = (len(BLOCKS) + NB // 2) * B
PIECES = 8
ROWS = PACK // PIECES
EXTRA = 8
ORDER = (3, 1, 2)
SLOTS = (0,) + ORDER

f32 = jnp.float32
bf16 = jnp.bfloat16
contract_cols = (((1,), (1,)), ((), ()))


def dot(left, right):
    return jnp.dot(left, right, preferred_element_type=f32)


def dot_t(left, right):
    return lax.dot_general(left, right, contract_cols, preferred_element_type=f32)


def dot_halves(left, right, product):
    axis = 0 if product is dot else 1
    cut = left.shape[1] // 2
    first, second = (slice(0, cut), slice(cut, None))
    pick = (lambda v, c: v[c]) if axis == 0 else (lambda v, c: v[:, c])
    return product(left[:, first], pick(right, first)) + product(left[:, second], pick(right, second))


def split(value):
    high = value.astype(bf16)
    return high, (value - high.astype(f32)).astype(bf16)


def dot_exact(left, right):
    return jnp.dot(left, right, precision=lax.Precision.HIGHEST, preferred_element_type=f32)


def identity_like(value):
    rows = lax.broadcasted_iota(jnp.int32, value.shape, 0)
    cols = lax.broadcasted_iota(jnp.int32, value.shape, 1)
    return rows == cols


def signed(value):
    value %= 1 << 32
    return jnp.int32(value - (1 << 32) if value >= 1 << 31 else value)


def write_dictionary(out_ref, seeds, shifts, first_row, rows):
    low = seeds * signed(mult_first) + signed(add_first) - shifts * signed(mult_second)
    wrapped = low + signed(L * mult_second)
    row = lax.broadcasted_iota(jnp.int32, (rows, B), 0) + first_row
    start = row * signed(mult_second)
    for tile in range(seeds.shape[1] // B):
        cut = slice(tile * B, (tile + 1) * B)
        x = start + jnp.where(row < shifts[:, cut], wrapped[:, cut], low[:, cut])
        x = x ^ lax.shift_right_logical(x, 15)
        x = x * signed(mult_third)
        x = (x ^ lax.shift_right_logical(x, 13)) & signed(1 << 11)
        value = jnp.where(x == 0, jnp.float32(1), jnp.float32(-1))
        out_ref[first_row : first_row + rows, cut] = value.astype(bf16)


def block_order(shape):
    return lax.broadcasted_iota(jnp.int32, shape, 0), lax.broadcasted_iota(jnp.int32, shape, 1)


def pack_lower(pack_ref, left, corner):
    def block(i, j):
        if j < NB // 2:
            return left[i * B : (i + 1) * B, j * B : (j + 1) * B]
        i, j = i - NB // 2, j - NB // 2
        return corner[i * B : (i + 1) * B, j * B : (j + 1) * B]

    for number, (i, j) in enumerate(BLOCKS):
        pack_ref[number * B : (number + 1) * B, :] = block(j, i)
    row, col = block_order((B, B))
    for pair in range(NB // 2):
        number = len(BLOCKS) + pair
        both = jnp.where(row <= col, block(2 * pair, 2 * pair), block(2 * pair + 1, 2 * pair + 1))
        pack_ref[number * B : (number + 1) * B, :] = both


def diagonal_of(block):
    row, col = block_order(block.shape)
    return jnp.sum(jnp.where(row == col, block, 0.0), axis=0, keepdims=True)


def unpack(pack_ref, out_ref, diagonals, shift):
    for number, (i, j) in enumerate(BLOCKS):
        block = pack_ref[number * B : (number + 1) * B, :]
        out_ref[j * B : (j + 1) * B, i * B : (i + 1) * B] = block
        out_ref[i * B : (i + 1) * B, j * B : (j + 1) * B] = block.T
    row, col = block_order((B, B))
    for pair in range(NB // 2):
        number = len(BLOCKS) + pair
        both = pack_ref[number * B : (number + 1) * B, :]
        turned = both.T
        upper = jnp.where(row <= col, both, turned)
        lower = jnp.where(row > col, both, turned)
        if diagonals is not None:
            lower = jnp.where(row == col, diagonals[pair], lower)
        for i, value in ((2 * pair, upper), (2 * pair + 1, lower)):
            if shift is not None:
                value = jnp.where(row == col, value + shift, value)
            out_ref[i * B : (i + 1) * B, i * B : (i + 1) * B] = value


def place_of_device():
    position = lax.axis_index("cols").astype(jnp.int32) * 4 + lax.axis_index("grp").astype(jnp.int32)
    core = lax.shift_right_logical(position, 2) & 1
    first, second = [lax.shift_right_logical(position, bit) & 3 for bit in STAGES[0]]
    own = jnp.where(core == 0, first, second)
    return own + 4 * (first + second - own) + 16 * core, position


def piece(which, place):
    core = lax.shift_right_logical(which, 4) & 1
    if place < PIECES // 2:
        number = core * 4 + ((which & 3) ^ place)
    else:
        number = (1 - core) * 4 + ((lax.shift_right_logical(which, 2) & 3) ^ (place - 4))
    return pl.multiple_of(number * ROWS, ROWS)


def extra_row(which, number, height, slots):
    core = lax.shift_right_logical(which, 4) & 1
    position = jnp.where(core == 0, which, lax.shift_right_logical(which, 2)) & 3
    place = position ^ number
    slot = sum(jnp.where(place == p, n, 0) for n, p in enumerate(slots))
    return pl.multiple_of(slot * height + 2 * ROWS, 8)


def send_pieces(pack_ref, keep_ref, send_ref, which, height, offset):
    half = PIECES // 2
    for place in range(PIECES):
        target, at = (keep_ref, place) if place < half else (send_ref, place - half)
        start = at * height + offset
        target[start : start + ROWS, :] = pack_ref[pl.ds(piece(which, place), ROWS), :]


def receive_pieces(pack_ref, own_ref, other_ref, which, height, offset):
    half = PIECES // 2
    for slot, place in enumerate(SLOTS):
        start = slot * height + offset
        for source, at in ((own_ref, place), (other_ref, place + half)):
            pack_ref[pl.ds(piece(which, at), ROWS), :] = source[start : start + ROWS, :]


def model_pack(pack_ref, weighted_ref, dict_ref, powers):
    high, low = split(powers)
    half = L // 2
    left = corner = None
    for part in (low, high):
        weighted_ref[...] = dict_ref[...] * part
        a = dot_halves(weighted_ref[...], dict_ref[:half, :], dot_t)
        c = dot_halves(weighted_ref[half:, :], dict_ref[half:, :], dot_t)
        left, corner = (a, c) if left is None else (left + a, corner + c)
    pack_lower(pack_ref, left * (1.0 / L), corner * (1.0 / L))


def first_kernel(
    seed_hbm, shift_hbm, power_hbm, active_hbm, channel_hbm,
    keep_ref, send_ref, dict_ref, power_ref,
    chan_ref, weighted_ref, pack_ref, left_ref, corner_ref, seed_ref, shift_ref, active_ref,
    chan_sems, row_sems,
):
    which, position = place_of_device()
    chunks = chan_ref.shape[0]
    width = chan_ref.shape[2]
    rows = [(seed_hbm, seed_ref), (shift_hbm, shift_ref), (active_hbm, active_ref), (power_hbm, power_ref)]
    row_copies = [pltpu.make_async_copy(a, b, row_sems.at[n]) for n, (a, b) in enumerate(rows)]
    copies = [
        pltpu.make_async_copy(
            channel_hbm.at[:, n * width : (n + 1) * width], chan_ref.at[n], chan_sems.at[n]
        )
        for n in range(chunks)
    ]
    for copy in row_copies + copies:
        copy.start()
    height = 2 * ROWS + EXTRA
    half = L // 2
    step = L // chunks

    def gram(n):
        copies[n].wait()
        block = chan_ref[n]
        a = dot_halves(block, block[:half], dot_t)
        c = dot_halves(block[half:], block[half:], dot_t)
        if n == 0:
            left_ref[...] = a
            corner_ref[...] = c
        else:
            left_ref[...] += a
            corner_ref[...] += c

    for n in range(2):
        gram(n)
    for copy in row_copies:
        copy.wait()
    units = seed_ref[...]
    shifts = shift_ref[...]
    count = shifts.shape[1]

    def in_bytes(value, number):
        return [lax.shift_right_logical(value, 8 * n) & 255 for n in range(number)]

    def table_of(parts, width):
        parts = parts + [jnp.zeros((16 - len(parts), width), jnp.int32)]
        return jnp.concatenate(parts, 0).astype(f32).astype(bf16)

    def chosen(hit):
        return jnp.where(hit, jnp.float32(1), jnp.float32(0)).astype(bf16)

    shape = (units.shape[1], count)
    user = lax.shift_right_logical(lax.broadcasted_iota(jnp.int32, shape, 1), int(math.log2(DELAYS)))
    spread = dot(table_of(in_bytes(units, 3), units.shape[1]), chosen(lax.broadcasted_iota(jnp.int32, shape, 0) == user))
    seed_bytes = [spread[n : n + 1].astype(jnp.int32) for n in range(3)]
    seeds = seed_bytes[0] + seed_bytes[1] * 256 + seed_bytes[2] * 65536

    local = active_ref[...] - position * count
    hit = lax.broadcasted_iota(jnp.int32, (count, local.shape[1]), 0) == local
    found = dot(table_of(seed_bytes + in_bytes(shifts, 2), count), chosen(hit))
    seeds_here = found[0:1] + 256.0 * found[1:2] + 65536.0 * found[2:3]
    shifts_here = found[3:4] + 256.0 * found[4:5]
    for n in range(chunks):
        if n >= 2:
            gram(n)
        write_dictionary(dict_ref, seeds, shifts, n * step, step)
    pack_lower(pack_ref, left_ref[...], corner_ref[...])
    send_pieces(pack_ref, keep_ref, send_ref, which, height, ROWS)
    core = lax.shift_right_logical(which, 4) & 1
    for number in range(NB):
        cut = slice(number * B, (number + 1) * B)
        rows = [seeds_here[:, cut], shifts_here[:, cut]]
        if number < NB // 2:
            cut = slice(B, 2 * B)
            rows.append(diagonal_of((left_ref if number == 0 else corner_ref)[cut, cut]))
        tile = jnp.concatenate(rows + [jnp.zeros((EXTRA - len(rows), B), f32)], 0)
        start = extra_row(which, number, height, range(PIECES // 2))
        keep_ref[pl.ds(start, EXTRA), :] = jnp.where(core == 0, tile, 0.0)
        send_ref[pl.ds(start, EXTRA), :] = jnp.where(core == 0, 0.0, tile)
    model_pack(pack_ref, weighted_ref, dict_ref, power_ref[...])
    send_pieces(pack_ref, keep_ref, send_ref, which, height, 0)


def invert(a_ref, x_ref, noise, squarings, terms, small):
    eye = identity_like(a_ref)
    one = jnp.where(eye, 1.0, 0.0).astype(f32)
    mean = a_ref[0:1, 0:1]
    b = a_ref[...] - mean * one
    bh, bl = split(b)
    b2 = dot(bh, bh)
    fourth = jnp.sum(jnp.sum(b2 * b2, axis=0, keepdims=True), axis=1, keepdims=True)
    reach = 1.02 * jnp.sqrt(jnp.sqrt(fourth))
    centre = 0.5 * (jnp.maximum(noise, mean - reach) + mean + reach)
    inv = 1.0 / centre
    e0 = (centre - mean) * inv
    e2 = (e0 * e0) * one - b * (2.0 * e0 * inv) + b2 * (inv * inv)
    power = e2.astype(bf16)
    x = ((1.0 + e0) * (one + e2) - (b + dot(bh, power)) * inv) * inv
    for _ in range(squarings):
        power = dot(power, power).astype(bf16)
        x = x + dot(x.astype(bf16), power)

    def refine(x):
        r = one - x.astype(f32) * mean - (dot(bh, x) + dot(bl, x))
        rb = r.astype(bf16)
        r2 = dot(rb, rb)
        near = r + r2
        total = near + dot(r2.astype(bf16), near.astype(bf16)) if terms == 4 else near
        th, tl = split(total)
        update = dot(x, th) + dot(x, tl) if terms == 4 else dot(x, th)
        x_ref[...] = x.astype(f32) + update
        return jnp.sum(r2 * r2)

    size = refine(x.astype(bf16))

    @pl.when(jnp.logical_not(size < small))
    def _():
        def more(state):
            count, size = state
            return jnp.logical_and(count < 12, jnp.logical_and(size > small, size < 1e8))

        def step(state):
            count, size = state
            return count + 1, refine(x_ref[...].astype(bf16))

        count, last = lax.while_loop(more, step, (jnp.int32(0), size))

        @pl.when(jnp.logical_not(last < small))
        def _():
            bound = jnp.max(jnp.sum(jnp.abs(a_ref[...]), axis=0, keepdims=True))
            x_ref[...] = one * (1.0 / bound)

            def more(state):
                count, size, before = state
                going = jnp.logical_or(size > 1e-2, size < 0.25 * before)
                return jnp.logical_and(count < 48, jnp.logical_and(size > 1e-12, going))

            def step(state):
                count, size, before = state
                x = x_ref[...]
                r = one - dot_exact(a_ref[...], x)
                x_ref[...] = x + dot_exact(x, r)
                return count + 1, jnp.sum(r * r), size

            lax.while_loop(more, step, (jnp.int32(0), jnp.float32(1e30), jnp.float32(1e38)))


def slopes(x_ref, high_ref, low_ref, dict_ref):
    x = x_ref[...]
    xh, xl = split(x)
    right = dot(high_ref[...], xh) + (dot(high_ref[...], xl) + dot(low_ref[...], xh))
    rh, rl = split(right)
    half = L // 2
    d = dict_ref[...]
    result = None
    for rows, cols in ((slice(0, half), slice(0, L)), (slice(half, L), slice(half, L))):
        lh, ll = xh[rows], xl[rows]
        if rows == cols:
            ch, cl = rh[:, cols], rl[:, cols]
            form = x[rows, cols] - (
                dot_halves(lh, ch, dot) + (dot_halves(lh, cl, dot) + dot_halves(ll, ch, dot))
            )
        else:
            form = x[rows] - (dot(lh, rh) + (dot(lh, rl) + dot(ll, rh)))
            form = jnp.concatenate([form[:, :half], 2.0 * form[:, half:]], 1)
        fh, fl = split(form)
        mapped = dot(fh, d[cols]) + dot(fl, d[cols])
        part = jnp.sum(mapped * d[rows].astype(f32), axis=0, keepdims=True)
        result = part if result is None else result + part
    return result * (1.0 / L)


def add_diagonal(ref, noise):
    for n in range(NB):
        cut = slice(n * B, (n + 1) * B)
        block = ref[cut, cut]
        ref[cut, cut] = jnp.where(identity_like(block), block + noise, block)


def second_kernel(
    total_samples,
    noise_ref, own_ref, other_ref, dict_ref, power_ref,
    keep_ref, send_ref, high_ref, low_ref, next_ref,
    a_ref, gram_ref, x_ref, pack_ref, act_ref, weighted_ref,
):
    which, _ = place_of_device()
    noise = noise_ref[0:1, 0:1]
    height = 2 * ROWS + EXTRA
    seeds, shifts, diagonals = [], [], []
    for number in range(NB):
        start = extra_row(which, number, height, SLOTS)
        near = own_ref[pl.ds(start, EXTRA), :]
        far = other_ref[pl.ds(start, EXTRA), :]
        tile = jnp.where(lax.shift_right_logical(which, 4) & 1 == 0, near, far)
        seeds.append(tile[0:1])
        shifts.append(tile[1:2])
        diagonals.append(tile[2:3])
    receive_pieces(pack_ref, own_ref, other_ref, which, height, ROWS)
    unpack(pack_ref, gram_ref, diagonals, None)
    receive_pieces(pack_ref, own_ref, other_ref, which, height, 0)
    unpack(pack_ref, a_ref, None, noise)
    seeds = jnp.concatenate(seeds, 1).astype(jnp.int32)
    shifts = jnp.concatenate(shifts, 1).astype(jnp.int32)
    write_dictionary(act_ref, seeds, shifts, 0, L)
    act = act_ref[...]
    gh, gl = split(gram_ref[...])
    th, tl = split(dot(act, gh) + dot(act, gl))
    half = L // 2
    scale = 1.0 / (L * total_samples)
    left = (dot_halves(th, act[:half], dot_t) + dot_halves(tl, act[:half], dot_t)) * scale
    corner = (dot_halves(th[half:], act[half:], dot_t) + dot_halves(tl[half:], act[half:], dot_t)) * scale
    gram_ref[:, :half] = left
    gram_ref[half:, half:] = corner
    for i in range(NB // 2):
        for j in range(NB // 2, NB):
            gram_ref[i * B : (i + 1) * B, j * B : (j + 1) * B] = left[j * B : (j + 1) * B, i * B : (i + 1) * B].T
    add_diagonal(gram_ref, noise)
    high_ref[...], low_ref[...] = split(gram_ref[...])
    invert(a_ref, x_ref, noise, 2, 4, 1e-4)

    gradient = slopes(x_ref, high_ref, low_ref, dict_ref)
    powers = jnp.maximum(power_ref[...] - gradient, 0.0)
    next_ref[...] = powers
    model_pack(pack_ref, weighted_ref, dict_ref, powers)
    send_pieces(pack_ref, keep_ref, send_ref, which, ROWS, 0)


def third_kernel(
    noise_ref, own_ref, other_ref, dict_ref, high_ref, low_ref, power_ref,
    next_ref, gradient_ref,
    a_ref, x_ref, pack_ref,
):
    which, _ = place_of_device()
    noise = noise_ref[0:1, 0:1]
    receive_pieces(pack_ref, own_ref, other_ref, which, ROWS, 0)
    unpack(pack_ref, a_ref, None, noise)
    invert(a_ref, x_ref, noise, 0, 2, 1.6e-7)
    gradient = slopes(x_ref, high_ref, low_ref, dict_ref)
    gradient_ref[...] = gradient
    next_ref[...] = jnp.maximum(power_ref[...] - gradient, 0.0)


def partner(value, masks):
    pairs = [(i, i ^ masks[1 if i & CORE else 0]) for i in range(128)]
    return lax.ppermute(value, AXES, pairs)


def around(stage, order):
    return [tuple(m << bit for bit in STAGES[stage]) for m in order]


def exchange(keep, send, height, side=None):
    received = partner(send, (CORE, CORE))
    pieces = [keep[c] + received[c] for c in (slice(n * height, (n + 1) * height) for n in range(4))]
    pieces, side = lax.optimization_barrier((pieces, side))
    order = (3, 2, 1)
    total = pieces[0]
    for arrived in [partner(pieces[m], masks) for m, masks in zip(order, around(0, order))]:
        total = total + arrived
    for stage in (1, 2):
        total = lax.optimization_barrier(total)
        for arrived in [partner(total, masks) for masks in around(stage, ORDER)]:
            total = total + arrived
    total = lax.optimization_barrier(total)
    own = jnp.concatenate([total] + [partner(total, masks) for masks in around(3, ORDER)], 0)
    return own, partner(own, (CORE, CORE)), side


VM = pl.BlockSpec(memory_space=pltpu.VMEM)
HB = pl.BlockSpec(memory_space=pltpu.HBM)


def shards(pilot_seed, delay_shift, active_column, channel, initial_power, noise_power):
    device_count = lax.axis_size("cols") * lax.axis_size("grp")
    total_samples = channel.shape[1] * device_count
    count = delay_shift.shape[0]
    units = pilot_seed.shape[0]
    active_count = active_column.shape[0]
    height = 2 * ROWS + EXTRA
    shape = jax.ShapeDtypeStruct
    row = shape((1, count), f32)
    square = (L, L)
    chunks = 8
    params = pltpu.CompilerParams(vmem_limit_bytes=48 << 20)

    keep, send, dictionary, start_power = pl.pallas_call(
        first_kernel,
        out_shape=(
            shape((4 * height, B), f32), shape((4 * height, B), f32), shape((L, count), bf16), row
        ),
        in_specs=[HB] * 5,
        out_specs=(VM,) * 4,
        scratch_shapes=[
            pltpu.VMEM((chunks, L, channel.shape[1] // chunks), bf16),
            pltpu.VMEM((L, count), bf16),
            pltpu.VMEM((PACK, B), f32),
            pltpu.VMEM((L, L // 2), f32),
            pltpu.VMEM((L // 2, L // 2), f32),
            pltpu.VMEM((1, units), jnp.int32),
            pltpu.VMEM((1, count), jnp.int32),
            pltpu.VMEM((1, active_count), jnp.int32),
            pltpu.SemaphoreType.DMA((chunks,)),
            pltpu.SemaphoreType.DMA((4,)),
        ],
        compiler_params=params,
        name="first",
    )(
        *(
            pltpu.with_memory_space_constraint(value, pltpu.HBM)
            for value in (
                pilot_seed.reshape(1, units), delay_shift.reshape(1, count), initial_power.reshape(1, count),
                active_column.reshape(1, active_count), channel,
            )
        ),
    )
    own, other, noise = exchange(keep, send, height, jnp.broadcast_to(noise_power.reshape(1, 1), (1, B)))
    half = shape(square, bf16)
    keep, send, high, low, powers = pl.pallas_call(
        functools.partial(second_kernel, total_samples),
        out_shape=(shape((4 * ROWS, B), f32), shape((4 * ROWS, B), f32), half, half, row),
        in_specs=[VM] * 5,
        out_specs=(VM, VM, VM, VM, VM),
        scratch_shapes=[
            pltpu.VMEM(square, f32),
            pltpu.VMEM(square, f32),
            pltpu.VMEM(square, f32),
            pltpu.VMEM((PACK, B), f32),
            pltpu.VMEM(square, bf16),
            pltpu.VMEM((L, count), bf16),
        ],
        compiler_params=params,
        name="second",
    )(noise, own, other, dictionary, start_power)
    own, other, _ = exchange(keep, send, ROWS)
    powers, gradient = pl.pallas_call(
        third_kernel,
        out_shape=(row, row),
        in_specs=[VM] * 7,
        out_specs=(VM, VM),
        scratch_shapes=[
            pltpu.VMEM(square, f32),
            pltpu.VMEM(square, f32),
            pltpu.VMEM((PACK, B), f32),
        ],
        compiler_params=params,
        name="third",
    )(noise, own, other, dictionary, high, low, powers)
    return (powers.reshape(count), gradient.reshape(count))


def solution(mesh):
    placed = (
        P(AXES),
        P(AXES),
        P(),
        P(None, AXES),
        P(AXES),
        P(),
    )
    return jax.shard_map(
        shards,
        mesh=mesh,
        in_specs=placed,
        out_specs=(P(AXES), P(AXES)),
        check_vma=False,
    )
```
